32 devices in a mesh: batch: 8 (over z, x), mp: 4 (over y, core).
Axes of the slice: x: 2, y: 2, z: 4, core: 2. Of those that a mesh axis runs over, the one named last changes fastest.
Arguments:
- tokens: bfloat16 [16, 2048, 768], P('batch', 'mp'), may hold values from -6 to 6
- cotangent: bfloat16 [16, 2048, 768], P('batch', 'mp'), may hold values from -6 to 6
- lengths: int32 [16], P('batch'), may hold values from 64 to 2048, as said below
- pre_attn_gain: bfloat16 [768], replicated, may hold values from 0.099609375 to 1.8984375
- pre_attn_bias: bfloat16 [768], replicated, may hold values from -3 to 3
- qkv_weight: bfloat16 [3, 768, 768], replicated, may hold values from -0.21875 to 0.21875
- conv_weight: bfloat16 [3, 3, 768], replicated, may hold values from -3 to 3
- out_weight: bfloat16 [768, 768], replicated, may hold values from -1.5 to 1.5
- pre_ffn_gain: bfloat16 [768], replicated, may hold values from 0.099609375 to 1.8984375
- pre_ffn_bias: bfloat16 [768], replicated, may hold values from -3 to 3
- up_weight: bfloat16 [768, 3072], replicated, may hold values from -0.21875 to 0.21875
- up_bias: bfloat16 [3072], replicated, may hold values from -3 to 3
- down_weight: bfloat16 [3072, 768], replicated, may hold values from -0.109375 to 0.109375
- down_bias: bfloat16 [768], replicated, may hold values from -3 to 3
Outputs:
- output: bfloat16 [16, 2048, 768], P('batch', 'mp')
- tokens_grad: bfloat16 [16, 2048, 768], P('batch', 'mp')
- pre_attn_gain_grad: float32 [768], P(('batch', 'mp'))
- pre_attn_bias_grad: float32 [768], P(('batch', 'mp'))
- qkv_weight_grad: float32 [3, 768, 768], P(None, 'batch', 'mp')
- conv_weight_grad: float32 [3, 3, 768], P(None, None, ('batch', 'mp'))
- out_weight_grad: float32 [768, 768], P(('batch', 'mp'))
- pre_ffn_gain_grad: float32 [768], P(('batch', 'mp'))
- pre_ffn_bias_grad: float32 [768], P(('batch', 'mp'))
- up_weight_grad: float32 [768, 3072], P(('batch', 'mp'))
- up_bias_grad: float32 [3072], P(('batch', 'mp'))
- down_weight_grad: float32 [3072, 768], P(('batch', 'mp'))
- down_bias_grad: float32 [768], P(('batch', 'mp'))
The draws below stay inside these ranges and needn't reach their ends.
Inputs may be any that keep to these rules, and one draw needn't show every extreme that they name: `lengths`: real tokens of each sequence; positions at or past it are padding. Some sequence has 2048 in every draw.
All inputs are finite; a program needn't handle non-finite values.
Results may differ from the reference program's by a relative error of at most 0.014.
The reference program's roundings to bfloat16 on the way count: a program that leaves them out, or rounds other values in their place, can miss the bound.
Values may be sent and summed in bfloat16 or wider, within the bound.
No kernel may reach another device: no remote copies, remote signals or barrier semaphores. Data moves between devices by JAX's collectives and lax.ppermute only.
A program may use at most 320 MiB of HBM per device.

```python
import jax
import jax.numpy as jnp
from jax import lax

D = 768
HEADS = 12
HEAD_DIM = 64
FF = 3072
KERNEL = 3
LEN = 2048
MIN_LEN = 64
QBLOCK = 512
SEQS = 16


def draw_lengths(key, part):
    first_key, second_key = jax.random.split(key)
    spread = jax.random.randint(first_key, (SEQS,), 0, 1025)
    span = LEN - MIN_LEN
    shorter = span * spread // 1024 * spread // 1024
    longest = jax.random.randint(second_key, (), 0, SEQS)
    return jnp.where(jnp.arange(SEQS, dtype=jnp.int32) == longest, LEN, LEN - shorter).astype(jnp.int32)


def with_spikes(values, own_key, source, target, shards_of, factor):
    def block_of(axis_at):
        return (jnp.arange(values.shape[axis_at]) // (values.shape[axis_at] // shards_of)).reshape((-1,) + (1,) * (values.ndim - 1 - axis_at))

    first = jax.random.permutation(own_key, shards_of)[block_of(target)]
    other_side = (block_of(target) + shards_of // 2) % shards_of
    return jnp.where((block_of(source) == first) | (block_of(source) == other_side), factor * values, values)


def steps_of(own_key, shape, pieces, smallest, top_value):
    def one(position, parts):
        heights = jax.random.uniform(jax.random.fold_in(jax.random.fold_in(own_key, 6), position), (parts,), jnp.float32, smallest / len(pieces), top_value / len(pieces))
        return jnp.repeat(jnp.exp(heights), shape[position] // parts).reshape((-1,) + (1,) * (len(shape) - position - 1))

    gain = one(*pieces[0])
    for cut in pieces[1:]:
        gain = gain * one(*cut)
    return gain


def normal_values(own_key, shape, width, bound, cuts=(), kind=jnp.bfloat16):
    drawn = jax.random.normal(own_key, shape, jnp.float32) * width
    if len(cuts) > 0:
        drawn = steps_of(own_key, shape, cuts, -0.22, 0.18) * drawn
    return jnp.clip(drawn, min=-bound, max=bound).astype(kind)


def bell_draw_with(own_key, dims, scale, most, cuts, heavy, kind=jnp.bfloat16):
    entries = scale * jax.random.normal(own_key, dims, jnp.float32)
    if cuts:
        entries = entries * steps_of(own_key, dims, cuts, -0.22, 0.18)
    return jnp.clip(with_spikes(entries, jax.random.fold_in(own_key, 3), *heavy), -most, most).astype(kind)


def setup_inputs(seed: int = 0) -> dict:
    keys = jax.random.split(jax.random.key(seed), 15)
    tokens = normal_values(keys[0], (SEQS, LEN, D), 1.0, 6.0, ((0, 8), (1, 4)))
    cotangent = bell_draw_with(keys[1], (SEQS, LEN, D), 1.0, 6.0, ((0, 8), (1, 4)), (0, 2, 8, 2.0))
    lengths = draw_lengths(jax.random.fold_in(keys[14], 71), 0)
    pre_attn_gain = jnp.clip(1.0 + 0.18 * jax.random.normal(keys[3], (D,), jnp.float32), 0.099609375, 1.8984375).astype(jnp.bfloat16)
    pre_attn_bias = normal_values(keys[4], (D,), 0.5, 3.0)
    qkv_weight = normal_values(keys[5], (3, D, D), D ** -0.5, 0.21875)
    conv_weight = normal_values(keys[6], (3, KERNEL, D), 0.6, 3.0)
    out_weight = normal_values(keys[7], (D, D), (D // 48) ** -0.5, 1.5)
    pre_ffn_gain = jnp.clip(1.0 + 0.18 * jax.random.normal(keys[8], (D,), jnp.float32), 0.099609375, 1.8984375).astype(jnp.bfloat16)
    pre_ffn_bias = normal_values(keys[9], (D,), 0.5, 3.0)
    up_weight = normal_values(keys[10], (D, FF), D ** -0.5, 0.21875)
    up_bias = normal_values(keys[11], (FF,), 0.5, 3.0)
    down_weight = normal_values(keys[12], (FF, D), FF ** -0.5, 0.109375)
    down_bias = normal_values(keys[13], (D,), 0.5, 3.0)
    return {"tokens": tokens, "cotangent": cotangent, "lengths": lengths, "pre_attn_gain": pre_attn_gain, "pre_attn_bias": pre_attn_bias, "qkv_weight": qkv_weight, "conv_weight": conv_weight, "out_weight": out_weight, "pre_ffn_gain": pre_ffn_gain, "pre_ffn_bias": pre_ffn_bias, "up_weight": up_weight, "up_bias": up_bias, "down_weight": down_weight, "down_bias": down_bias}


EPSILON = 1e-05
NEGATIVE = -1000000000.0
HIGHEST = lax.Precision.HIGHEST

@jax.custom_vjp
def low(v):
    return lax.optimization_barrier(v.astype(jnp.bfloat16)).astype(jnp.float32)

@jax.custom_vjp
def low_back(v):
    return v

def low_keep(v):
    return (low(v), None)

def low_pass(kept, grad):
    return (grad,)

def back_keep(v):
    return (v, None)

def back_low(kept, grad):
    return (low(grad),)
low.defvjp(low_keep, low_pass)
low_back.defvjp(back_keep, back_low)

def layer_norm(values, norm_gain, offset):
    center = values - lax.optimization_barrier(jnp.mean(values, axis=-1, keepdims=True))
    scaled = center * lax.rsqrt(lax.optimization_barrier(jnp.mean(center * center, axis=-1, keepdims=True)) + EPSILON)
    return scaled * norm_gain + offset

def causal_conv(values, kernel):
    taps = kernel.shape[1]
    seq_len = values.shape[0]
    padded = jnp.pad(values, ((taps - 1, 0), (0, 0), (0, 0)))
    total_sum = jnp.zeros_like(values)
    for offset in range(taps):
        first = taps - 1 - offset
        total_sum = total_sum + kernel[:, offset, :] * padded[first:first + seq_len]
    return total_sum

def attend(mixed, length):
    seq_len = mixed.shape[0]
    head_vals = mixed.reshape(seq_len, 3, HEADS, HEAD_DIM)
    queries = head_vals[:, 0]
    key_heads = head_vals[:, 1]
    values = head_vals[:, 2]
    blocks = seq_len // QBLOCK
    key_pos = jnp.arange(seq_len, dtype=jnp.int32)

    @jax.checkpoint
    def one_block(block_args):
        block_q, first = block_args
        scores = jnp.einsum('qhd,khd->hqk', block_q, key_heads, precision=HIGHEST) * HEAD_DIM ** (-0.5)
        query_pos = first + jnp.arange(QBLOCK, dtype=jnp.int32)
        allowed = (key_pos[None, :] <= query_pos[:, None]) & (key_pos[None, :] < length)
        scores = low_back(jnp.where(allowed[None], scores, NEGATIVE))
        log_total = jax.nn.logsumexp(scores, axis=-1, keepdims=True)
        prob_block = low(jnp.exp(scores - log_total))
        return jnp.einsum('hqk,khd->qhd', prob_block, values, precision=HIGHEST)
    starts = jnp.arange(blocks, dtype=jnp.int32) * QBLOCK
    out_parts = lax.map(one_block, (queries.reshape(blocks, QBLOCK, HEADS, HEAD_DIM), starts))
    return out_parts.reshape(seq_len, HEADS * HEAD_DIM)

def forward(params, tokens_row, length):
    seq_len = tokens_row.shape[0]
    valid_rows = (jnp.arange(seq_len, dtype=jnp.int32) < length)[:, None]
    normed = low(layer_norm(tokens_row, params[0], params[1]))
    projected = low_back(low(jnp.einsum('td,cde->tce', normed, params[2], precision=HIGHEST)))
    mixed = low(causal_conv(projected, params[3]))
    heads_out = low_back(low(attend(mixed, length)))
    attended = low_back(jnp.dot(heads_out, params[4], precision=HIGHEST))
    residual = tokens_row + attended
    normed_ffn = low(layer_norm(residual, params[5], params[6]))
    hidden_pre = low_back(jnp.dot(normed_ffn, params[7], precision=HIGHEST) + params[8])
    activated = low(jnp.square(jnp.maximum(hidden_pre, 0.0)))
    ffn_out = low_back(jnp.dot(activated, params[9], precision=HIGHEST) + params[10])
    return jnp.where(valid_rows, residual + ffn_out, 0.0)

def reference(tokens, cotangent, lengths, pre_attn_gain, pre_attn_bias, qkv_weight, conv_weight, out_weight, pre_ffn_gain, pre_ffn_bias, up_weight, up_bias, down_weight, down_bias):
    params = tuple((entry.astype(jnp.float32) for entry in (pre_attn_gain, pre_attn_bias, qkv_weight, conv_weight, out_weight, pre_ffn_gain, pre_ffn_bias, up_weight, up_bias, down_weight, down_bias)))

    def one_sequence(running, inputs):
        tokens_row, cotangent_row, length = inputs
        result, pullback = jax.vjp(lambda weights, token_rows: forward(weights, token_rows, length), params, tokens_row.astype(jnp.float32))
        weight_grads, rows_grad = pullback(cotangent_row.astype(jnp.float32))
        running = jax.tree.map(jnp.add, running, weight_grads)
        return (running, (result.astype(jnp.bfloat16), rows_grad.astype(jnp.bfloat16)))
    zero_grads = jax.tree.map(jnp.zeros_like, params)
    running, outputs = lax.scan(one_sequence, zero_grads, (tokens, cotangent, lengths))
    return (outputs[0], outputs[1], running[0], running[1], running[2], running[3], running[4], running[5], running[6], running[7], running[8], running[9], running[10])
```

```python
import functools

import jax
import jax.numpy as jnp
from jax import lax
from jax.experimental import pallas as pl
from jax.experimental.pallas import tpu as pltpu
from jax.sharding import PartitionSpec as P

HEAD_DIM = 64
LANES = 128
EPSILON = 1e-05
NEGATIVE = -1000000000.0
QBLOCK = 512
KBLOCK = 256
VMEM_BYTES = 60 << 20
F32 = jnp.float32
BF16 = jnp.bfloat16

CORE = [(i, i ^ 1) for i in range(4)]
PAIR = [(i, i ^ 2) for i in range(4)]


def dot_nt(left, right):
    return lax.dot_general(left, right, (((1,), (1,)), ((), ())), preferred_element_type=F32)


def dot_nn(left, right):
    return lax.dot_general(left, right, (((1,), (0,)), ((), ())), preferred_element_type=F32)


def dot_tn(left, right):
    return lax.dot_general(left, right, (((0,), (0,)), ((), ())), preferred_element_type=F32)


def params():
    return pltpu.CompilerParams(vmem_limit_bytes=VMEM_BYTES)


SMEM_SPEC = pl.BlockSpec(memory_space=pltpu.SMEM)


def norm_stats(values):
    center = values - jnp.mean(values, axis=-1, keepdims=True)
    inv_std = lax.rsqrt(jnp.mean(center * center, axis=-1, keepdims=True) + EPSILON)
    return center * inv_std, inv_std


def norm_backward(grad_out, norm_gain, scaled, inv_std):
    weighted = grad_out * norm_gain
    return inv_std * (
        weighted
        - jnp.mean(weighted, axis=-1, keepdims=True)
        - scaled * jnp.mean(weighted * scaled, axis=-1, keepdims=True)
    )


def project_kernel(x_ref, gain_ref, bias_ref, w_ref, normed_ref, proj_ref):
    scaled, _ = norm_stats(x_ref[...].astype(F32))
    normed = (scaled * gain_ref[...] + bias_ref[...]).astype(BF16)
    normed_ref[...] = normed
    proj_ref[...] = dot_nn(normed, w_ref[...]).astype(BF16)


def project(x, gain, bias, weight):
    rows, width = x.shape
    cols = weight.shape[1]
    tile = min(256, rows)
    return pl.pallas_call(
        project_kernel,
        grid=(rows // tile,),
        in_specs=[
            pl.BlockSpec((tile, width), lambda i: (i, 0)),
            pl.BlockSpec((1, width), lambda i: (0, 0)),
            pl.BlockSpec((1, width), lambda i: (0, 0)),
            pl.BlockSpec((width, cols), lambda i: (0, 0)),
        ],
        out_specs=[
            pl.BlockSpec((tile, width), lambda i: (i, 0)),
            pl.BlockSpec((tile, cols), lambda i: (i, 0)),
        ],
        out_shape=[
            jax.ShapeDtypeStruct((rows, width), BF16),
            jax.ShapeDtypeStruct((rows, cols), BF16),
        ],
        compiler_params=params(),
        cost_estimate=pl.CostEstimate(
            flops=2 * rows * width * cols, bytes_accessed=6 * rows * width, transcendentals=0
        ),
        name="project",
    )(x, gain, bias, weight)


def only_head(values, head):
    lane = lax.broadcasted_iota(jnp.int32, values.shape, 1)
    return jnp.where((lane // HEAD_DIM) == head, values, jnp.zeros_like(values))


def load_natural(member, blocks, dest, size, shift=0):
    for slot, block in enumerate(blocks):
        start = pl.multiple_of(lax.bitwise_xor(member, slot) * size, 8) + shift
        start = pl.multiple_of(start, 8)
        dest[pl.ds(start, size), :] = block.astype(dest.dtype)


def attend_kernel(
    m_ref, p0, p1, p2, p3, taps_ref, mixed_ref, own_ref, send_ref, lse_ref, pj, kh, vt, on, qs
):
    member = m_ref[0]
    size = p0.shape[0]
    length = 4 * size
    scale = jnp.asarray(HEAD_DIM ** (-0.5), BF16)
    for c in range(3):
        cols = slice(c * LANES, (c + 1) * LANES)
        pj[c, 0:8, :] = jnp.zeros((8, LANES), F32)
        load_natural(member, [p[:, cols] for p in (p0, p1, p2, p3)], pj.at[c], size, 8)
    for c in range(3):
        total = taps_ref[0, 3 * c : 3 * c + 1, :] * pj[c, 8 : 8 + length, :]
        total = total + taps_ref[0, 3 * c + 1 : 3 * c + 2, :] * pj[c, 7 : 7 + length, :]
        total = total + taps_ref[0, 3 * c + 2 : 3 * c + 3, :] * pj[c, 6 : 6 + length, :]
        mixed = total.astype(BF16)
        mixed_ref[:, c * LANES : (c + 1) * LANES] = mixed
        if c == 0:
            qs[...] = mixed * scale
        elif c == 1:
            kh[0] = only_head(mixed, 0)
            kh[1] = only_head(mixed, 1)
        else:
            vt[...] = mixed.T
    for first in range(0, length, QBLOCK):
        queries = qs[first : first + QBLOCK, :]
        keys = first + QBLOCK
        outs = []
        for head in range(2):
            scores = dot_nt(kh[head, 0:keys, :], queries)
            key_pos = lax.broadcasted_iota(jnp.int32, (QBLOCK, QBLOCK), 0)
            query_pos = lax.broadcasted_iota(jnp.int32, (QBLOCK, QBLOCK), 1)
            corner = jnp.where(key_pos <= query_pos, scores[first:keys, :], NEGATIVE)
            if first:
                scores = jnp.concatenate([scores[:first, :], corner], axis=0)
            else:
                scores = corner
            top = jnp.max(scores, axis=0, keepdims=True)
            weights = jnp.exp(scores - top)
            total = jnp.sum(weights, axis=0, keepdims=True)
            part = dot_nn(
                vt[head * HEAD_DIM : (head + 1) * HEAD_DIM, 0:keys], weights.astype(BF16)
            )
            outs.append(part * (1.0 / total))
            lse_ref[0, head : head + 1, first : first + QBLOCK] = top + jnp.log(total)
        on[first : first + QBLOCK, :] = jnp.concatenate(outs, axis=0).T.astype(BF16)
    for slot in range(4):
        start = pl.multiple_of(lax.bitwise_xor(member, slot) * size, size)
        block = on[pl.ds(start, size), :]
        dest = (own_ref, send_ref)[slot % 2]
        dest[slot // 2 * size : (slot // 2 + 1) * size, :] = block


def attend(member, proj, taps):
    size = proj[0].shape[0]
    pairs = proj[0].shape[1] // (3 * LANES)
    length = 4 * size
    width = pairs * LANES
    return pl.pallas_call(
        attend_kernel,
        grid=(pairs,),
        in_specs=[SMEM_SPEC]
        + [pl.BlockSpec((size, 3 * LANES), lambda p: (0, p))] * 4
        + [pl.BlockSpec((1, 16, LANES), lambda p: (p, 0, 0))],
        out_specs=[
            pl.BlockSpec((length, 3 * LANES), lambda p: (0, p)),
            pl.BlockSpec((2 * size, LANES), lambda p: (0, p)),
            pl.BlockSpec((2 * size, LANES), lambda p: (0, p)),
            pl.BlockSpec((1, 2, length), lambda p: (p, 0, 0)),
        ],
        out_shape=[
            jax.ShapeDtypeStruct((length, 3 * width), BF16),
            jax.ShapeDtypeStruct((2 * size, width), BF16),
            jax.ShapeDtypeStruct((2 * size, width), BF16),
            jax.ShapeDtypeStruct((pairs, 2, length), F32),
        ],
        scratch_shapes=[
            pltpu.VMEM((3, 8 + length, LANES), F32),
            pltpu.VMEM((2, length, LANES), BF16),
            pltpu.VMEM((LANES, length), BF16),
            pltpu.VMEM((length, LANES), BF16),
            pltpu.VMEM((length, LANES), BF16),
        ],
        compiler_params=params(),
        cost_estimate=pl.CostEstimate(
            flops=pairs * 14 * 10**9, bytes_accessed=12 << 20, transcendentals=0
        ),
        name="attend",
    )(member, *proj, taps)


def attend_back_kernel(
    m_ref,
    p0,
    p1,
    p2,
    p3,
    mixed_ref,
    lse_ref,
    taps_ref,
    own_ref,
    send_ref,
    down_ref,
    drecv_ref,
    gown_ref,
    gsend_ref,
    gconv_ref,
    pj,
    dm,
    qh,
    doh,
    kt,
    dl,
    dqa,
    nat,
):
    member = m_ref[0]
    size = p0.shape[0]
    length = 4 * size
    scale = jnp.asarray(HEAD_DIM ** (-0.5), BF16)
    halves = [slice(0, size), slice(size, 2 * size)]
    load_natural(
        member,
        [own_ref[halves[0]], send_ref[halves[0]], own_ref[halves[1]], send_ref[halves[1]]],
        nat.at[0],
        size,
    )
    load_natural(
        member,
        [down_ref[halves[0]], drecv_ref[halves[0]], down_ref[halves[1]], drecv_ref[halves[1]]],
        nat.at[1],
        size,
    )
    grads = nat[1]
    product = (grads.astype(F32) * nat[0].astype(F32)).T
    for head in range(2):
        dl[head : head + 1, :] = jnp.sum(
            product[head * HEAD_DIM : (head + 1) * HEAD_DIM, :], axis=0, keepdims=True
        )
        doh[head] = only_head(grads, head)
        qh[head] = only_head(mixed_ref[:, 0:LANES], head) * scale
    kt[...] = mixed_ref[:, LANES : 2 * LANES].T
    for c in range(3):
        cols = slice(c * LANES, (c + 1) * LANES)
        pj[c, 0:8, :] = jnp.zeros((8, LANES), F32)
        dm[c, length : length + 8, :] = jnp.zeros((8, LANES), F32)
        load_natural(member, [p[:, cols] for p in (p0, p1, p2, p3)], pj.at[c], size, 8)
    for first in range(0, length, KBLOCK):
        keys = mixed_ref[first : first + KBLOCK, LANES : 2 * LANES]
        values = mixed_ref[first : first + KBLOCK, 2 * LANES : 3 * LANES]
        sum_v = None
        sum_k = None
        for head in range(2):
            scores = dot_nt(keys, qh[head, first:, :])
            key_pos = lax.broadcasted_iota(jnp.int32, (KBLOCK, KBLOCK), 0)
            query_pos = lax.broadcasted_iota(jnp.int32, (KBLOCK, KBLOCK), 1)
            corner = jnp.where(key_pos <= query_pos, scores[:, :KBLOCK], NEGATIVE)
            if first + KBLOCK < length:
                scores = jnp.concatenate([corner, scores[:, KBLOCK:]], axis=1)
            else:
                scores = corner
            probs = jnp.exp(scores - lse_ref[0, head : head + 1, first:])
            grad_probs = dot_nt(values, doh[head, first:, :])
            grad_scores = (probs * (grad_probs - dl[head : head + 1, first:])).astype(BF16)
            part_v = dot_nn(probs.astype(BF16), doh[head, first:, :])
            part_k = dot_nn(grad_scores, qh[head, first:, :])
            sum_v = part_v if sum_v is None else sum_v + part_v
            sum_k = part_k if sum_k is None else sum_k + part_k
            lanes = slice(head * HEAD_DIM, (head + 1) * HEAD_DIM)
            part_q = dot_nn(kt[lanes, first : first + KBLOCK], grad_scores)
            if first == 0:
                dqa[lanes, :] = part_q
            else:
                dqa[lanes, first:] += part_q
        dm[1, first : first + KBLOCK, :] = sum_k
        dm[2, first : first + KBLOCK, :] = sum_v
    dm[0, 0:length, :] = dqa[...].T * HEAD_DIM ** (-0.5)
    for c in range(3):
        grad = dm[c, 0:length, :]
        for s in range(3):
            gconv_ref[3 * c + s : 3 * c + s + 1, :] = jnp.sum(
                grad * pj[c, 8 - s : 8 - s + length, :], axis=0, keepdims=True
            )
        total = taps_ref[0, 3 * c : 3 * c + 1, :] * grad
        total = total + taps_ref[0, 3 * c + 1 : 3 * c + 2, :] * dm[c, 1 : 1 + length, :]
        total = total + taps_ref[0, 3 * c + 2 : 3 * c + 3, :] * dm[c, 2 : 2 + length, :]
        nat[0] = total.astype(BF16)
        for slot in range(4):
            start = pl.multiple_of(lax.bitwise_xor(member, slot) * size, size)
            dest = (gown_ref, gsend_ref)[slot % 2]
            dest[slot // 2 * size : (slot // 2 + 1) * size, c * LANES : (c + 1) * LANES] = nat[
                0, pl.ds(start, size), :
            ]


def attend_back(pair, member, proj, mixed, lse, taps, own, send, grad_own, grad_recv):
    size = proj[0].shape[0]
    length = 4 * size
    half_spec = pl.BlockSpec((2 * size, LANES), lambda i: (0, pair))
    return pl.pallas_call(
        attend_back_kernel,
        grid=(1,),
        in_specs=[SMEM_SPEC]
        + [pl.BlockSpec((size, 3 * LANES), lambda i: (0, pair))] * 4
        + [
            pl.BlockSpec((length, 3 * LANES), lambda i: (0, pair)),
            pl.BlockSpec((1, 2, length), lambda i: (pair, 0, 0)),
            pl.BlockSpec((1, 16, LANES), lambda i: (pair, 0, 0)),
        ]
        + [half_spec] * 4,
        out_specs=[
            pl.BlockSpec((2 * size, 3 * LANES), lambda i: (0, 0)),
            pl.BlockSpec((2 * size, 3 * LANES), lambda i: (0, 0)),
            pl.BlockSpec((16, LANES), lambda i: (0, 0)),
        ],
        out_shape=[
            jax.ShapeDtypeStruct((2 * size, 3 * LANES), BF16),
            jax.ShapeDtypeStruct((2 * size, 3 * LANES), BF16),
            jax.ShapeDtypeStruct((16, LANES), F32),
        ],
        scratch_shapes=[
            pltpu.VMEM((3, 8 + length, LANES), F32),
            pltpu.VMEM((3, 8 + length, LANES), F32),
            pltpu.VMEM((2, length, LANES), BF16),
            pltpu.VMEM((2, length, LANES), BF16),
            pltpu.VMEM((LANES, length), BF16),
            pltpu.VMEM((8, length), F32),
            pltpu.VMEM((LANES, length), F32),
            pltpu.VMEM((2, length, LANES), BF16),
        ],
        compiler_params=params(),
        cost_estimate=pl.CostEstimate(
            flops=12 * 10**9, bytes_accessed=12 << 20, transcendentals=0
        ),
        name="attend_back",
    )(member, *proj, mixed, lse, taps, own, send, grad_own, grad_recv)


def ordered(chunks, order):
    bits = len(order)
    return [
        sum(((i >> (bits - 1 - n)) & 1) << order[n] for n in range(bits)) for i in range(chunks)
    ]


def split_store(m_ref, pieces, keep_ref, send_ref):
    flag = m_ref[0] == 0
    keep_ref[...] = jnp.where(flag, pieces[0], pieces[1]).astype(BF16).reshape(keep_ref.shape)
    send_ref[...] = jnp.where(flag, pieces[1], pieces[0]).astype(BF16).reshape(send_ref.shape)


def rows_kernel(order, m_ref, x_ref, y_ref, keep_ref, send_ref):
    total = dot_tn(x_ref[...], y_ref[...])
    chunks = 2 ** len(order)
    size = total.shape[0] // chunks
    pieces = []
    for k in ordered(chunks, order):
        for tile in range(total.shape[1] // LANES):
            pieces.append(
                total[k * size : (k + 1) * size, tile * LANES : (tile + 1) * LANES]
            )
    middle = len(pieces) // 2
    split_store(
        m_ref,
        [jnp.concatenate(pieces[:middle], axis=0), jnp.concatenate(pieces[middle:], axis=0)],
        keep_ref,
        send_ref,
    )


def rows_grad(flag, x, y, order, name):
    tokens, rows = x.shape
    cols = y.shape[1]
    chunks = 2 ** len(order)
    tile = 2 * LANES
    block = rows // chunks * 2
    out = jax.ShapeDtypeStruct((chunks // 2, rows * cols // chunks // LANES, LANES), BF16)
    spec = pl.BlockSpec((chunks // 2, block, LANES), lambda j: (0, j, 0))
    return pl.pallas_call(
        functools.partial(rows_kernel, order),
        grid=(cols // tile,),
        in_specs=[
            SMEM_SPEC,
            pl.BlockSpec((tokens, rows), lambda j: (0, 0)),
            pl.BlockSpec((tokens, tile), lambda j: (0, j)),
        ],
        out_specs=[spec, spec],
        out_shape=[out, out],
        compiler_params=params(),
        cost_estimate=pl.CostEstimate(
            flops=2 * tokens * rows * cols, bytes_accessed=16 << 20, transcendentals=0
        ),
        name=name,
    )(flag, x, y)


def rows_restore(flat, rows, cols):
    return flat.reshape(cols // (2 * LANES), 2, rows, LANES).transpose(2, 0, 1, 3).reshape(rows, cols)


def whole_kernel(order, m_ref, x_ref, y_ref, keep_ref, send_ref):
    total = dot_tn(x_ref[...], y_ref[...])
    chunks = 2 ** len(order)
    size = total.shape[0] // chunks
    pieces = [total[k * size : (k + 1) * size] for k in ordered(chunks, order)]
    middle = len(pieces) // 2
    split_store(
        m_ref,
        [jnp.concatenate(pieces[:middle], axis=0), jnp.concatenate(pieces[middle:], axis=0)],
        keep_ref,
        send_ref,
    )


def whole_grad(flag, x, y, order, tile, name):
    tokens, rows = x.shape
    cols = y.shape[1]
    chunks = 2 ** len(order)
    out = jax.ShapeDtypeStruct((chunks // 2, rows // chunks, cols), BF16)
    spec = pl.BlockSpec((chunks // 2, rows // chunks, tile), lambda j: (0, 0, j))
    return pl.pallas_call(
        functools.partial(whole_kernel, order),
        grid=(cols // tile,),
        in_specs=[
            SMEM_SPEC,
            pl.BlockSpec((tokens, rows), lambda j: (0, 0)),
            pl.BlockSpec((tokens, tile), lambda j: (0, j)),
        ],
        out_specs=[spec, spec],
        out_shape=[out, out],
        compiler_params=params(),
        cost_estimate=pl.CostEstimate(
            flops=2 * tokens * rows * cols, bytes_accessed=16 << 20, transcendentals=0
        ),
        name=name,
    )(flag, x, y)


def qkv_kernel(order, m_ref, n0, n1, n2, n3, gown_ref, gsend_ref, keep_ref, send_ref):
    size = n0.shape[0]
    total = dot_tn(n0[...], gown_ref[0:size, :])
    total = total + dot_tn(n2[...], gown_ref[size:, :])
    total = total + dot_tn(n1[...], gsend_ref[0:size, :])
    total = total + dot_tn(n3[...], gsend_ref[size:, :])
    chunks = 2 ** len(order)
    rows = total.shape[0] // chunks
    pieces = [total[k * rows : (k + 1) * rows] for k in ordered(chunks, order)]
    middle = chunks // 2
    split_store(
        m_ref,
        [jnp.concatenate(pieces[:middle], axis=0), jnp.concatenate(pieces[middle:], axis=0)],
        keep_ref,
        send_ref,
    )


def qkv_grad(flag, normed, grad_own, grad_send, order):
    rows = normed[0].shape[1]
    cols = grad_own.shape[1]
    chunks = 2 ** len(order)
    out = jax.ShapeDtypeStruct((chunks // 2, rows // chunks, cols), BF16)
    return pl.pallas_call(
        functools.partial(qkv_kernel, order),
        in_specs=[SMEM_SPEC] + [pl.BlockSpec(memory_space=pltpu.VMEM)] * 6,
        out_specs=[pl.BlockSpec(memory_space=pltpu.VMEM)] * 2,
        out_shape=[out, out],
        compiler_params=params(),
        cost_estimate=pl.CostEstimate(
            flops=8 * normed[0].shape[0] * rows * cols, bytes_accessed=8 << 20, transcendentals=0
        ),
        name="qkv_grad",
    )(flag, *normed, grad_own, grad_send)


def input_grad_kernel(
    o0, o1, o2, r0, r1, r2, wown_ref, woth_ref, x_ref, gres_ref, gain_ref, out_ref, sums_ref, buf
):
    for n, ref in enumerate((o0, o1, o2, r0, r1, r2)):
        buf[:, n * 3 * LANES : (n + 1) * 3 * LANES] = ref[...]
    cols = 9 * LANES
    grad = dot_nt(buf[:, :cols], wown_ref[...]) + dot_nt(buf[:, cols:], woth_ref[...])
    scaled, inv_std = norm_stats(x_ref[...].astype(F32))
    sums_ref[0:1, :] = jnp.sum(grad * scaled, axis=0, keepdims=True)
    sums_ref[1:2, :] = jnp.sum(grad, axis=0, keepdims=True)
    total = gres_ref[...] + norm_backward(grad, gain_ref[...], scaled, inv_std)
    out_ref[...] = total.astype(BF16)


def input_grad(slot, owns, recvs, w_own, w_oth, x, grad_residual, gain):
    rows, width = x.shape
    part = pl.BlockSpec((rows, 3 * LANES), lambda i: (slot, 0))
    full = lambda a: pl.BlockSpec(a.shape, lambda i: (0, 0))
    return pl.pallas_call(
        input_grad_kernel,
        grid=(1,),
        in_specs=[part] * 6
        + [full(w_own), full(w_oth), full(x)]
        + [pl.BlockSpec((rows, width), lambda i: (slot, 0)), full(gain)],
        out_specs=[
            pl.BlockSpec((rows, width), lambda i: (0, 0)),
            pl.BlockSpec((8, width), lambda i: (0, 0)),
        ],
        out_shape=[
            jax.ShapeDtypeStruct((rows, width), BF16),
            jax.ShapeDtypeStruct((8, width), F32),
        ],
        scratch_shapes=[pltpu.VMEM((rows, 18 * LANES), BF16)],
        compiler_params=params(),
        cost_estimate=pl.CostEstimate(
            flops=2 * rows * width * 18 * LANES, bytes_accessed=8 << 20, transcendentals=0
        ),
        name="input_grad",
    )(*owns, *recvs, w_own, w_oth, x, grad_residual, gain)


def halve(keep, recv, stages):
    parts = [(keep, 0), (recv, 0)]
    count = keep.shape[0]
    for axis, perm, bit in stages:
        count = count // 2

        def take(which):
            total = None
            for array, start in parts:
                piece = lax.dynamic_slice_in_dim(array, start + which * count, count, 0)
                piece = piece.astype(F32)
                total = piece if total is None else total + piece
            return total

        arrived = lax.ppermute(take(1 - bit).astype(BF16), axis, perm)
        parts = [(array, start + bit * count) for array, start in parts] + [(arrived, 0)]
    total = None
    for array, start in parts:
        piece = lax.dynamic_slice_in_dim(array, start, count, 0).astype(F32)
        total = piece if total is None else total + piece
    return total


def everyone(value, hops):
    for axis, perm in hops:
        value = value + lax.ppermute(value, axis, perm)
    return value


def on_device(
    tokens,
    cotangent,
    lengths,
    pre_attn_gain,
    pre_attn_bias,
    qkv_weight,
    conv_weight,
    out_weight,
    pre_ffn_gain,
    pre_ffn_bias,
    up_weight,
    up_bias,
    down_weight,
    down_bias,
):
    groups = lax.axis_size("mp")
    batch_groups = lax.axis_size("batch")
    devices = groups * batch_groups
    member = lax.axis_index("mp")
    batch = lax.axis_index("batch")
    seqs, rows, width = tokens.shape
    ff = up_weight.shape[1]
    quarter = width // groups
    assert groups == 4 and seqs == 2 and quarter % HEAD_DIM == 0
    fast = batch_groups == 8 and (width // devices) % 8 == 0
    half = member // 2
    core = member % 2
    me = member.astype(jnp.int32).reshape(1)
    gain_attn = pre_attn_gain.astype(F32).reshape(1, width)
    bias_attn = pre_attn_bias.astype(F32).reshape(1, width)
    gain_ffn = pre_ffn_gain.astype(F32)
    bias_ffn = pre_ffn_bias.astype(F32)

    def swap_core(value):
        return lax.ppermute(value, "mp", CORE)

    def swap_pair(value):
        return lax.ppermute(value, "mp", PAIR)

    def pick(value, index):
        return lax.dynamic_index_in_dim(value, index, 0, keepdims=False)

    tok_own = pick(tokens, half)
    tok_pair = swap_pair(pick(tokens, 1 - half))
    tok_core = swap_core(tok_own)
    tok_cross = swap_core(tok_pair)
    cot_pair = swap_pair(pick(cotangent, 1 - half))
    cot = jnp.concatenate([pick(cotangent, half), cot_pair], axis=0)
    length = pick(lengths, half)
    row = jnp.arange(rows, dtype=jnp.int32)
    row_pos = jnp.concatenate([member * rows + row, jnp.bitwise_xor(member, 2) * rows + row])
    valid = (row_pos < length)[:, None]

    pairs = width // 2 // LANES
    by_core = qkv_weight.reshape(3, width, 2, 2, quarter).transpose(3, 1, 0, 2, 4)
    by_core = by_core.reshape(2, width, 3, pairs, LANES).transpose(0, 1, 3, 2, 4)
    by_core = by_core.reshape(2, width, 3 * width // 2)
    w_own = pick(by_core, core)
    w_oth = pick(by_core, 1 - core)
    taps = conv_weight.shape[1]
    taps_own = pick(conv_weight.reshape(3, taps, 2, 2, quarter).transpose(3, 0, 1, 2, 4), core)
    taps_own = taps_own.astype(F32).reshape(3 * taps, pairs, LANES).transpose(1, 0, 2)
    taps_own = jnp.pad(taps_own, ((0, 0), (0, 16 - 3 * taps), (0, 0)))
    out_core = out_weight.reshape(2, 2, quarter, width).transpose(1, 0, 2, 3)
    out_core = out_core.reshape(2, width // 2, width)
    out_all = jnp.concatenate([pick(out_core, core), pick(out_core, 1 - core)], axis=0)

    toks = (tok_own, tok_core, tok_pair, tok_cross)
    normed, proj = zip(*[project(t, gain_attn, bias_attn, w_own) for t in toks])
    mixed, heads_own, heads_send, lse = attend(me, proj, taps_own)
    heads_recv = swap_core(heads_send)
    heads_all = jnp.concatenate([heads_own, heads_recv], axis=1)

    mine = jnp.concatenate([tok_own, tok_pair], axis=0).astype(F32)
    residual = mine + jnp.dot(heads_all, out_all, preferred_element_type=F32)
    scaled_ffn, inv_ffn = norm_stats(residual)
    normed_ffn = (scaled_ffn * gain_ffn + bias_ffn).astype(BF16)
    hidden_pre = jnp.dot(normed_ffn, up_weight, preferred_element_type=F32) + up_bias.astype(F32)
    relu_part = jnp.maximum(hidden_pre, 0.0)
    activated = jnp.square(relu_part).astype(BF16)
    ffn_out = jnp.dot(activated, down_weight, preferred_element_type=F32)
    ffn_out = ffn_out + down_bias.astype(F32)
    result = jnp.where(valid, residual + ffn_out, 0.0).astype(BF16)
    result_pair = swap_pair(result[rows:])
    grad_ffn = jnp.where(valid, cot, jnp.zeros_like(cot))
    grad_y = grad_ffn.astype(F32)
    grad_down_bias = jnp.sum(grad_y, axis=0)
    grad_act = jnp.einsum("td,fd->tf", grad_ffn, down_weight, preferred_element_type=F32)
    grad_pre = (2.0 * relu_part * grad_act).astype(BF16)
    grad_up_bias = jnp.sum(grad_pre.astype(F32), axis=0)
    grad_normed_ffn = jnp.einsum("tf,df->td", grad_pre, up_weight, preferred_element_type=F32)
    grad_gain_ffn = jnp.sum(grad_normed_ffn * scaled_ffn, axis=0)
    grad_bias_ffn = jnp.sum(grad_normed_ffn, axis=0)
    grad_residual = grad_y + norm_backward(grad_normed_ffn, gain_ffn, scaled_ffn, inv_ffn)
    grad_attended = grad_residual.astype(BF16)
    grad_heads = jnp.einsum("td,ed->te", grad_attended, out_all, preferred_element_type=F32)
    grad_heads = grad_heads.astype(BF16)
    grad_own = grad_heads[:, : width // 2]
    grad_recv = swap_core(grad_heads[:, width // 2 :])

    flat_core = core.astype(jnp.int32).reshape(1)
    g_own, g_send, g_recv, g_conv = [], [], [], []
    for pair in range(pairs):
        own, send, conv = attend_back(
            pair, me, proj, mixed, lse, taps_own, heads_own, heads_send, grad_own, grad_recv
        )
        g_own.append(own)
        g_send.append(send)
        g_recv.append(swap_core(send))
        g_conv.append(conv)
    grad_in_pair, sums_pair = input_grad(
        1, g_own, g_recv, w_own, w_oth, tok_pair, grad_residual, gain_attn
    )
    grad_in_back = swap_pair(grad_in_pair)
    grad_in_own, sums_own = input_grad(
        0, g_own, g_recv, w_own, w_oth, tok_own, grad_residual, gain_attn
    )

    def both(first, second):
        return jnp.stack([jnp.where(half == 0, first, second), jnp.where(half == 0, second, first)])

    result_all = both(result[:rows], result_pair)
    tokens_grad = both(grad_in_own, grad_in_back)

    sums = sums_pair + sums_own
    conv_own = jnp.stack(g_conv)[:, : 3 * taps].transpose(1, 0, 2).reshape(3, taps, 2, quarter)
    conv_full = jnp.zeros((3, taps, 2, 2, quarter), F32)
    conv_full = lax.dynamic_update_slice_in_dim(conv_full, conv_own[:, :, :, None], core, 3)
    conv_full = conv_full.reshape(3 * taps, width)
    early = jnp.concatenate(
        [
            grad_up_bias.reshape(ff // width, width),
            grad_down_bias[None],
            grad_gain_ffn[None],
            grad_bias_ffn[None],
        ],
        axis=0,
    )
    late = jnp.concatenate([sums[0:2], conv_full], axis=0)
    index = batch * groups + member
    share = width // devices

    if not fast:
        axes = ("batch", "mp")
        grad_up = jnp.einsum("td,tf->df", normed_ffn, grad_pre, preferred_element_type=F32)
        grad_down = jnp.einsum("tf,td->fd", activated, grad_ffn, preferred_element_type=F32)
        grad_out = jnp.einsum("te,td->ed", heads_all, grad_attended, preferred_element_type=F32)
        grad_out = grad_out.reshape(2, 2, quarter, width)
        grad_out = jnp.where(core == 0, grad_out, grad_out[::-1])
        grad_out = grad_out.transpose(1, 0, 2, 3).reshape(width, width)
        grad_qkv = 0.0
        for n, (norm, slot) in enumerate(zip(normed, (0, 0, 1, 1))):
            source = (g_own, g_send)[n % 2]
            grads = jnp.concatenate([g[slot * rows : (slot + 1) * rows] for g in source], axis=1)
            grad_qkv = grad_qkv + jnp.einsum("td,te->de", norm, grads, preferred_element_type=F32)
        grad_qkv = grad_qkv.reshape(width, pairs, 3, LANES).transpose(2, 0, 1, 3)
        grad_qkv = grad_qkv.reshape(3, width, 2, 1, quarter)
        qkv_full = jnp.zeros((3, width, 2, 2, quarter), F32)
        qkv_full = lax.dynamic_update_slice_in_dim(qkv_full, grad_qkv, core, 3)
        part = width // batch_groups
        qkv_flat = qkv_full.reshape(3, batch_groups, part, groups, quarter)
        qkv_flat = qkv_flat.transpose(1, 3, 0, 2, 4).reshape(devices * 3 * part, quarter)

        def scatter(value):
            return lax.psum_scatter(value, axes, scatter_dimension=0, tiled=True)

        early_sum = lax.psum(early, axes)
        late_sum = lax.psum(late, axes)
        qkv_out = scatter(qkv_flat).reshape(3, part, quarter)
        up_out, down_out, out_out = scatter(grad_up), scatter(grad_down), scatter(grad_out)
    else:
        bits = {
            "core": core,
            "pair": half,
            "x": batch % 2,
            "z0": batch // 2 % 2,
            "z1": batch // 4,
        }
        flip = {
            "core": ("mp", CORE),
            "pair": ("mp", PAIR),
            "x": ("batch", [(i, i ^ 1) for i in range(8)]),
            "z0": ("batch", [(i, i ^ 2) for i in range(8)]),
            "z1": ("batch", [(i, i ^ 4) for i in range(8)]),
        }
        place = {"core": 0, "pair": 1, "x": 2, "z0": 3, "z1": 4}
        hops = [flip[n] for n in ("core", "pair", "x", "z0", "z1")]

        def reduce(grads, names):
            keep, send = grads
            axis, perm = flip[names[0]]
            recv = lax.ppermute(send, axis, perm)
            return halve(keep, recv, [flip[n] + (bits[n],) for n in names[1:]])

        first = ("core", "pair", "x", "z0", "z1")
        second = ("core", "x", "pair", "z0", "z1")
        third = ("x", "z0", "z1")
        order_first = [place[n] for n in first]
        order_second = [place[n] for n in second]
        order_third = [place[n] - 2 for n in third]
        flag_core = flat_core
        flag_x = bits["x"].astype(jnp.int32).reshape(1)
        grads_down = whole_grad(
            flag_core, activated, grad_ffn, order_second, 2 * LANES, "down_grad"
        )
        grads_up = rows_grad(flag_core, normed_ffn, grad_pre, order_first, "up_grad")
        out_order = jnp.where(core == 0, 0, 1)
        heads_sorted = jnp.concatenate(
            [
                jnp.where(core == 0, heads_own, heads_recv)[:, :quarter],
                jnp.where(core == 0, heads_recv, heads_own)[:, :quarter],
                jnp.where(core == 0, heads_own, heads_recv)[:, quarter:],
                jnp.where(core == 0, heads_recv, heads_own)[:, quarter:],
            ],
            axis=1,
        )
        grads_out = rows_grad(flag_core, heads_sorted, grad_attended, order_second, "out_grad")
        down_out = reduce(grads_down, second).reshape(ff // devices, width)
        up_out = rows_restore(reduce(grads_up, first), share, ff)
        out_out = rows_restore(reduce(grads_out, second), share, width)
        qkv_parts = []
        for pair in range(pairs):
            grads = qkv_grad(flag_x, normed, g_own[pair], g_send[pair], order_third)
            total = reduce(grads, third)
            qkv_parts.append(total.reshape(width // batch_groups, 3, LANES))
        qkv_all = jnp.stack(qkv_parts, axis=1).transpose(2, 0, 1, 3)
        qkv_all = qkv_all.reshape(3, width // batch_groups, 2, quarter).transpose(2, 0, 1, 3)
        arrived = lax.ppermute(pick(qkv_all, 1 - half).astype(BF16), "mp", PAIR)
        qkv_out = pick(qkv_all, half) + arrived.astype(F32)
        early_sum = everyone(early, hops)
        late_sum = everyone(late, hops)

    def own_part(value):
        count = value.shape[0]
        return pick(value.reshape(count, devices, share).transpose(1, 0, 2), index)

    early_own = own_part(early_sum[ff // width :])
    late_own = own_part(late_sum)
    up_bias_own = pick(early_sum[: ff // width].reshape(devices, ff // devices), index)
    return (
        result_all,
        tokens_grad,
        late_own[0],
        late_own[1],
        qkv_out,
        late_own[2:].reshape(3, taps, share),
        out_out,
        early_own[1],
        early_own[2],
        up_out,
        up_bias_own,
        down_out,
        early_own[0],
    )


def solution(mesh):
    in_specs = (
        P("batch", "mp", None),
        P("batch", "mp", None),
        P("batch"),
    ) + (P(),) * 11
    out_specs = (
        P("batch", "mp", None),
        P("batch", "mp", None),
        P(("batch", "mp")),
        P(("batch", "mp")),
        P(None, "batch", "mp"),
        P(None, None, ("batch", "mp")),
        P(("batch", "mp"), None),
        P(("batch", "mp")),
        P(("batch", "mp")),
        P(("batch", "mp"), None),
        P(("batch", "mp")),
        P(("batch", "mp"), None),
        P(("batch", "mp")),
    )
    return jax.shard_map(
        on_device, mesh=mesh, in_specs=in_specs, out_specs=out_specs, check_vma=False
    )
```

```python
import functools

import jax
import jax.numpy as jnp
from jax import lax
from jax.experimental import pallas as pl
from jax.experimental.pallas import tpu as pltpu
from jax.sharding import PartitionSpec as P

HEAD_DIM = 64
LANES = 128
EPSILON = 1e-05
NEGATIVE = -1000000000.0
QBLOCK = 512
KBLOCK = 256
VMEM_BYTES = 60 << 20
F32 = jnp.float32
BF16 = jnp.bfloat16

CORE = [(i, i ^ 1) for i in range(4)]
PAIR = [(i, i ^ 2) for i in range(4)]


def dot_nt(left, right):
    return lax.dot_general(left, right, (((1,), (1,)), ((), ())), preferred_element_type=F32)


def dot_nn(left, right):
    return lax.dot_general(left, right, (((1,), (0,)), ((), ())), preferred_element_type=F32)


def dot_tn(left, right):
    return lax.dot_general(left, right, (((0,), (0,)), ((), ())), preferred_element_type=F32)


def params():
    return pltpu.CompilerParams(vmem_limit_bytes=VMEM_BYTES)


def once(shape, index_map):
    return pl.BlockSpec(shape, index_map, pipeline_mode=pl.Buffered(1))


def still(array):
    return once(array.shape, lambda *_: (0,) * array.ndim)


SMEM_SPEC = pl.BlockSpec(memory_space=pltpu.SMEM)


def norm_stats(values):
    center = values - jnp.mean(values, axis=-1, keepdims=True)
    inv_std = lax.rsqrt(jnp.mean(center * center, axis=-1, keepdims=True) + EPSILON)
    return center * inv_std, inv_std


def norm_backward(grad_out, norm_gain, scaled, inv_std):
    weighted = grad_out * norm_gain
    return inv_std * (
        weighted
        - jnp.mean(weighted, axis=-1, keepdims=True)
        - scaled * jnp.mean(weighted * scaled, axis=-1, keepdims=True)
    )


def project_kernel(s_ref, x_ref, gain_ref, bias_ref, w_ref, normed_ref, proj_ref):
    tile = 128
    for first in range(0, x_ref.shape[0], tile):
        rows = slice(first, first + tile)
        scaled, _ = norm_stats(x_ref[rows, :].astype(F32))
        normed = (scaled * gain_ref[...] + bias_ref[...]).astype(BF16)
        normed_ref[:, rows] = normed.T
        proj_ref[rows, :] = dot_nn(normed, w_ref[...]).astype(BF16)


def project(scalars, x, gain, bias, weights):
    rows, width = x.shape
    cols = weights.shape[1] // 2
    return pl.pallas_call(
        project_kernel,
        grid_spec=pltpu.PrefetchScalarGridSpec(
            num_scalar_prefetch=1,
            grid=(1,),
            in_specs=[
                pl.BlockSpec((rows, width), lambda i, s: (0, 0)),
                pl.BlockSpec((1, width), lambda i, s: (0, 0)),
                pl.BlockSpec((1, width), lambda i, s: (0, 0)),
                pl.BlockSpec((width, cols), lambda i, s: (0, s[0])),
            ],
            out_specs=[
                pl.BlockSpec((width, rows), lambda i, s: (0, 0)),
                pl.BlockSpec((rows, cols), lambda i, s: (0, 0)),
            ],
        ),
        out_shape=[
            jax.ShapeDtypeStruct((width, rows), BF16),
            jax.ShapeDtypeStruct((rows, cols), BF16),
        ],
        compiler_params=params(),
        cost_estimate=pl.CostEstimate(
            flops=2 * rows * width * cols, bytes_accessed=6 * rows * width, transcendentals=0
        ),
        name="project",
    )(scalars, x, gain, bias, weights)


def store_parts(flag, parts, keep_ref, send_ref):
    first = jnp.concatenate(parts[0], axis=0)
    second = jnp.concatenate(parts[1], axis=0)
    keep = jnp.where(flag == 0, first, second)
    send = jnp.where(flag == 0, second, first)
    keep_ref[...] = keep.astype(BF16).reshape(keep_ref.shape)
    send_ref[...] = send.astype(BF16).reshape(send_ref.shape)


def lane_tiles(values):
    return [values[:, n : n + LANES] for n in range(0, values.shape[1], LANES)]


def only_head(values, head):
    lane = lax.broadcasted_iota(jnp.int32, values.shape, 1)
    return jnp.where((lane // HEAD_DIM) == head, values, jnp.zeros_like(values))


def load_natural(member, blocks, dest, size, shift=0):
    for slot, block in enumerate(blocks):
        start = pl.multiple_of(lax.bitwise_xor(member, slot) * size, 8) + shift
        start = pl.multiple_of(start, 8)
        dest[pl.ds(start, size), :] = block.astype(dest.dtype)


def attend_kernel(
    m_ref, p0, p1, p2, p3, taps_ref, mixed_ref, own_ref, send_ref, lse_ref, pj, kh, vt, on, qs
):
    member = m_ref[1]
    size = p0.shape[0]
    length = 4 * size
    scale = jnp.asarray(HEAD_DIM ** (-0.5), BF16)
    for c in range(3):
        cols = slice(c * LANES, (c + 1) * LANES)
        pj[c, 0:8, :] = jnp.zeros((8, LANES), F32)
        load_natural(member, [p[:, cols] for p in (p0, p1, p2, p3)], pj.at[c], size, 8)
    for c in range(3):
        total = taps_ref[0, 3 * c : 3 * c + 1, :] * pj[c, 8 : 8 + length, :]
        total = total + taps_ref[0, 3 * c + 1 : 3 * c + 2, :] * pj[c, 7 : 7 + length, :]
        total = total + taps_ref[0, 3 * c + 2 : 3 * c + 3, :] * pj[c, 6 : 6 + length, :]
        mixed = total.astype(BF16)
        mixed_ref[:, c * LANES : (c + 1) * LANES] = mixed
        if c == 0:
            qs[...] = mixed * scale
        elif c == 1:
            kh[0] = only_head(mixed, 0)
            kh[1] = only_head(mixed, 1)
        else:
            vt[...] = mixed.T
    for first in range(0, length, QBLOCK):
        queries = qs[first : first + QBLOCK, :]
        keys = first + QBLOCK
        outs = []
        for head in range(2):
            scores = dot_nt(kh[head, 0:keys, :], queries)
            key_pos = lax.broadcasted_iota(jnp.int32, (QBLOCK, QBLOCK), 0)
            query_pos = lax.broadcasted_iota(jnp.int32, (QBLOCK, QBLOCK), 1)
            corner = jnp.where(key_pos <= query_pos, scores[first:keys, :], NEGATIVE)
            if first:
                scores = jnp.concatenate([scores[:first, :], corner], axis=0)
            else:
                scores = corner
            top = jnp.max(scores, axis=0, keepdims=True)
            weights = jnp.exp(scores - top)
            total = jnp.sum(weights, axis=0, keepdims=True)
            part = dot_nn(
                vt[head * HEAD_DIM : (head + 1) * HEAD_DIM, 0:keys], weights.astype(BF16)
            )
            outs.append(part * (1.0 / total))
            lse_ref[0, head : head + 1, first : first + QBLOCK] = top + jnp.log(total)
        on[first : first + QBLOCK, :] = jnp.concatenate(outs, axis=0).T.astype(BF16)
    for slot in range(4):
        start = pl.multiple_of(lax.bitwise_xor(member, slot) * size, size)
        block = on[pl.ds(start, size), :]
        dest = (own_ref, send_ref)[slot % 2]
        dest[slot // 2 * size : (slot // 2 + 1) * size, :] = block


def attend(member, proj, taps):
    size = proj[0].shape[0]
    pairs = proj[0].shape[1] // (3 * LANES)
    length = 4 * size
    width = pairs * LANES
    return pl.pallas_call(
        attend_kernel,
        grid=(pairs,),
        in_specs=[SMEM_SPEC]
        + [pl.BlockSpec((size, 3 * LANES), lambda p: (0, p))] * 4
        + [pl.BlockSpec((1, 16, LANES), lambda p: (p, 0, 0))],
        out_specs=[
            pl.BlockSpec((length, 3 * LANES), lambda p: (0, p)),
            pl.BlockSpec((2 * size, LANES), lambda p: (0, p)),
            pl.BlockSpec((2 * size, LANES), lambda p: (0, p)),
            pl.BlockSpec((1, 2, length), lambda p: (p, 0, 0)),
        ],
        out_shape=[
            jax.ShapeDtypeStruct((length, 3 * width), BF16),
            jax.ShapeDtypeStruct((2 * size, width), BF16),
            jax.ShapeDtypeStruct((2 * size, width), BF16),
            jax.ShapeDtypeStruct((pairs, 2, length), F32),
        ],
        scratch_shapes=[
            pltpu.VMEM((3, 8 + length, LANES), F32),
            pltpu.VMEM((2, length, LANES), BF16),
            pltpu.VMEM((LANES, length), BF16),
            pltpu.VMEM((length, LANES), BF16),
            pltpu.VMEM((length, LANES), BF16),
        ],
        compiler_params=params(),
        cost_estimate=pl.CostEstimate(
            flops=pairs * 14 * 10**9, bytes_accessed=12 << 20, transcendentals=0
        ),
        name="attend",
    )(member, *proj, taps)


def attend_back_kernel(
    m_ref,
    p0,
    p1,
    p2,
    p3,
    mixed_ref,
    lse_ref,
    taps_ref,
    own_ref,
    send_ref,
    down_ref,
    drecv_ref,
    n0,
    n1,
    n2,
    n3,
    gown_ref,
    gsend_ref,
    gconv_ref,
    keep_ref,
    give_ref,
    pj,
    dm,
    qh,
    doh,
    kt,
    dl,
    dqa,
    nat,
    gp,
):
    member = m_ref[1]
    size = p0.shape[0]
    length = 4 * size
    scale = jnp.asarray(HEAD_DIM ** (-0.5), BF16)
    halves = [slice(0, size), slice(size, 2 * size)]
    load_natural(
        member,
        [own_ref[halves[0]], send_ref[halves[0]], own_ref[halves[1]], send_ref[halves[1]]],
        nat.at[0],
        size,
    )
    load_natural(
        member,
        [down_ref[halves[0]], drecv_ref[halves[0]], down_ref[halves[1]], drecv_ref[halves[1]]],
        nat.at[1],
        size,
    )
    grads = nat[1]
    product = (grads.astype(F32) * nat[0].astype(F32)).T
    for head in range(2):
        dl[head : head + 1, :] = jnp.sum(
            product[head * HEAD_DIM : (head + 1) * HEAD_DIM, :], axis=0, keepdims=True
        )
        doh[head] = only_head(grads, head)
        qh[head] = only_head(mixed_ref[:, 0:LANES], head) * scale
    kt[...] = mixed_ref[:, LANES : 2 * LANES].T
    for c in range(3):
        cols = slice(c * LANES, (c + 1) * LANES)
        pj[c, 0:8, :] = jnp.zeros((8, LANES), F32)
        dm[c, length : length + 8, :] = jnp.zeros((8, LANES), F32)
        load_natural(member, [p[:, cols] for p in (p0, p1, p2, p3)], pj.at[c], size, 8)
    for first in range(0, length, KBLOCK):
        keys = mixed_ref[first : first + KBLOCK, LANES : 2 * LANES]
        values = mixed_ref[first : first + KBLOCK, 2 * LANES : 3 * LANES]
        sum_v = None
        sum_k = None
        for head in range(2):
            scores = dot_nt(keys, qh[head, first:, :])
            key_pos = lax.broadcasted_iota(jnp.int32, (KBLOCK, KBLOCK), 0)
            query_pos = lax.broadcasted_iota(jnp.int32, (KBLOCK, KBLOCK), 1)
            corner = jnp.where(key_pos <= query_pos, scores[:, :KBLOCK], NEGATIVE)
            if first + KBLOCK < length:
                scores = jnp.concatenate([corner, scores[:, KBLOCK:]], axis=1)
            else:
                scores = corner
            probs = jnp.exp(scores - lse_ref[0, head : head + 1, first:])
            grad_probs = dot_nt(values, doh[head, first:, :])
            grad_scores = (probs * (grad_probs - dl[head : head + 1, first:])).astype(BF16)
            part_v = dot_nn(probs.astype(BF16), doh[head, first:, :])
            part_k = dot_nn(grad_scores, qh[head, first:, :])
            sum_v = part_v if sum_v is None else sum_v + part_v
            sum_k = part_k if sum_k is None else sum_k + part_k
            lanes = slice(head * HEAD_DIM, (head + 1) * HEAD_DIM)
            part_q = dot_nn(kt[lanes, first : first + KBLOCK], grad_scores)
            if first == 0:
                dqa[lanes, :] = part_q
            else:
                dqa[lanes, first:] += part_q
        dm[1, first : first + KBLOCK, :] = sum_k
        dm[2, first : first + KBLOCK, :] = sum_v
    dm[0, 0:length, :] = dqa[...].T * HEAD_DIM ** (-0.5)
    for c in range(3):
        grad = dm[c, 0:length, :]
        for s in range(3):
            gconv_ref[3 * c + s : 3 * c + s + 1, :] = jnp.sum(
                grad * pj[c, 8 - s : 8 - s + length, :], axis=0, keepdims=True
            )
        total = taps_ref[0, 3 * c : 3 * c + 1, :] * grad
        total = total + taps_ref[0, 3 * c + 1 : 3 * c + 2, :] * dm[c, 1 : 1 + length, :]
        total = total + taps_ref[0, 3 * c + 2 : 3 * c + 3, :] * dm[c, 2 : 2 + length, :]
        gp[:, c * LANES : (c + 1) * LANES] = total.astype(BF16)
    total = None
    for slot, norm in enumerate((n0, n1, n2, n3)):
        start = pl.multiple_of(lax.bitwise_xor(member, slot) * size, size)
        dest = (gown_ref, gsend_ref)[slot % 2]
        block = gp[pl.ds(start, size), :]
        dest[slot // 2 * size : (slot // 2 + 1) * size, :] = block
        part = dot_nn(norm[...], block)
        total = part if total is None else total + part
    rows = total.shape[0] // 8
    store_parts(
        m_ref[3],
        [
            [total[b * rows : (b + 1) * rows] for b in (x, x + 4, x + 2, x + 6)]
            for x in range(2)
        ],
        keep_ref,
        give_ref,
    )


def attend_back(pair, member, proj, mixed, lse, taps, own, send, grad_own, grad_recv, normed):
    size = proj[0].shape[0]
    length = 4 * size
    width = normed[0].shape[0]
    part = jax.ShapeDtypeStruct((2, 2, width // 8, 3 * LANES), BF16)
    half_spec = pl.BlockSpec((2 * size, LANES), lambda i: (0, pair))
    return pl.pallas_call(
        attend_back_kernel,
        grid=(1,),
        in_specs=[SMEM_SPEC]
        + [pl.BlockSpec((size, 3 * LANES), lambda i: (0, pair))] * 4
        + [
            pl.BlockSpec((length, 3 * LANES), lambda i: (0, pair)),
            pl.BlockSpec((1, 2, length), lambda i: (pair, 0, 0)),
            pl.BlockSpec((1, 16, LANES), lambda i: (pair, 0, 0)),
        ]
        + [half_spec] * 4
        + [pl.BlockSpec((width, size), lambda i: (0, 0))] * 4,
        out_specs=[
            pl.BlockSpec((2 * size, 3 * LANES), lambda i: (0, 0)),
            pl.BlockSpec((2 * size, 3 * LANES), lambda i: (0, 0)),
            pl.BlockSpec((16, LANES), lambda i: (0, 0)),
            pl.BlockSpec(part.shape, lambda i: (0, 0, 0, 0)),
            pl.BlockSpec(part.shape, lambda i: (0, 0, 0, 0)),
        ],
        out_shape=[
            jax.ShapeDtypeStruct((2 * size, 3 * LANES), BF16),
            jax.ShapeDtypeStruct((2 * size, 3 * LANES), BF16),
            jax.ShapeDtypeStruct((16, LANES), F32),
            part,
            part,
        ],
        scratch_shapes=[
            pltpu.VMEM((3, 8 + length, LANES), F32),
            pltpu.VMEM((3, 8 + length, LANES), F32),
            pltpu.VMEM((2, length, LANES), BF16),
            pltpu.VMEM((2, length, LANES), BF16),
            pltpu.VMEM((LANES, length), BF16),
            pltpu.VMEM((8, length), F32),
            pltpu.VMEM((LANES, length), F32),
            pltpu.VMEM((2, length, LANES), BF16),
            pltpu.VMEM((length, 3 * LANES), BF16),
        ],
        compiler_params=params(),
        cost_estimate=pl.CostEstimate(
            flops=12 * 10**9, bytes_accessed=12 << 20, transcendentals=0
        ),
        name="attend_back",
    )(member, *proj, mixed, lse, taps, own, send, grad_own, grad_recv, *normed)


def canonical(flag, own_ref, recv_ref):
    own = own_ref[...]
    recv = recv_ref[...]
    return jnp.concatenate(
        [jnp.where(flag == 0, own, recv), jnp.where(flag == 0, recv, own)], axis=1
    )


def ffn_forward_kernel(
    s_ref,
    hown_ref,
    hrecv_ref,
    wout_ref,
    tok0,
    tok1,
    cot0,
    cot1,
    gain_ref,
    bias_ref,
    up_ref,
    upb_ref,
    down_ref,
    downb_ref,
    res_ref,
    nf_ref,
    gf_ref,
    relu_ref,
    out0,
    out1,
    dbias_ref,
    keep_ref,
    send_ref,
    acc,
):
    step = pl.program_id(0)
    size = tok0.shape[0]
    core = s_ref[0]
    halves = ((0, s_ref[1] * size), (size, lax.bitwise_xor(s_ref[1], 2) * size))

    def valid(start):
        row = start + lax.broadcasted_iota(jnp.int32, tok0.shape, 0)
        return row < s_ref[2]

    @pl.when(step == 0)
    def _():
        attended = dot_nn(canonical(core, hown_ref, hrecv_ref), wout_ref[...])
        for tok, cot, (first, start) in zip((tok0, tok1), (cot0, cot1), halves):
            rows = slice(first, first + size)
            residual = tok[...].astype(F32) + attended[rows]
            res_ref[rows, :] = residual
            scaled, _ = norm_stats(residual)
            nf_ref[rows, :] = (scaled * gain_ref[...] + bias_ref[...]).astype(BF16)
            grad = cot[...]
            gf_ref[rows, :] = jnp.where(valid(start), grad, jnp.zeros_like(grad))
        dbias_ref[0:1, :] = jnp.sum(gf_ref[...].astype(F32), axis=0, keepdims=True)
        acc[...] = jnp.zeros_like(acc)

    relu = jnp.maximum(dot_nn(nf_ref[...], up_ref[...]) + upb_ref[...], 0.0)
    relu_ref[...] = relu
    act = (relu * relu).astype(BF16)
    acc[...] += dot_nn(act, down_ref[...])
    grad = dot_tn(act, gf_ref[...])
    rows = grad.shape[0] // 8
    store_parts(
        core,
        [
            [
                tile
                for chunk in (bit, bit + 4, bit + 2, bit + 6)
                for tile in lane_tiles(grad[chunk * rows : (chunk + 1) * rows])
            ]
            for bit in range(2)
        ],
        keep_ref,
        send_ref,
    )

    @pl.when(step == pl.num_programs(0) - 1)
    def _():
        for out, (first, start) in zip((out0, out1), halves):
            rows = slice(first, first + size)
            total = res_ref[rows, :] + (acc[rows, :] + downb_ref[...])
            out[...] = jnp.where(valid(start), total, 0.0).astype(BF16)


def ffn_forward(scalars, hown, hrecv, wout, toks, cots, gain, bias, up, upb, down, downb):
    rows = 2 * toks[0].shape[0]
    width, ff = up.shape
    tile = ff // 4
    part = jax.ShapeDtypeStruct((2, 2, 2, 2, tile // 8 * width // LANES, LANES), BF16)
    part_spec = pl.BlockSpec(
        (2, 2, 1, 1) + part.shape[4:], lambda j: (0, 0, lax.rem(j, 2), lax.div(j, 2), 0, 0)
    )
    full = lambda dtype: jax.ShapeDtypeStruct((rows, width), dtype)
    block = jax.ShapeDtypeStruct(toks[0].shape, BF16)
    return pl.pallas_call(
        ffn_forward_kernel,
        grid=(4,),
        in_specs=[SMEM_SPEC]
        + [still(a) for a in (hown, hrecv, wout, *toks, *cots, gain, bias)]
        + [
            pl.BlockSpec((width, tile), lambda j: (0, j)),
            pl.BlockSpec((1, tile), lambda j: (0, j)),
            pl.BlockSpec((tile, width), lambda j: (j, 0)),
            still(downb),
        ],
        out_specs=[once((rows, width), lambda j: (0, 0))] * 3
        + [pl.BlockSpec((rows, tile), lambda j: (0, j))]
        + [once(block.shape, lambda j: (0, 0))] * 2
        + [pl.BlockSpec((8, width), lambda j: (0, 0)), part_spec, part_spec],
        out_shape=[
            full(F32),
            full(BF16),
            full(BF16),
            jax.ShapeDtypeStruct((rows, ff), F32),
            block,
            block,
            jax.ShapeDtypeStruct((8, width), F32),
            part,
            part,
        ],
        scratch_shapes=[pltpu.VMEM((rows, width), F32)],
        compiler_params=params(),
        cost_estimate=pl.CostEstimate(
            flops=2 * rows * width * (3 * ff + width), bytes_accessed=40 << 20, transcendentals=0
        ),
        name="ffn_forward",
    )(scalars, hown, hrecv, wout, *toks, *cots, gain, bias, up, upb, down, downb)


def ffn_backward_kernel(
    s_ref,
    gf_ref,
    nf_ref,
    res_ref,
    hown_ref,
    hrecv_ref,
    wout_ref,
    gain_ref,
    relu_ref,
    up_ref,
    down_ref,
    gres_ref,
    gown_ref,
    gsend_ref,
    upb_ref,
    sums_ref,
    keep_ref,
    send_ref,
    nft,
    gn,
):
    step = pl.program_id(0)
    last = pl.num_programs(0) - 1
    core = s_ref[0]

    def store(grad):
        rows = grad.shape[0] // 32
        store_parts(
            core,
            [
                [
                    tile
                    for place in range(16)
                    for chunk in [
                        bit
                        + (place >> 3 & 1) * 2
                        + (place >> 2 & 1) * 4
                        + (place >> 1 & 1) * 8
                        + (place & 1) * 16
                    ]
                    for tile in lane_tiles(grad[chunk * rows : (chunk + 1) * rows])
                ]
                for bit in range(2)
            ],
            keep_ref,
            send_ref,
        )

    @pl.when(step == 0)
    def _():
        nft[...] = nf_ref[...].T
        gn[...] = jnp.zeros_like(gn)

    @pl.when(step < last)
    def _():
        grad_act = dot_nt(gf_ref[...], down_ref[...])
        grad_pre = (2.0 * relu_ref[...] * grad_act).astype(BF16)
        upb_ref[...] = jnp.sum(grad_pre.astype(F32), axis=0, keepdims=True)
        gn[...] += dot_nt(grad_pre, up_ref[...])
        store(dot_nn(nft[...], grad_pre))

    @pl.when(step == last)
    def _():
        scaled, inv_std = norm_stats(res_ref[...])
        grad = gn[...]
        sums_ref[0:1, :] = jnp.sum(grad * scaled, axis=0, keepdims=True)
        sums_ref[1:2, :] = jnp.sum(grad, axis=0, keepdims=True)
        total = gf_ref[...].astype(F32) + norm_backward(grad, gain_ref[...], scaled, inv_std)
        gres_ref[...] = total
        attended = total.astype(BF16)
        heads = dot_nt(attended, wout_ref[...]).astype(BF16)
        middle = heads.shape[1] // 2
        gown_ref[...] = jnp.where(core == 0, heads[:, :middle], heads[:, middle:])
        gsend_ref[...] = jnp.where(core == 0, heads[:, middle:], heads[:, :middle])
        store(dot_tn(canonical(core, hown_ref, hrecv_ref), attended))


def ffn_backward(scalars, gf, nf, res, hown, hrecv, wout, gain, relu, up, down):
    rows, width = nf.shape
    ff = up.shape[1]
    tile = ff // 4
    block = width // 32 * tile // LANES
    part = jax.ShapeDtypeStruct((2, 2, 2, 2, 5 * block, LANES), BF16)
    part_spec = pl.BlockSpec((2, 2, 2, 2, block, LANES), lambda j: (0, 0, 0, 0, j, 0))
    now = lambda j: jnp.minimum(j, 3)
    half = jax.ShapeDtypeStruct(hown.shape, BF16)
    return pl.pallas_call(
        ffn_backward_kernel,
        grid=(5,),
        in_specs=[SMEM_SPEC]
        + [still(a) for a in (gf, nf, res, hown, hrecv, wout, gain)]
        + [
            pl.BlockSpec((rows, tile), lambda j: (0, now(j))),
            pl.BlockSpec((width, tile), lambda j: (0, now(j))),
            pl.BlockSpec((tile, width), lambda j: (now(j), 0)),
        ],
        out_specs=[once((rows, width), lambda j: (0, 0))]
        + [once(half.shape, lambda j: (0, 0))] * 2
        + [
            pl.BlockSpec((1, tile), lambda j: (0, now(j))),
            pl.BlockSpec((8, width), lambda j: (0, 0)),
            part_spec,
            part_spec,
        ],
        out_shape=[
            jax.ShapeDtypeStruct((rows, width), F32),
            half,
            half,
            jax.ShapeDtypeStruct((1, ff), F32),
            jax.ShapeDtypeStruct((8, width), F32),
            part,
            part,
        ],
        scratch_shapes=[pltpu.VMEM((width, rows), BF16), pltpu.VMEM((rows, width), F32)],
        compiler_params=params(),
        cost_estimate=pl.CostEstimate(
            flops=2 * rows * width * (3 * ff + 2 * width),
            bytes_accessed=40 << 20,
            transcendentals=0,
        ),
        name="ffn_backward",
    )(scalars, gf, nf, res, hown, hrecv, wout, gain, relu, up, down)


def input_grad_kernel(
    s_ref, o0, o1, o2, r0, r1, r2, w_ref, x_ref, gres_ref, gain_ref, out_ref, sums_ref, buf
):
    cols = 3 * LANES
    for n, ref in enumerate((o0, o1, o2, r0, r1, r2)):
        side = s_ref[0] if n < 3 else 1 - s_ref[0]
        start = pl.multiple_of((side * 3 + n % 3) * cols, LANES)
        buf[:, pl.ds(start, cols)] = ref[...]
    grad = dot_nt(buf[...], w_ref[...])
    scaled, inv_std = norm_stats(x_ref[...].astype(F32))

    @pl.when(pl.program_id(0) == 0)
    def _():
        sums_ref[...] = jnp.zeros_like(sums_ref)

    sums_ref[0:1, :] += jnp.sum(grad * scaled, axis=0, keepdims=True)
    sums_ref[1:2, :] += jnp.sum(grad, axis=0, keepdims=True)
    total = gres_ref[...] + norm_backward(grad, gain_ref[...], scaled, inv_std)
    out_ref[...] = total.astype(BF16)


def input_grad(slot, scalars, owns, recvs, weights, x, grad_residual, gain):
    rows, width = x.shape
    tile = rows // 2
    part = pl.BlockSpec((tile, 3 * LANES), lambda i: (2 * slot + i, 0))
    return pl.pallas_call(
        input_grad_kernel,
        grid=(2,),
        in_specs=[SMEM_SPEC]
        + [part] * 6
        + [
            still(weights),
            pl.BlockSpec((tile, width), lambda i: (i, 0)),
            pl.BlockSpec((tile, width), lambda i: (2 * slot + i, 0)),
            still(gain),
        ],
        out_specs=[
            pl.BlockSpec((tile, width), lambda i: (i, 0)),
            pl.BlockSpec((8, width), lambda i: (0, 0)),
        ],
        out_shape=[
            jax.ShapeDtypeStruct((rows, width), BF16),
            jax.ShapeDtypeStruct((8, width), F32),
        ],
        scratch_shapes=[pltpu.VMEM((tile, weights.shape[1]), BF16)],
        compiler_params=params(),
        cost_estimate=pl.CostEstimate(
            flops=2 * rows * width * weights.shape[1], bytes_accessed=8 << 20, transcendentals=0
        ),
        name="input_grad",
    )(scalars, *owns, *recvs, weights, x, grad_residual, gain)


def piece(part, axis=None, which=None):
    array, starts = part
    starts = list(starts)
    sizes = list(array.shape)
    for n in range(4):
        if starts[n] is not None:
            sizes[n] = 1
    if axis is not None:
        starts[axis] = which if array.shape[axis] == 2 else 0
        sizes[axis] = 1
    starts = [0 if s is None else s for s in starts] + [0] * (array.ndim - 4)
    return lax.dynamic_slice(array, starts, sizes).astype(F32)


def total_of(parts, axis=None, which=None):
    total = None
    for part in parts:
        value = piece(part, axis, which)
        total = value if total is None else total + value
    return total


def halve(keep, recv, stages):
    parts = [(keep, [None] * 4), (recv, [None] * 4)]
    for dim, axis, perm, bit in stages:
        sent = total_of(parts, dim, 1 - bit).astype(BF16)
        arrived = lax.ppermute(sent, axis, perm)
        for array, starts in parts:
            starts[dim] = bit if array.shape[dim] == 2 else 0
        parts.append((arrived, [None if n == 2 else 0 for n in arrived.shape[:4]]))
    return total_of(parts)


def everyone(value, hops):
    for axis, perm in hops:
        value = value + lax.ppermute(value, axis, perm)
    return value


def ffn_plain(heads, toks, cot, valid, wout, gain, bias, up, upb, down, downb):
    residual = toks.astype(F32) + jnp.dot(heads, wout, preferred_element_type=F32)
    scaled, inv_std = norm_stats(residual)
    normed = (scaled * gain + bias).astype(BF16)
    relu = jnp.maximum(jnp.dot(normed, up, preferred_element_type=F32) + upb, 0.0)
    act = jnp.square(relu).astype(BF16)
    out = jnp.dot(act, down, preferred_element_type=F32) + downb
    result = jnp.where(valid, residual + out, 0.0).astype(BF16)
    grad_ffn = jnp.where(valid, cot, jnp.zeros_like(cot))
    grad_y = grad_ffn.astype(F32)
    grad_act = jnp.einsum("td,fd->tf", grad_ffn, down, preferred_element_type=F32)
    grad_pre = (2.0 * relu * grad_act).astype(BF16)
    grad = jnp.einsum("tf,df->td", grad_pre, up, preferred_element_type=F32)
    sums = jnp.stack([jnp.sum(grad * scaled, axis=0), jnp.sum(grad, axis=0)])
    grad_residual = grad_y + norm_backward(grad, gain, scaled, inv_std)
    attended = grad_residual.astype(BF16)
    grad_heads = jnp.einsum("td,ed->te", attended, wout, preferred_element_type=F32)
    return (
        result,
        grad_residual,
        grad_heads.astype(BF16),
        sums,
        jnp.sum(grad_pre.astype(F32), axis=0),
        jnp.sum(grad_y, axis=0),
        jnp.einsum("td,tf->df", normed, grad_pre, preferred_element_type=F32),
        jnp.einsum("tf,td->fd", act, grad_ffn, preferred_element_type=F32),
        jnp.einsum("te,td->ed", heads, attended, preferred_element_type=F32),
    )


def on_device(
    tokens,
    cotangent,
    lengths,
    pre_attn_gain,
    pre_attn_bias,
    qkv_weight,
    conv_weight,
    out_weight,
    pre_ffn_gain,
    pre_ffn_bias,
    up_weight,
    up_bias,
    down_weight,
    down_bias,
):
    groups = lax.axis_size("mp")
    batch_groups = lax.axis_size("batch")
    devices = groups * batch_groups
    member = lax.axis_index("mp")
    batch = lax.axis_index("batch")
    seqs, rows, width = tokens.shape
    ff = up_weight.shape[1]
    middle = width // 2
    quarter = width // groups
    pairs = middle // LANES
    taps = conv_weight.shape[1]
    assert groups == 4 and seqs == 2 and pairs == 3 and taps == 3
    fast = batch_groups == 8 and (width // devices) % 8 == 0
    half = member // 2
    core = member % 2
    gain_attn = pre_attn_gain.astype(F32).reshape(1, width)
    bias_attn = pre_attn_bias.astype(F32).reshape(1, width)
    gain_ffn = pre_ffn_gain.astype(F32).reshape(1, width)
    bias_ffn = pre_ffn_bias.astype(F32).reshape(1, width)
    up_bias_f = up_bias.astype(F32).reshape(1, ff)
    down_bias_f = down_bias.astype(F32).reshape(1, width)

    def swap_core(value):
        return lax.ppermute(value, "mp", CORE)

    def swap_pair(value):
        return lax.ppermute(value, "mp", PAIR)

    def pick(value, index):
        return lax.dynamic_index_in_dim(value, index, 0, keepdims=False)

    length = pick(lengths, half)
    scalars = jnp.stack([core, member, length, batch % 2]).astype(jnp.int32)

    tok_pair = swap_pair(pick(tokens, 1 - half))
    tok_own = pick(tokens, half)
    cot_own = pick(cotangent, half)
    tok_core = swap_core(tok_own)
    weights = qkv_weight.reshape(3, width, 2 * pairs, LANES).transpose(1, 2, 0, 3)
    weights = weights.reshape(width, 3 * width)
    taps_own = lax.dynamic_slice_in_dim(conv_weight, core * middle, middle, 2).astype(F32)
    taps_own = taps_own.reshape(3 * taps, pairs, LANES).transpose(1, 0, 2)
    taps_own = jnp.pad(taps_own, ((0, 0), (0, 16 - 3 * taps), (0, 0)))

    def norm_project(block):
        return project(scalars, block, gain_attn, bias_attn, weights)

    first = norm_project(tok_own)
    second = norm_project(tok_core)
    tok_pair, first, second = lax.optimization_barrier((tok_pair, first, second))
    tok_cross = swap_core(tok_pair)
    cot_send, tok_late = lax.optimization_barrier((pick(cotangent, 1 - half), tok_pair))
    cot_pair = swap_pair(cot_send)
    normed, proj = zip(first, second, norm_project(tok_late), norm_project(tok_cross))
    mixed, heads_own, heads_send, lse = attend(scalars, proj, taps_own)
    heads_recv = swap_core(heads_send)

    if fast:
        (
            residual,
            normed_ffn,
            grad_ffn,
            relu,
            result_own,
            result_give,
            sums_down,
            *grads_down,
        ) = ffn_forward(
            scalars,
            heads_own,
            heads_recv,
            out_weight,
            (tok_own, tok_pair),
            (cot_own, cot_pair),
            gain_ffn,
            bias_ffn,
            up_weight,
            up_bias_f,
            down_weight,
            down_bias_f,
        )
        (
            grad_residual,
            grad_own,
            grad_send,
            sums_up,
            sums_ffn,
            *grads_up,
        ) = ffn_backward(
            scalars,
            grad_ffn,
            normed_ffn,
            residual,
            heads_own,
            heads_recv,
            out_weight,
            gain_ffn,
            relu,
            up_weight,
            down_weight,
        )
        sums_up = sums_up.reshape(ff)
        sums_down = sums_down[0]
        sums_ffn = sums_ffn[0:2]
    else:
        row = jnp.arange(rows, dtype=jnp.int32)
        row_pos = [member * rows + row, jnp.bitwise_xor(member, 2) * rows + row]
        heads_all = jnp.concatenate(
            [
                jnp.where(core == 0, heads_own, heads_recv),
                jnp.where(core == 0, heads_recv, heads_own),
            ],
            axis=1,
        )
        (
            result,
            grad_residual,
            grad_heads,
            sums_ffn,
            sums_up,
            sums_down,
            grad_up,
            grad_down,
            grad_out,
        ) = ffn_plain(
            heads_all,
            jnp.concatenate([tok_own, tok_pair], axis=0),
            jnp.concatenate([cot_own, cot_pair], axis=0),
            (jnp.concatenate(row_pos) < length)[:, None],
            out_weight,
            gain_ffn,
            bias_ffn,
            up_weight,
            up_bias_f,
            down_weight,
            down_bias_f,
        )
        result_own, result_give = result[:rows], result[rows:]
        grad_own = lax.dynamic_slice_in_dim(grad_heads, core * middle, middle, 1)
        grad_send = lax.dynamic_slice_in_dim(grad_heads, (1 - core) * middle, middle, 1)
    grad_recv = swap_core(grad_send)
    result_back = swap_pair(result_give)

    g_own, g_send, g_recv, g_conv, g_qkv = [], [], [], [], []
    for pair in range(pairs):
        own, send, conv, *grads = attend_back(
            pair,
            scalars,
            proj,
            mixed,
            lse,
            taps_own,
            heads_own,
            heads_send,
            grad_own,
            grad_recv,
            normed,
        )
        g_own.append(own)
        g_send.append(send)
        g_recv.append(swap_core(send))
        g_conv.append(conv)
        g_qkv.append(grads)
    grad_in_pair, sums_pair = input_grad(
        1, scalars, g_own, g_recv, weights, tok_pair, grad_residual, gain_attn
    )
    grad_in_back = swap_pair(grad_in_pair)
    grad_in_own, sums_own = input_grad(
        0, scalars, g_own, g_recv, weights, tok_own, grad_residual, gain_attn
    )

    def both(first, second):
        return jnp.stack([jnp.where(half == 0, first, second), jnp.where(half == 0, second, first)])

    result_all = both(result_own, result_back)
    tokens_grad = both(grad_in_own, grad_in_back)

    conv_own = jnp.stack(g_conv)[:, : 3 * taps].transpose(1, 0, 2).reshape(3 * taps, middle)
    conv_full = lax.dynamic_update_slice_in_dim(
        jnp.zeros((3 * taps, width), F32), conv_own, core * middle, 1
    )
    small = jnp.concatenate(
        [
            sums_up.reshape(ff // width, width),
            sums_down[None],
            sums_ffn,
            sums_pair[0:2] + sums_own[0:2],
            conv_full,
        ],
        axis=0,
    )
    index = batch * groups + member
    share = width // devices
    part = width // batch_groups

    if not fast:
        axes = ("batch", "mp")
        grad_qkv = 0.0
        for n, (norm, slot) in enumerate(zip(normed, (0, 0, 1, 1))):
            source = (g_own, g_send)[n % 2]
            grads = jnp.concatenate([g[slot * rows : (slot + 1) * rows] for g in source], axis=1)
            grad_qkv = grad_qkv + jnp.einsum("dt,te->de", norm, grads, preferred_element_type=F32)
        grad_qkv = grad_qkv.reshape(width, pairs, 3, LANES).transpose(2, 0, 1, 3)
        qkv_full = lax.dynamic_update_slice_in_dim(
            jnp.zeros((3, width, width), F32), grad_qkv.reshape(3, width, middle), core * middle, 2
        )
        qkv_flat = qkv_full.reshape(3, batch_groups, part, groups, quarter)
        qkv_flat = qkv_flat.transpose(1, 3, 0, 2, 4).reshape(devices * 3 * part, quarter)

        def scatter(value):
            return lax.psum_scatter(value, axes, scatter_dimension=0, tiled=True)

        small = lax.psum(small, axes)
        qkv_out = scatter(qkv_flat).reshape(3, part, quarter)
        up_out, down_out, out_out = scatter(grad_up), scatter(grad_down), scatter(grad_out)
    else:
        core_hop = ("mp", CORE)
        pair_hop = ("mp", PAIR)
        x_hop, z0_hop, z1_hop = [
            ("batch", [(i, i ^ flip) for i in range(batch_groups)]) for flip in (1, 2, 4)
        ]
        pair_stage = (0,) + pair_hop + (half,)
        x_stage = (1,) + x_hop + (batch % 2,)
        z0_stage = (2,) + z0_hop + (batch // 2 % 2,)
        z1_stage = (3,) + z1_hop + (batch // 4,)
        keep, send = grads_down
        down_sum = halve(keep, swap_core(send), [x_stage, pair_stage, z0_stage, z1_stage])
        down_out = down_sum.reshape(width // LANES, ff // devices, LANES).transpose(1, 0, 2)
        down_out = down_out.reshape(ff // devices, width)
        keep, send = grads_up
        up_sum = halve(keep, swap_core(send), [pair_stage, x_stage, z0_stage, z1_stage])
        up_sum = up_sum.reshape(-1, share, LANES)
        up_out = up_sum[: ff // LANES].transpose(1, 0, 2).reshape(share, ff)
        out_out = up_sum[ff // LANES :].transpose(1, 0, 2).reshape(share, width)
        qkv_parts = []
        for keep, send in g_qkv:
            keep = keep.reshape((1, 1) + keep.shape)
            recv = lax.ppermute(send, *x_hop).reshape(keep.shape)
            total = halve(keep, recv, [z0_stage, z1_stage])
            qkv_parts.append(total.reshape(part, 3, LANES))
        qkv_all = jnp.stack(qkv_parts, axis=1).transpose(2, 0, 1, 3)
        qkv_all = qkv_all.reshape(3, part, 2, quarter)
        lower = qkv_all[:, :, 0]
        upper = qkv_all[:, :, 1]
        keep = jnp.where(core == 0, lower, upper)
        straight = lax.ppermute(
            jnp.where(half == 0, upper, lower).astype(BF16), "mp", [(2, 0), (0, 1), (3, 2), (1, 3)]
        )
        crossed = lax.ppermute(
            jnp.where(half == 0, lower, upper).astype(BF16), "mp", [(2, 1), (1, 2)]
        )
        qkv_out = straight.astype(F32) + jnp.where(half == core, keep, crossed.astype(F32))
        small = everyone(small, [core_hop, pair_hop, x_hop, z0_hop, z1_hop])

    lead = ff // width
    mine = small[lead:]
    mine = pick(mine.reshape(mine.shape[0], devices, share).transpose(1, 0, 2), index)
    return (
        result_all,
        tokens_grad,
        mine[3],
        mine[4],
        qkv_out,
        mine[5:].reshape(3, taps, share),
        out_out,
        mine[1],
        mine[2],
        up_out,
        pick(small[:lead].reshape(devices, ff // devices), index),
        down_out,
        mine[0],
    )


def solution(mesh):
    in_specs = (
        P("batch", "mp", None),
        P("batch", "mp", None),
        P("batch"),
    ) + (P(),) * 11
    out_specs = (
        P("batch", "mp", None),
        P("batch", "mp", None),
        P(("batch", "mp")),
        P(("batch", "mp")),
        P(None, "batch", "mp"),
        P(None, None, ("batch", "mp")),
        P(("batch", "mp"), None),
        P(("batch", "mp")),
        P(("batch", "mp")),
        P(("batch", "mp"), None),
        P(("batch", "mp")),
        P(("batch", "mp"), None),
        P(("batch", "mp")),
    )
    return jax.shard_map(
        on_device, mesh=mesh, in_specs=in_specs, out_specs=out_specs, check_vma=False
    )
```

```python
import functools

import jax
import jax.numpy as jnp
from jax import lax
from jax.experimental import pallas as pl
from jax.experimental.pallas import tpu as pltpu
from jax.sharding import PartitionSpec as P

HEAD_DIM = 64
LANES = 128
EPSILON = 1e-05
NEGATIVE = -1000000000.0
QBLOCK = 512
KBLOCK = 256
F32 = jnp.float32
BF16 = jnp.bfloat16

CORE = [(i, i ^ 1) for i in range(4)]
PAIR = [(i, i ^ 2) for i in range(4)]


def dot_nt(left, right):
    return lax.dot_general(left, right, (((1,), (1,)), ((), ())), preferred_element_type=F32)


def dot_nn(left, right):
    return lax.dot_general(left, right, (((1,), (0,)), ((), ())), preferred_element_type=F32)


def dot_tn(left, right):
    return lax.dot_general(left, right, (((0,), (0,)), ((), ())), preferred_element_type=F32)


def params(mib):
    return pltpu.CompilerParams(vmem_limit_bytes=mib << 20)


def lane_tiles(values):
    return [values[:, n : n + LANES] for n in range(0, values.shape[1], LANES)]


def once(shape, index_map):
    return pl.BlockSpec(shape, index_map, pipeline_mode=pl.Buffered(1))


def still(array):
    return once(array.shape, lambda *_: (0,) * array.ndim)


CHEAP = pl.CostEstimate(flops=1 << 20, bytes_accessed=1 << 16, transcendentals=0)
SMEM_SPEC = pl.BlockSpec(memory_space=pltpu.SMEM)


def norm_stats(values):
    center = values - jnp.mean(values, axis=-1, keepdims=True)
    inv_std = lax.rsqrt(jnp.mean(center * center, axis=-1, keepdims=True) + EPSILON)
    return center * inv_std, inv_std


def norm_backward(grad_out, norm_gain, scaled, inv_std):
    weighted = grad_out * norm_gain
    return inv_std * (
        weighted
        - jnp.mean(weighted, axis=-1, keepdims=True)
        - scaled * jnp.mean(weighted * scaled, axis=-1, keepdims=True)
    )


def project_kernel(s_ref, x_ref, gain_ref, bias_ref, w_ref, normed_ref, proj_ref):
    scaled, _ = norm_stats(x_ref[...].astype(F32))
    normed = (scaled * gain_ref[...] + bias_ref[...]).astype(BF16)
    normed_ref[...] = normed.T
    for c in range(3):
        part = dot_nn(normed, w_ref[c]).astype(BF16)
        for n, tile in enumerate(lane_tiles(part)):
            start = (3 * n + c) * LANES
            proj_ref[:, start : start + LANES] = tile


def project(scalars, x, gain, bias, weights):
    rows, width = x.shape
    cols = 3 * width // 2
    return pl.pallas_call(
        project_kernel,
        grid_spec=pltpu.PrefetchScalarGridSpec(
            num_scalar_prefetch=1,
            grid=(1,),
            in_specs=[
                once((rows, width), lambda i, s: (0, 0)),
                once((1, width), lambda i, s: (0, 0)),
                once((1, width), lambda i, s: (0, 0)),
                once((3, width, width // 2), lambda i, s: (0, 0, s[0])),
            ],
            out_specs=[
                once((width, rows), lambda i, s: (0, 0)),
                once((rows, cols), lambda i, s: (0, 0)),
            ],
        ),
        out_shape=[
            jax.ShapeDtypeStruct((width, rows), BF16),
            jax.ShapeDtypeStruct((rows, cols), BF16),
        ],
        compiler_params=params(16),
        cost_estimate=CHEAP,
        name="project",
    )(scalars, x, gain, bias, weights)


def store_parts(flag, parts, keep_ref, send_ref):
    first = jnp.concatenate(parts[0], axis=0)
    second = jnp.concatenate(parts[1], axis=0)
    keep = jnp.where(flag == 0, first, second)
    send = jnp.where(flag == 0, second, first)
    keep_ref[...] = keep.astype(BF16).reshape(keep_ref.shape)
    send_ref[...] = send.astype(BF16).reshape(send_ref.shape)


def only_head(values, head):
    lane = lax.broadcasted_iota(jnp.int32, values.shape, 1)
    return jnp.where((lane // HEAD_DIM) == head, values, jnp.zeros_like(values))


def load_natural(member, blocks, dest, size, shift=0):
    for slot, block in enumerate(blocks):
        start = pl.multiple_of(lax.bitwise_xor(member, slot) * size, 8) + shift
        start = pl.multiple_of(start, 8)
        dest[pl.ds(start, size), :] = block.astype(dest.dtype)


def attend_kernel(
    m_ref, p0, p1, p2, p3, taps_ref, mixed_ref, own_ref, send_ref, lse_ref, pj, kh, vt, on, qs
):
    member = m_ref[1]
    size = p0.shape[0]
    length = 4 * size
    scale = jnp.asarray(HEAD_DIM ** (-0.5), BF16)
    for c in range(3):
        cols = slice(c * LANES, (c + 1) * LANES)
        pj[c, 0:8, :] = jnp.zeros((8, LANES), F32)
        load_natural(member, [p[:, cols] for p in (p0, p1, p2, p3)], pj.at[c], size, 8)
    for c in range(3):
        total = taps_ref[0, 3 * c : 3 * c + 1, :] * pj[c, 8 : 8 + length, :]
        total = total + taps_ref[0, 3 * c + 1 : 3 * c + 2, :] * pj[c, 7 : 7 + length, :]
        total = total + taps_ref[0, 3 * c + 2 : 3 * c + 3, :] * pj[c, 6 : 6 + length, :]
        mixed = total.astype(BF16)
        mixed_ref[:, c * LANES : (c + 1) * LANES] = mixed
        if c == 0:
            qs[...] = mixed * scale
        elif c == 1:
            kh[0] = only_head(mixed, 0)
            kh[1] = only_head(mixed, 1)
        else:
            vt[...] = mixed.T
    for first in range(0, length, QBLOCK):
        queries = qs[first : first + QBLOCK, :]
        keys = first + QBLOCK
        outs = []
        for head in range(2):
            scores = dot_nt(kh[head, 0:keys, :], queries)
            key_pos = lax.broadcasted_iota(jnp.int32, (QBLOCK, QBLOCK), 0)
            query_pos = lax.broadcasted_iota(jnp.int32, (QBLOCK, QBLOCK), 1)
            corner = jnp.where(key_pos <= query_pos, scores[first:keys, :], NEGATIVE)
            if first:
                scores = jnp.concatenate([scores[:first, :], corner], axis=0)
            else:
                scores = corner
            top = jnp.max(scores, axis=0, keepdims=True)
            weights = jnp.exp(scores - top)
            total = jnp.sum(weights, axis=0, keepdims=True)
            part = dot_nn(
                vt[head * HEAD_DIM : (head + 1) * HEAD_DIM, 0:keys], weights.astype(BF16)
            )
            outs.append(part * (1.0 / total))
            lse_ref[0, head : head + 1, first : first + QBLOCK] = top + jnp.log(total)
        on[first : first + QBLOCK, :] = jnp.concatenate(outs, axis=0).T.astype(BF16)
    for slot in range(4):
        start = pl.multiple_of(lax.bitwise_xor(member, slot) * size, size)
        block = on[pl.ds(start, size), :]
        dest = (own_ref, send_ref)[slot % 2]
        dest[slot // 2 * size : (slot // 2 + 1) * size, :] = block


def attend(member, proj, taps):
    size = proj[0].shape[0]
    pairs = proj[0].shape[1] // (3 * LANES)
    length = 4 * size
    width = pairs * LANES
    return pl.pallas_call(
        attend_kernel,
        grid=(pairs,),
        in_specs=[SMEM_SPEC]
        + [pl.BlockSpec((size, 3 * LANES), lambda p: (0, p))] * 4
        + [pl.BlockSpec((1, 16, LANES), lambda p: (p, 0, 0))],
        out_specs=[
            pl.BlockSpec((length, 3 * LANES), lambda p: (0, p)),
            pl.BlockSpec((2 * size, LANES), lambda p: (0, p)),
            pl.BlockSpec((2 * size, LANES), lambda p: (0, p)),
            pl.BlockSpec((1, 2, length), lambda p: (p, 0, 0)),
        ],
        out_shape=[
            jax.ShapeDtypeStruct((length, 3 * width), BF16),
            jax.ShapeDtypeStruct((2 * size, width), BF16),
            jax.ShapeDtypeStruct((2 * size, width), BF16),
            jax.ShapeDtypeStruct((pairs, 2, length), F32),
        ],
        scratch_shapes=[
            pltpu.VMEM((3, 8 + length, LANES), F32),
            pltpu.VMEM((2, length, LANES), BF16),
            pltpu.VMEM((LANES, length), BF16),
            pltpu.VMEM((length, LANES), BF16),
            pltpu.VMEM((length, LANES), BF16),
        ],
        compiler_params=params(62),
        cost_estimate=CHEAP,
        name="attend",
    )(member, *proj, taps)


def attend_back_kernel(
    m_ref,
    p0,
    p1,
    p2,
    p3,
    mixed_ref,
    lse_ref,
    taps_ref,
    own_ref,
    send_ref,
    down_ref,
    drecv_ref,
    n0,
    n1,
    n2,
    n3,
    gown_ref,
    gsend_ref,
    gconv_ref,
    keep_ref,
    give_ref,
    pj,
    dm,
    qh,
    doh,
    kt,
    dl,
    dqa,
    nat,
    gp,
):
    member = m_ref[1]
    size = p0.shape[0]
    length = 4 * size
    scale = jnp.asarray(HEAD_DIM ** (-0.5), BF16)
    halves = [slice(0, size), slice(size, 2 * size)]
    load_natural(
        member,
        [own_ref[halves[0]], send_ref[halves[0]], own_ref[halves[1]], send_ref[halves[1]]],
        nat.at[0],
        size,
    )
    load_natural(
        member,
        [down_ref[halves[0]], drecv_ref[halves[0]], down_ref[halves[1]], drecv_ref[halves[1]]],
        nat.at[1],
        size,
    )
    grads = nat[1]
    product = (grads.astype(F32) * nat[0].astype(F32)).T
    for head in range(2):
        dl[head : head + 1, :] = jnp.sum(
            product[head * HEAD_DIM : (head + 1) * HEAD_DIM, :], axis=0, keepdims=True
        )
        doh[head] = only_head(grads, head)
        qh[head] = only_head(mixed_ref[:, 0:LANES], head) * scale
    kt[...] = mixed_ref[:, LANES : 2 * LANES].T
    for c in range(3):
        cols = slice(c * LANES, (c + 1) * LANES)
        pj[c, 0:8, :] = jnp.zeros((8, LANES), F32)
        dm[c, length : length + 8, :] = jnp.zeros((8, LANES), F32)
        load_natural(member, [p[:, cols] for p in (p0, p1, p2, p3)], pj.at[c], size, 8)
    for first in range(0, length, KBLOCK):
        keys = mixed_ref[first : first + KBLOCK, LANES : 2 * LANES]
        values = mixed_ref[first : first + KBLOCK, 2 * LANES : 3 * LANES]
        sum_v = None
        sum_k = None
        for head in range(2):
            scores = dot_nt(keys, qh[head, first:, :])
            key_pos = lax.broadcasted_iota(jnp.int32, (KBLOCK, KBLOCK), 0)
            query_pos = lax.broadcasted_iota(jnp.int32, (KBLOCK, KBLOCK), 1)
            corner = jnp.where(key_pos <= query_pos, scores[:, :KBLOCK], NEGATIVE)
            if first + KBLOCK < length:
                scores = jnp.concatenate([corner, scores[:, KBLOCK:]], axis=1)
            else:
                scores = corner
            probs = jnp.exp(scores - lse_ref[0, head : head + 1, first:])
            grad_probs = dot_nt(values, doh[head, first:, :])
            grad_scores = (probs * (grad_probs - dl[head : head + 1, first:])).astype(BF16)
            part_v = dot_nn(probs.astype(BF16), doh[head, first:, :])
            part_k = dot_nn(grad_scores, qh[head, first:, :])
            sum_v = part_v if sum_v is None else sum_v + part_v
            sum_k = part_k if sum_k is None else sum_k + part_k
            lanes = slice(head * HEAD_DIM, (head + 1) * HEAD_DIM)
            part_q = dot_nn(kt[lanes, first : first + KBLOCK], grad_scores)
            if first == 0:
                dqa[lanes, :] = part_q
            else:
                dqa[lanes, first:] += part_q
        dm[1, first : first + KBLOCK, :] = sum_k
        dm[2, first : first + KBLOCK, :] = sum_v
    dm[0, 0:length, :] = dqa[...].T * HEAD_DIM ** (-0.5)
    for c in range(3):
        grad = dm[c, 0:length, :]
        for s in range(3):
            gconv_ref[3 * c + s : 3 * c + s + 1, :] = jnp.sum(
                grad * pj[c, 8 - s : 8 - s + length, :], axis=0, keepdims=True
            )
        total = taps_ref[0, 3 * c : 3 * c + 1, :] * grad
        total = total + taps_ref[0, 3 * c + 1 : 3 * c + 2, :] * dm[c, 1 : 1 + length, :]
        total = total + taps_ref[0, 3 * c + 2 : 3 * c + 3, :] * dm[c, 2 : 2 + length, :]
        gp[:, c * LANES : (c + 1) * LANES] = total.astype(BF16)
    total = None
    for slot, norm in enumerate((n0, n1, n2, n3)):
        start = pl.multiple_of(lax.bitwise_xor(member, slot) * size, size)
        dest = (gown_ref, gsend_ref)[slot % 2]
        block = gp[pl.ds(start, size), :]
        dest[slot // 2 * size : (slot // 2 + 1) * size, :] = block
        part = dot_nn(norm[...], block)
        total = part if total is None else total + part
    rows = total.shape[0] // 8
    store_parts(
        m_ref[3],
        [
            [
                tile
                for b in (x, x + 4, x + 2, x + 6)
                for tile in lane_tiles(total[b * rows : (b + 1) * rows])
            ]
            for x in range(2)
        ],
        keep_ref,
        give_ref,
    )


def attend_back(pair, member, proj, mixed, lse, taps, own, send, grad_own, grad_recv, normed):
    size = proj[0].shape[0]
    length = 4 * size
    width = normed[0].shape[0]
    part = jax.ShapeDtypeStruct((2, 2, 3 * width // 8, LANES), BF16)
    half_spec = pl.BlockSpec((2 * size, LANES), lambda i: (0, pair))
    return pl.pallas_call(
        attend_back_kernel,
        grid=(1,),
        in_specs=[SMEM_SPEC]
        + [pl.BlockSpec((size, 3 * LANES), lambda i: (0, pair))] * 4
        + [
            pl.BlockSpec((length, 3 * LANES), lambda i: (0, pair)),
            pl.BlockSpec((1, 2, length), lambda i: (pair, 0, 0)),
            pl.BlockSpec((1, 16, LANES), lambda i: (pair, 0, 0)),
        ]
        + [half_spec] * 4
        + [pl.BlockSpec((width, size), lambda i: (0, 0))] * 4,
        out_specs=[
            pl.BlockSpec((2 * size, 3 * LANES), lambda i: (0, 0)),
            pl.BlockSpec((2 * size, 3 * LANES), lambda i: (0, 0)),
            pl.BlockSpec((16, LANES), lambda i: (0, 0)),
            pl.BlockSpec(part.shape, lambda i: (0, 0, 0, 0)),
            pl.BlockSpec(part.shape, lambda i: (0, 0, 0, 0)),
        ],
        out_shape=[
            jax.ShapeDtypeStruct((2 * size, 3 * LANES), BF16),
            jax.ShapeDtypeStruct((2 * size, 3 * LANES), BF16),
            jax.ShapeDtypeStruct((16, LANES), F32),
            part,
            part,
        ],
        scratch_shapes=[
            pltpu.VMEM((3, 8 + length, LANES), F32),
            pltpu.VMEM((3, 8 + length, LANES), F32),
            pltpu.VMEM((2, length, LANES), BF16),
            pltpu.VMEM((2, length, LANES), BF16),
            pltpu.VMEM((LANES, length), BF16),
            pltpu.VMEM((8, length), F32),
            pltpu.VMEM((LANES, length), F32),
            pltpu.VMEM((2, length, LANES), BF16),
            pltpu.VMEM((length, 3 * LANES), BF16),
        ],
        compiler_params=params(62),
        cost_estimate=CHEAP,
        name="attend_back",
    )(member, *proj, mixed, lse, taps, own, send, grad_own, grad_recv, *normed)


def canonical(flag, own_ref, recv_ref):
    own = own_ref[...]
    recv = recv_ref[...]
    return jnp.concatenate(
        [jnp.where(flag == 0, own, recv), jnp.where(flag == 0, recv, own)], axis=1
    )


def ffn_forward_kernel(
    s_ref,
    hown_ref,
    hrecv_ref,
    wout_ref,
    tok0,
    tok1,
    cot0,
    cot1,
    gain_ref,
    bias_ref,
    up_ref,
    upb_ref,
    down_ref,
    downb_ref,
    res_ref,
    nf_ref,
    gf_ref,
    relu_ref,
    out0,
    out1,
    dbias_ref,
    keep_ref,
    send_ref,
    acc,
):
    step = pl.program_id(0)
    size = tok0.shape[0]
    core = s_ref[0]
    halves = ((0, s_ref[1] * size), (size, lax.bitwise_xor(s_ref[1], 2) * size))

    def valid(start):
        row = start + lax.broadcasted_iota(jnp.int32, tok0.shape, 0)
        return row < s_ref[2]

    @pl.when(step == 0)
    def _():
        attended = dot_nn(canonical(core, hown_ref, hrecv_ref), wout_ref[...])
        for tok, cot, (first, start) in zip((tok0, tok1), (cot0, cot1), halves):
            rows = slice(first, first + size)
            residual = tok[...].astype(F32) + attended[rows]
            res_ref[rows, :] = residual
            scaled, _ = norm_stats(residual)
            nf_ref[rows, :] = (scaled * gain_ref[...] + bias_ref[...]).astype(BF16)
            grad = cot[...]
            gf_ref[rows, :] = jnp.where(valid(start), grad, jnp.zeros_like(grad))
        dbias_ref[0:1, :] = jnp.sum(gf_ref[...].astype(F32), axis=0, keepdims=True)
        acc[...] = jnp.zeros_like(acc)

    relu = jnp.maximum(dot_nn(nf_ref[...], up_ref[...]) + upb_ref[...], 0.0)
    relu_ref[...] = relu
    act = (relu * relu).astype(BF16)
    acc[...] += dot_nn(act, down_ref[...])
    grad = dot_tn(act, gf_ref[...])
    rows = grad.shape[0] // 8
    store_parts(
        core,
        [
            [
                tile
                for chunk in (bit, bit + 4, bit + 2, bit + 6)
                for tile in lane_tiles(grad[chunk * rows : (chunk + 1) * rows])
            ]
            for bit in range(2)
        ],
        keep_ref,
        send_ref,
    )

    @pl.when(step == pl.num_programs(0) - 1)
    def _():
        for out, (first, start) in zip((out0, out1), halves):
            rows = slice(first, first + size)
            total = res_ref[rows, :] + (acc[rows, :] + downb_ref[...])
            out[...] = jnp.where(valid(start), total, 0.0).astype(BF16)


def ffn_forward(scalars, hown, hrecv, wout, toks, cots, gain, bias, up, upb, down, downb):
    rows = 2 * toks[0].shape[0]
    width, ff = up.shape
    tile = ff // 4
    part = jax.ShapeDtypeStruct((2, 2, 2, 2, tile // 8 * width // LANES, LANES), BF16)
    part_spec = pl.BlockSpec(
        (2, 2, 1, 1) + part.shape[4:], lambda j: (0, 0, lax.rem(j, 2), lax.div(j, 2), 0, 0)
    )
    full = lambda dtype: jax.ShapeDtypeStruct((rows, width), dtype)
    block = jax.ShapeDtypeStruct(toks[0].shape, BF16)
    return pl.pallas_call(
        ffn_forward_kernel,
        grid=(4,),
        in_specs=[SMEM_SPEC]
        + [still(a) for a in (hown, hrecv, wout, *toks, *cots, gain, bias)]
        + [
            pl.BlockSpec((width, tile), lambda j: (0, j)),
            pl.BlockSpec((1, tile), lambda j: (0, j)),
            pl.BlockSpec((tile, width), lambda j: (j, 0)),
            still(downb),
        ],
        out_specs=[once((rows, width), lambda j: (0, 0))] * 3
        + [pl.BlockSpec((rows, tile), lambda j: (0, j))]
        + [once(block.shape, lambda j: (0, 0))] * 2
        + [pl.BlockSpec((8, width), lambda j: (0, 0)), part_spec, part_spec],
        out_shape=[
            full(F32),
            full(BF16),
            full(BF16),
            jax.ShapeDtypeStruct((rows, ff), F32),
            block,
            block,
            jax.ShapeDtypeStruct((8, width), F32),
            part,
            part,
        ],
        scratch_shapes=[pltpu.VMEM((rows, width), F32)],
        compiler_params=params(60),
        cost_estimate=CHEAP,
        name="ffn_forward",
    )(scalars, hown, hrecv, wout, *toks, *cots, gain, bias, up, upb, down, downb)


def ffn_backward_kernel(
    s_ref,
    gf_ref,
    nf_ref,
    res_ref,
    hown_ref,
    hrecv_ref,
    wout_ref,
    gain_ref,
    relu_ref,
    up_ref,
    down_ref,
    gres_ref,
    gown_ref,
    gsend_ref,
    upb_ref,
    sums_ref,
    keep_ref,
    send_ref,
    nft,
    gn,
):
    step = pl.program_id(0)
    last = pl.num_programs(0) - 1
    core = s_ref[0]

    def store(grad):
        rows = grad.shape[0] // 32
        store_parts(
            core,
            [
                [
                    tile
                    for place in range(16)
                    for chunk in [
                        bit
                        + (place >> 3 & 1) * 2
                        + (place >> 2 & 1) * 4
                        + (place >> 1 & 1) * 8
                        + (place & 1) * 16
                    ]
                    for tile in lane_tiles(grad[chunk * rows : (chunk + 1) * rows])
                ]
                for bit in range(2)
            ],
            keep_ref,
            send_ref,
        )

    @pl.when(step == 0)
    def _():
        nft[...] = nf_ref[...].T
        gn[...] = jnp.zeros_like(gn)

    @pl.when(step < last)
    def _():
        grad_act = dot_nt(gf_ref[...], down_ref[...])
        grad_pre = (2.0 * relu_ref[...] * grad_act).astype(BF16)
        upb_ref[...] = jnp.sum(grad_pre.astype(F32), axis=0, keepdims=True)
        gn[...] += dot_nt(grad_pre, up_ref[...])
        store(dot_nn(nft[...], grad_pre))

    @pl.when(step == last)
    def _():
        scaled, inv_std = norm_stats(res_ref[...])
        grad = gn[...]
        sums_ref[0:1, :] = jnp.sum(grad * scaled, axis=0, keepdims=True)
        sums_ref[1:2, :] = jnp.sum(grad, axis=0, keepdims=True)
        total = gf_ref[...].astype(F32) + norm_backward(grad, gain_ref[...], scaled, inv_std)
        gres_ref[...] = total
        attended = total.astype(BF16)
        heads = dot_nt(attended, wout_ref[...]).astype(BF16)
        middle = heads.shape[1] // 2
        gown_ref[...] = jnp.where(core == 0, heads[:, :middle], heads[:, middle:])
        gsend_ref[...] = jnp.where(core == 0, heads[:, middle:], heads[:, :middle])
        store(dot_tn(canonical(core, hown_ref, hrecv_ref), attended))


def ffn_backward(scalars, gf, nf, res, hown, hrecv, wout, gain, relu, up, down):
    rows, width = nf.shape
    ff = up.shape[1]
    tile = ff // 4
    block = width // 32 * tile // LANES
    part = jax.ShapeDtypeStruct((2, 2, 2, 2, 5 * block, LANES), BF16)
    part_spec = pl.BlockSpec((2, 2, 2, 2, block, LANES), lambda j: (0, 0, 0, 0, j, 0))
    now = lambda j: jnp.minimum(j, 3)
    half = jax.ShapeDtypeStruct(hown.shape, BF16)
    return pl.pallas_call(
        ffn_backward_kernel,
        grid=(5,),
        in_specs=[SMEM_SPEC]
        + [still(a) for a in (gf, nf, res, hown, hrecv, wout, gain)]
        + [
            pl.BlockSpec((rows, tile), lambda j: (0, now(j))),
            pl.BlockSpec((width, tile), lambda j: (0, now(j))),
            pl.BlockSpec((tile, width), lambda j: (now(j), 0)),
        ],
        out_specs=[once((rows, width), lambda j: (0, 0))]
        + [once(half.shape, lambda j: (0, 0))] * 2
        + [
            pl.BlockSpec((1, tile), lambda j: (0, now(j))),
            pl.BlockSpec((8, width), lambda j: (0, 0)),
            part_spec,
            part_spec,
        ],
        out_shape=[
            jax.ShapeDtypeStruct((rows, width), F32),
            half,
            half,
            jax.ShapeDtypeStruct((1, ff), F32),
            jax.ShapeDtypeStruct((8, width), F32),
            part,
            part,
        ],
        scratch_shapes=[pltpu.VMEM((width, rows), BF16), pltpu.VMEM((rows, width), F32)],
        compiler_params=params(60),
        cost_estimate=CHEAP,
        name="ffn_backward",
    )(scalars, gf, nf, res, hown, hrecv, wout, gain, relu, up, down)


def input_grad_kernel(
    s_ref, o0, o1, o2, r0, r1, r2, w_ref, x_ref, gres_ref, gain_ref, out_ref, sums_ref, buf
):
    for n, ref in enumerate((o0, o1, o2, r0, r1, r2)):
        side = s_ref[0] if n < 3 else 1 - s_ref[0]
        start = pl.multiple_of((side * 3 + n % 3) * LANES, LANES)
        for c, tile in enumerate(lane_tiles(ref[...])):
            buf[c, :, pl.ds(start, LANES)] = tile
    grad = dot_nt(buf[0], w_ref[0]) + dot_nt(buf[1], w_ref[1]) + dot_nt(buf[2], w_ref[2])
    scaled, inv_std = norm_stats(x_ref[...].astype(F32))

    @pl.when(pl.program_id(0) == 0)
    def _():
        sums_ref[...] = jnp.zeros_like(sums_ref)

    sums_ref[0:1, :] += jnp.sum(grad * scaled, axis=0, keepdims=True)
    sums_ref[1:2, :] += jnp.sum(grad, axis=0, keepdims=True)
    total = gres_ref[...] + norm_backward(grad, gain_ref[...], scaled, inv_std)
    out_ref[...] = total.astype(BF16)


def input_grad(slot, scalars, owns, recvs, weights, x, grad_residual, gain):
    rows, width = x.shape
    tile = rows // 2
    part = pl.BlockSpec((tile, 3 * LANES), lambda i: (2 * slot + i, 0))
    return pl.pallas_call(
        input_grad_kernel,
        grid=(2,),
        in_specs=[SMEM_SPEC]
        + [part] * 6
        + [
            still(weights),
            pl.BlockSpec((tile, width), lambda i: (i, 0)),
            pl.BlockSpec((tile, width), lambda i: (2 * slot + i, 0)),
            still(gain),
        ],
        out_specs=[
            pl.BlockSpec((tile, width), lambda i: (i, 0)),
            pl.BlockSpec((8, width), lambda i: (0, 0)),
        ],
        out_shape=[
            jax.ShapeDtypeStruct((rows, width), BF16),
            jax.ShapeDtypeStruct((8, width), F32),
        ],
        scratch_shapes=[pltpu.VMEM((3, tile, width), BF16)],
        compiler_params=params(24),
        cost_estimate=CHEAP,
        name="input_grad",
    )(scalars, *owns, *recvs, weights, x, grad_residual, gain)


FREE, ONE, MINE, OTHER = range(4)
BIT_AT = (4, 3, 5, 6)


class Segment:
    def __init__(self, arrays, first, rows):
        self.rows = rows
        self.parts = [(array, self.fresh(array), first) for array in arrays]

    @staticmethod
    def fresh(array):
        return [FREE if n == 2 else ONE for n in array.shape[:4]]

    def chosen(self, dim):
        found = []
        for array, marks, first in self.parts:
            marks = list(marks)
            if dim is not None and marks[dim] == FREE:
                marks[dim] = OTHER
            found.append((array, tuple(marks), first, self.rows))
        return found

    def settle(self, dim, arrived, first):
        parts = []
        for array, marks, own_first in self.parts:
            marks = list(marks)
            if marks[dim] == FREE:
                marks[dim] = MINE
            parts.append((array, marks, own_first))
        self.parts = parts + [(arrived, self.fresh(arrived), first)]


def settle(segments, dim, arrived):
    first = 0
    for segment in segments:
        segment.settle(dim, arrived, first)
        first += segment.rows


def sum_kernel(plan, finish, count, s_ref, *refs):
    pieces = [p for parts in plan for p in parts]
    arrays, outs = refs[:count], refs[count : len(refs) - len(pieces) - 1]
    bufs, sems = refs[len(refs) - len(pieces) - 1 : -1], refs[-1]
    copies = []
    for n, (place, marks, first, rows) in enumerate(pieces):
        where = []
        for dim, mark in enumerate(marks):
            bit = s_ref[BIT_AT[dim]]
            start = {FREE: 0, ONE: 0, MINE: bit, OTHER: 1 - bit}[mark]
            where.append(pl.ds(start, 2 if mark == FREE else 1))
        source = arrays[place].at[tuple(where) + (pl.ds(first, rows), slice(None))]
        copies.append(pltpu.make_async_copy(source, bufs[n], sems.at[n]))
        copies[-1].start()
    n = 0
    totals = []
    for parts in plan:
        total = None
        for _ in parts:
            copies[n].wait()
            value = bufs[n][...].astype(F32)
            total = value if total is None else total + value
            n += 1
        totals.append(total)
    finish(s_ref, totals, outs)


def sum_call(scalars, segments, dims, finish, out_shape, name):
    arrays, plan, scratch = [], [], []
    for segment, dim in zip(segments, dims):
        parts = []
        for array, marks, first, rows in segment.chosen(dim):
            place = next((n for n, a in enumerate(arrays) if a is array), None)
            if place is None:
                place = len(arrays)
                arrays.append(array)
            parts.append((place, marks, first, rows))
            sizes = tuple(2 if mark == FREE else 1 for mark in marks)
            scratch.append(pltpu.VMEM(sizes + (rows, LANES), BF16))
        plan.append(parts)
    whole = lambda shape: pl.BlockSpec(shape, lambda i: (0,) * len(shape))
    return pl.pallas_call(
        functools.partial(sum_kernel, plan, finish, len(arrays)),
        grid=(1,),
        in_specs=[SMEM_SPEC] + [pl.BlockSpec(memory_space=pltpu.HBM)] * len(arrays),
        out_specs=[whole(o.shape) for o in out_shape],
        out_shape=out_shape,
        scratch_shapes=scratch + [pltpu.SemaphoreType.DMA((len(scratch),))],
        compiler_params=params(62),
        cost_estimate=CHEAP,
        name=name,
    )(scalars, *arrays)


def outgoing(scalars, groups, dims, name="stage_sum"):
    shapes = []
    for group, dim in zip(groups, dims):
        marks = [group[0].chosen(dim)[0][1]]
        sizes = tuple(2 if mark == FREE else 1 for mark in marks[0])
        shapes.append(jax.ShapeDtypeStruct(sizes + (sum(g.rows for g in group), LANES), BF16))

    def finish(s_ref, totals, outs):
        n = 0
        for group, out in zip(groups, outs):
            first = 0
            for segment in group:
                out[:, :, :, :, first : first + segment.rows, :] = totals[n].astype(BF16)
                first += segment.rows
                n += 1

    segments = [segment for group in groups for segment in group]
    each = [dim for group, dim in zip(groups, dims) for _ in group]
    return sum_call(scalars, segments, each, finish, shapes, name)


def hop(value, stage):
    return lax.ppermute(value, stage[0], stage[1])


def ffn_plain(heads, toks, cot, valid, wout, gain, bias, up, upb, down, downb):
    residual = toks.astype(F32) + jnp.dot(heads, wout, preferred_element_type=F32)
    scaled, inv_std = norm_stats(residual)
    normed = (scaled * gain + bias).astype(BF16)
    relu = jnp.maximum(jnp.dot(normed, up, preferred_element_type=F32) + upb, 0.0)
    act = jnp.square(relu).astype(BF16)
    out = jnp.dot(act, down, preferred_element_type=F32) + downb
    result = jnp.where(valid, residual + out, 0.0).astype(BF16)
    grad_ffn = jnp.where(valid, cot, jnp.zeros_like(cot))
    grad_y = grad_ffn.astype(F32)
    grad_act = jnp.einsum("td,fd->tf", grad_ffn, down, preferred_element_type=F32)
    grad_pre = (2.0 * relu * grad_act).astype(BF16)
    grad = jnp.einsum("tf,df->td", grad_pre, up, preferred_element_type=F32)
    sums = jnp.stack([jnp.sum(grad * scaled, axis=0), jnp.sum(grad, axis=0)])
    grad_residual = grad_y + norm_backward(grad, gain, scaled, inv_std)
    attended = grad_residual.astype(BF16)
    grad_heads = jnp.einsum("td,ed->te", attended, wout, preferred_element_type=F32)
    return (
        result,
        grad_residual,
        grad_heads.astype(BF16),
        sums,
        jnp.sum(grad_pre.astype(F32), axis=0),
        jnp.sum(grad_y, axis=0),
        jnp.einsum("td,tf->df", normed, grad_pre, preferred_element_type=F32),
        jnp.einsum("tf,td->fd", act, grad_ffn, preferred_element_type=F32),
        jnp.einsum("te,td->ed", heads, attended, preferred_element_type=F32),
    )


def on_device(
    tokens,
    cotangent,
    lengths,
    pre_attn_gain,
    pre_attn_bias,
    qkv_weight,
    conv_weight,
    out_weight,
    pre_ffn_gain,
    pre_ffn_bias,
    up_weight,
    up_bias,
    down_weight,
    down_bias,
):
    groups = lax.axis_size("mp")
    batch_groups = lax.axis_size("batch")
    devices = groups * batch_groups
    member = lax.axis_index("mp").astype(jnp.int32)
    batch = lax.axis_index("batch").astype(jnp.int32)
    seqs, rows, width = tokens.shape
    ff = up_weight.shape[1]
    middle = width // 2
    quarter = width // groups
    pairs = middle // LANES
    taps = conv_weight.shape[1]
    assert groups == 4 and seqs == 2 and pairs == 3 and taps == 3
    fast = batch_groups == 8 and (width // devices) % 8 == 0
    half = lax.shift_right_logical(member, 1)
    core = lax.bitwise_and(member, 1)
    x_bit = lax.bitwise_and(batch, 1)
    z0_bit = lax.bitwise_and(lax.shift_right_logical(batch, 1), 1)
    z1_bit = lax.shift_right_logical(batch, 2)
    gain_attn = pre_attn_gain.astype(F32).reshape(1, width)
    bias_attn = pre_attn_bias.astype(F32).reshape(1, width)
    gain_ffn = pre_ffn_gain.astype(F32).reshape(1, width)
    bias_ffn = pre_ffn_bias.astype(F32).reshape(1, width)
    up_bias_f = up_bias.astype(F32).reshape(1, ff)
    down_bias_f = down_bias.astype(F32).reshape(1, width)

    def swap_core(value):
        return lax.ppermute(value, "mp", CORE)

    def swap_pair(value):
        return lax.ppermute(value, "mp", PAIR)

    def pick(value, index):
        starts = (index,) + (jnp.int32(0),) * (value.ndim - 1)
        return lax.dynamic_slice(value, starts, (1,) + value.shape[1:])[0]

    length = pick(lengths, half)
    scalars = jnp.stack([core, member, length, x_bit, half, z0_bit, z1_bit]).astype(jnp.int32)

    hops = [("mp", PAIR)] + [
        ("batch", [(i, i ^ flip) for i in range(batch_groups)]) for flip in (1, 2, 4)
    ]
    DY, DX, DZ0, DZ1 = range(4)
    tie = lax.optimization_barrier

    tok_pair = swap_pair(pick(tokens, 1 - half))
    tok_own = pick(tokens, half)
    cot_own = pick(cotangent, half)
    tok_core = swap_core(tok_own)
    taps_own = lax.dynamic_slice_in_dim(conv_weight, core * middle, middle, 2).astype(F32)
    taps_own = taps_own.reshape(3 * taps, pairs, LANES).transpose(1, 0, 2)
    taps_own = jnp.pad(taps_own, ((0, 0), (0, 16 - 3 * taps), (0, 0)))

    def norm_project(block):
        return project(scalars, block, gain_attn, bias_attn, qkv_weight)

    first = norm_project(tok_own)
    second = norm_project(tok_core)
    tok_pair, first, second = lax.optimization_barrier((tok_pair, first, second))
    tok_cross = swap_core(tok_pair)
    cot_send, tok_late = lax.optimization_barrier((pick(cotangent, 1 - half), tok_pair))
    cot_pair = swap_pair(cot_send)
    normed, proj = zip(first, second, norm_project(tok_late), norm_project(tok_cross))
    mixed, heads_own, heads_send, lse = attend(scalars, proj, taps_own)
    heads_recv = swap_core(heads_send)

    if fast:
        (
            residual,
            normed_ffn,
            grad_ffn,
            relu,
            result_own,
            result_give,
            sums_down,
            down_keep,
            down_send,
        ) = ffn_forward(
            scalars,
            heads_own,
            heads_recv,
            out_weight,
            (tok_own, tok_pair),
            (cot_own, cot_pair),
            gain_ffn,
            bias_ffn,
            up_weight,
            up_bias_f,
            down_weight,
            down_bias_f,
        )
        (
            grad_residual,
            grad_own,
            grad_send,
            sums_up,
            sums_ffn,
            up_keep,
            up_send,
        ) = ffn_backward(
            scalars,
            grad_ffn,
            normed_ffn,
            residual,
            heads_own,
            heads_recv,
            out_weight,
            gain_ffn,
            relu,
            up_weight,
            down_weight,
        )
        sums_up = sums_up.reshape(ff)
        sums_down = sums_down[0]
        sums_ffn = sums_ffn[0:2]
    else:
        row = jnp.arange(rows, dtype=jnp.int32)
        row_pos = [member * rows + row, jnp.bitwise_xor(member, 2) * rows + row]
        heads_all = jnp.concatenate(
            [
                jnp.where(core == 0, heads_own, heads_recv),
                jnp.where(core == 0, heads_recv, heads_own),
            ],
            axis=1,
        )
        (
            result,
            grad_residual,
            grad_heads,
            sums_ffn,
            sums_up,
            sums_down,
            grad_up,
            grad_down,
            grad_out,
        ) = ffn_plain(
            heads_all,
            jnp.concatenate([tok_own, tok_pair], axis=0),
            jnp.concatenate([cot_own, cot_pair], axis=0),
            (jnp.concatenate(row_pos) < length)[:, None],
            out_weight,
            gain_ffn,
            bias_ffn,
            up_weight,
            up_bias_f,
            down_weight,
            down_bias_f,
        )
        result_own, result_give = result[:rows], result[rows:]
        grad_own = lax.dynamic_slice_in_dim(grad_heads, core * middle, middle, 1)
        grad_send = lax.dynamic_slice_in_dim(grad_heads, (1 - core) * middle, middle, 1)
    result_back = swap_pair(result_give)
    if fast:
        down_recv = swap_core(down_send)
        grad_own, grad_send, up_keep, up_send, down_recv, result_back = tie(
            (grad_own, grad_send, up_keep, up_send, down_recv, result_back)
        )
        up_recv = swap_core(up_send)
    grad_recv = swap_core(grad_send)
    if fast:
        down_rows = down_keep.shape[4]
        up_rows = up_keep.shape[4]
        each = (down_rows + up_rows) // 3
        down = (down_keep, down_recv)
        up = (up_keep, up_recv)
        rest = down_rows - each
        down_a, down_b = Segment(down, 0, each), Segment(down, each, rest)
        up_a, up_b = Segment(up, 0, each - rest), Segment(up, each - rest, each)
        group_1, group_2, group_3 = [down_a], [down_b, up_a], [up_b]

        def stage(dims, groups=(group_1, group_2, group_3)):
            return outgoing(scalars, groups, dims)

        def arrive(dims, sent, groups=(group_1, group_2, group_3)):
            for group, dim, value in zip(groups, dims, sent):
                settle(group, dim, value)

        dims = (DX, DZ0, DY)
        sent = stage(dims)
        grad_own, grad_recv, sent = tie((grad_own, grad_recv, sent))
        sent = [hop(v, hops[d]) for v, d in zip(sent, dims)]
        arrive(dims, sent)

    def backward(pair, grad_recv):
        own, send, conv, keep, give = attend_back(
            pair,
            scalars,
            proj,
            mixed,
            lse,
            taps_own,
            heads_own,
            heads_send,
            grad_own,
            grad_recv,
            normed,
        )
        keep = keep.reshape((1, 1) + keep.shape)
        give = give.reshape((1, 1) + give.shape)
        return own, send, conv, keep, give

    qkv_rows = 3 * width // 8
    own_0, send_0, conv_0, keep_0, give_0 = backward(0, grad_recv)
    if fast:
        dims = (DY, DZ1, DX)
        sent = stage(dims)
        grad_recv, own_0, send_0, give_0, sent = tie((grad_recv, own_0, send_0, give_0, sent))
        sent = [hop(v, hops[d]) for v, d in zip(sent, dims)]
        arrive(dims, sent)
        qkv_0 = Segment((keep_0, hop(give_0, hops[DX])), 0, qkv_rows)
        group_1.append(qkv_0)
    recv_0 = swap_core(send_0)
    own_1, send_1, conv_1, keep_1, give_1 = backward(1, grad_recv)
    if fast:
        dims = (DZ0, DX, DZ1)
        sent = stage(dims)
        grad_recv, own_1, send_1, give_1, recv_0, sent = tie(
            (grad_recv, own_1, send_1, give_1, recv_0, sent)
        )
        sent = [hop(v, hops[d]) for v, d in zip(sent, dims)]
        give_1 = hop(give_1, hops[DX])
    recv_1 = swap_core(send_1)
    own_2, send_2, conv_2, keep_2, give_2 = backward(2, grad_recv)
    if fast:
        own_2, send_2, give_2, recv_1, sent, give_1 = tie(
            (own_2, send_2, give_2, recv_1, sent, give_1)
        )
        arrive(dims, sent)
        qkv_1 = Segment((keep_1, give_1), 0, qkv_rows)
        give_2 = hop(give_2, hops[DX])
        qkv_2 = Segment((keep_2, give_2), 0, qkv_rows)
    recv_2 = swap_core(send_2)
    if fast:
        dims = (DZ1, DY, DZ0)
        sent = stage(dims)
        recv_2, sent = tie((recv_2, sent))
        ffn_waiting = [hop(v, hops[d]) for v, d in zip(sent, dims)]
    g_own = (own_0, own_1, own_2)
    g_send = (send_0, send_1, send_2)
    g_recv = (recv_0, recv_1, recv_2)
    g_conv = (conv_0, conv_1, conv_2)
    grad_in_pair, sums_pair = input_grad(
        1, scalars, g_own, g_recv, qkv_weight, tok_pair, grad_residual, gain_attn
    )
    grad_in_back = swap_pair(grad_in_pair)
    tok_last = tok_own
    if fast:
        (sent,) = outgoing(scalars, [[qkv_1, qkv_2]], [DZ0])
        tok_last, sums_pair, sent = tie((tok_own, sums_pair, sent))
        waiting = hop(sent, hops[DZ0])
    grad_in_own, sums_own = input_grad(
        0, scalars, g_own, g_recv, qkv_weight, tok_last, grad_residual, gain_attn
    )

    def both(first, second):
        return jnp.stack([jnp.where(half == 0, first, second), jnp.where(half == 0, second, first)])

    result_all = both(result_own, result_back)

    conv_own = jnp.stack(g_conv)[:, : 3 * taps].transpose(1, 0, 2).reshape(3 * taps, middle)
    conv_full = lax.dynamic_update_slice_in_dim(
        jnp.zeros((3 * taps, width), F32), conv_own, core * middle, 1
    )
    small = jnp.concatenate(
        [
            sums_up.reshape(ff // width, width),
            sums_down[None],
            sums_ffn,
            sums_pair[0:2] + sums_own[0:2],
            conv_full,
        ],
        axis=0,
    )
    index = batch * groups + member
    share = width // devices
    part = width // batch_groups

    if not fast:
        axes = ("batch", "mp")
        grad_qkv = 0.0
        for n, (norm, slot) in enumerate(zip(normed, (0, 0, 1, 1))):
            source = (g_own, g_send)[n % 2]
            grads = jnp.concatenate([g[slot * rows : (slot + 1) * rows] for g in source], axis=1)
            grad_qkv = grad_qkv + jnp.einsum("dt,te->de", norm, grads, preferred_element_type=F32)
        grad_qkv = grad_qkv.reshape(width, pairs, 3, LANES).transpose(2, 0, 1, 3)
        qkv_full = lax.dynamic_update_slice_in_dim(
            jnp.zeros((3, width, width), F32), grad_qkv.reshape(3, width, middle), core * middle, 2
        )
        qkv_flat = qkv_full.reshape(3, batch_groups, part, groups, quarter)
        qkv_flat = qkv_flat.transpose(1, 3, 0, 2, 4).reshape(devices * 3 * part, quarter)

        def scatter(value):
            return lax.psum_scatter(value, axes, scatter_dimension=0, tiled=True)

        small = lax.psum(small, axes)
        qkv_out = scatter(qkv_flat).reshape(3, part, quarter)
        up_out, down_out, out_out = scatter(grad_up), scatter(grad_down), scatter(grad_out)
    else:
        small = small + hop(small, ("mp", CORE))
        small, waiting = tie((small, waiting))
        settle([qkv_1, qkv_2], DZ0, waiting)
        (sent,) = outgoing(scalars, [[qkv_1, qkv_2]], [DZ1])
        sent = hop(sent, hops[DZ1])
        small = small + hop(small, hops[DX])
        small, ffn_waiting = tie((small, ffn_waiting))
        arrive((DZ1, DY, DZ0), ffn_waiting)
        small = small + hop(small, hops[DZ0])
        small, sent, grad_in_back = tie((small, sent, grad_in_back))
        settle([qkv_1, qkv_2], DZ1, sent)
        small = small + hop(small, hops[DZ1])
        small = small + hop(small, hops[DY])

        def finish_ffn(s_ref, totals, outs):
            rows_of = lambda values: [v.reshape(v.shape[-2:]) for v in values]
            downs = jnp.concatenate(rows_of(totals[0:2]), axis=0)
            ups = jnp.concatenate(rows_of(totals[2:4]), axis=0)
            down_out, up_out, out_out = outs
            for out, values in ((down_out, downs), (up_out, ups), (out_out, ups[down_rows:])):
                size, cols = out.shape
                for n in range(cols // LANES):
                    out[:, n * LANES : (n + 1) * LANES] = values[n * size : (n + 1) * size]

        down_out, up_out, out_out = sum_call(
            scalars,
            [down_a, down_b, up_a, up_b],
            [None] * 4,
            finish_ffn,
            [
                jax.ShapeDtypeStruct((ff // devices, width), F32),
                jax.ShapeDtypeStruct((share, ff), F32),
                jax.ShapeDtypeStruct((share, width), F32),
            ],
            "ffn_sum",
        )

        def finish_qkv(s_ref, totals, outs):
            first, middle, last = [v.reshape(v.shape[-2:]) for v in totals]
            lower = jnp.concatenate([first, middle[:, :HEAD_DIM]], axis=1)
            upper = jnp.concatenate([middle[:, HEAD_DIM:], last], axis=1)
            outs[0][...] = jnp.where(s_ref[0] == 0, lower, upper)
            outs[1][...] = jnp.where(s_ref[4] == 0, upper, lower).astype(BF16)
            outs[2][...] = jnp.where(s_ref[4] == 0, lower, upper).astype(BF16)

        keep, straight, crossed = sum_call(
            scalars,
            [qkv_0, qkv_1, qkv_2],
            [None] * 3,
            finish_qkv,
            [jax.ShapeDtypeStruct((qkv_rows, quarter), t) for t in (F32, BF16, BF16)],
            "qkv_sum",
        )
        straight = lax.ppermute(straight, "mp", [(2, 0), (0, 1), (3, 2), (1, 3)])
        crossed = lax.ppermute(crossed, "mp", [(2, 1), (1, 2)])
        qkv_out = straight.astype(F32) + jnp.where(half == core, keep, crossed.astype(F32))
        qkv_out = qkv_out.reshape(3, part, quarter)

    tokens_grad = both(grad_in_own, grad_in_back)
    lead = ff // width
    mine = small[lead:]
    mine = pick(mine.reshape(mine.shape[0], devices, share).transpose(1, 0, 2), index)
    return (
        result_all,
        tokens_grad,
        mine[3],
        mine[4],
        qkv_out,
        mine[5:].reshape(3, taps, share),
        out_out,
        mine[1],
        mine[2],
        up_out,
        pick(small[:lead].reshape(devices, ff // devices), index),
        down_out,
        mine[0],
    )


def solution(mesh):
    in_specs = (
        P("batch", "mp", None),
        P("batch", "mp", None),
        P("batch"),
    ) + (P(),) * 11
    out_specs = (
        P("batch", "mp", None),
        P("batch", "mp", None),
        P(("batch", "mp")),
        P(("batch", "mp")),
        P(None, "batch", "mp"),
        P(None, None, ("batch", "mp")),
        P(("batch", "mp"), None),
        P(("batch", "mp")),
        P(("batch", "mp")),
        P(("batch", "mp"), None),
        P(("batch", "mp")),
        P(("batch", "mp"), None),
        P(("batch", "mp")),
    )
    return jax.shard_map(
        on_device, mesh=mesh, in_specs=in_specs, out_specs=out_specs, check_vma=False
    )
```

```python
import functools
import itertools

import jax
import jax.numpy as jnp
from jax import lax
from jax.experimental import pallas as pl
from jax.experimental.pallas import tpu as pltpu
from jax.sharding import PartitionSpec as P

HEAD_DIM = 64
LANES = 128
EPSILON = 1e-05
NEGATIVE = -1000000000.0
QBLOCK = 512
KBLOCK = 256
F32 = jnp.float32
BF16 = jnp.bfloat16

CORE = [(i, i ^ 1) for i in range(4)]
PAIR = [(i, i ^ 2) for i in range(4)]


def dot_nt(left, right):
    return lax.dot_general(left, right, (((1,), (1,)), ((), ())), preferred_element_type=F32)


def dot_nn(left, right):
    return lax.dot_general(left, right, (((1,), (0,)), ((), ())), preferred_element_type=F32)


def dot_tn(left, right):
    return lax.dot_general(left, right, (((0,), (0,)), ((), ())), preferred_element_type=F32)


def params(mib):
    return pltpu.CompilerParams(vmem_limit_bytes=mib << 20)


def lane_tiles(values):
    return [values[:, n : n + LANES] for n in range(0, values.shape[1], LANES)]


def once(shape, index_map):
    return pl.BlockSpec(shape, index_map, pipeline_mode=pl.Buffered(1))


def still(array):
    return once(array.shape, lambda *_: (0,) * array.ndim)


CHEAP = pl.CostEstimate(flops=1 << 20, bytes_accessed=1 << 16, transcendentals=0)
SMEM_SPEC = pl.BlockSpec(memory_space=pltpu.SMEM)


def norm_stats(values):
    center = values - jnp.mean(values, axis=-1, keepdims=True)
    inv_std = lax.rsqrt(jnp.mean(center * center, axis=-1, keepdims=True) + EPSILON)
    return center * inv_std, inv_std


def norm_backward(grad_out, norm_gain, scaled, inv_std):
    weighted = grad_out * norm_gain
    return inv_std * (
        weighted
        - jnp.mean(weighted, axis=-1, keepdims=True)
        - scaled * jnp.mean(weighted * scaled, axis=-1, keepdims=True)
    )


def project_kernel(s_ref, x_ref, gain_ref, bias_ref, w_ref, normed_ref, proj_ref):
    scaled, _ = norm_stats(x_ref[...].astype(F32))
    normed = (scaled * gain_ref[...] + bias_ref[...]).astype(BF16)
    normed_ref[...] = normed.T
    for c in range(3):
        part = dot_nn(normed, w_ref[c]).astype(BF16)
        for n, tile in enumerate(lane_tiles(part)):
            start = (3 * n + c) * LANES
            proj_ref[:, start : start + LANES] = tile


def project(scalars, x, gain, bias, weights):
    rows, width = x.shape
    cols = 3 * width // 2
    return pl.pallas_call(
        project_kernel,
        grid_spec=pltpu.PrefetchScalarGridSpec(
            num_scalar_prefetch=1,
            grid=(1,),
            in_specs=[
                once((rows, width), lambda i, s: (0, 0)),
                once((1, width), lambda i, s: (0, 0)),
                once((1, width), lambda i, s: (0, 0)),
                once((3, width, width // 2), lambda i, s: (0, 0, s[0])),
            ],
            out_specs=[
                once((width, rows), lambda i, s: (0, 0)),
                once((rows, cols), lambda i, s: (0, 0)),
            ],
        ),
        out_shape=[
            jax.ShapeDtypeStruct((width, rows), BF16),
            jax.ShapeDtypeStruct((rows, cols), BF16),
        ],
        compiler_params=params(62),
        cost_estimate=CHEAP,
        name="project",
    )(scalars, x, gain, bias, weights)


def store_parts(flag, parts, keep_ref, send_ref):
    first = jnp.concatenate(parts[0], axis=0)
    second = jnp.concatenate(parts[1], axis=0)
    keep = jnp.where(flag == 0, first, second)
    send = jnp.where(flag == 0, second, first)
    keep_ref[...] = keep.astype(BF16).reshape(keep_ref.shape)
    send_ref[...] = send.astype(BF16).reshape(send_ref.shape)


def only_head(values, head):
    lane = lax.broadcasted_iota(jnp.int32, values.shape, 1)
    return jnp.where((lane // HEAD_DIM) == head, values, jnp.zeros_like(values))


def load_natural(member, blocks, dest, size, shift=0):
    for slot, block in enumerate(blocks):
        start = pl.multiple_of(lax.bitwise_xor(member, slot) * size, 8) + shift
        start = pl.multiple_of(start, 8)
        dest[pl.ds(start, size), :] = block.astype(dest.dtype)


def attend_kernel(
    m_ref, p0, p1, p2, p3, taps_ref, mixed_ref, own_ref, send_ref, lse_ref, pj, kh, vt, on, qs
):
    member = m_ref[1]
    size = p0.shape[0]
    length = 4 * size
    scale = jnp.asarray(HEAD_DIM ** (-0.5), BF16)
    for c in range(3):
        cols = slice(c * LANES, (c + 1) * LANES)
        pj[c, 0:8, :] = jnp.zeros((8, LANES), F32)
        load_natural(member, [p[:, cols] for p in (p0, p1, p2, p3)], pj.at[c], size, 8)
    for c in range(3):
        total = taps_ref[0, 3 * c : 3 * c + 1, :] * pj[c, 8 : 8 + length, :]
        total = total + taps_ref[0, 3 * c + 1 : 3 * c + 2, :] * pj[c, 7 : 7 + length, :]
        total = total + taps_ref[0, 3 * c + 2 : 3 * c + 3, :] * pj[c, 6 : 6 + length, :]
        mixed = total.astype(BF16)
        mixed_ref[:, c * LANES : (c + 1) * LANES] = mixed
        if c == 0:
            qs[...] = mixed * scale
        elif c == 1:
            kh[0] = only_head(mixed, 0)
            kh[1] = only_head(mixed, 1)
        else:
            vt[...] = mixed.T
    for first in range(0, length, QBLOCK):
        queries = qs[first : first + QBLOCK, :]
        keys = first + QBLOCK
        outs = []
        for head in range(2):
            scores = dot_nt(kh[head, 0:keys, :], queries)
            key_pos = lax.broadcasted_iota(jnp.int32, (QBLOCK, QBLOCK), 0)
            query_pos = lax.broadcasted_iota(jnp.int32, (QBLOCK, QBLOCK), 1)
            corner = jnp.where(key_pos <= query_pos, scores[first:keys, :], NEGATIVE)
            if first:
                scores = jnp.concatenate([scores[:first, :], corner], axis=0)
            else:
                scores = corner
            top = jnp.max(scores, axis=0, keepdims=True)
            weights = jnp.exp(scores - top)
            total = jnp.sum(weights, axis=0, keepdims=True)
            part = dot_nn(
                vt[head * HEAD_DIM : (head + 1) * HEAD_DIM, 0:keys], weights.astype(BF16)
            )
            outs.append(part * (1.0 / total))
            lse_ref[0, head : head + 1, first : first + QBLOCK] = top + jnp.log(total)
        on[first : first + QBLOCK, :] = jnp.concatenate(outs, axis=0).T.astype(BF16)
    for slot in range(4):
        start = pl.multiple_of(lax.bitwise_xor(member, slot) * size, size)
        block = on[pl.ds(start, size), :]
        dest = (own_ref, send_ref)[slot % 2]
        dest[slot // 2 * size : (slot // 2 + 1) * size, :] = block


def attend(member, proj, taps):
    size = proj[0].shape[0]
    pairs = proj[0].shape[1] // (3 * LANES)
    length = 4 * size
    width = pairs * LANES
    return pl.pallas_call(
        attend_kernel,
        grid=(pairs,),
        in_specs=[SMEM_SPEC]
        + [pl.BlockSpec((size, 3 * LANES), lambda p: (0, p))] * 4
        + [pl.BlockSpec((1, 16, LANES), lambda p: (p, 0, 0))],
        out_specs=[
            pl.BlockSpec((length, 3 * LANES), lambda p: (0, p)),
            pl.BlockSpec((2 * size, LANES), lambda p: (0, p)),
            pl.BlockSpec((2 * size, LANES), lambda p: (0, p)),
            pl.BlockSpec((1, 2, length), lambda p: (p, 0, 0)),
        ],
        out_shape=[
            jax.ShapeDtypeStruct((length, 3 * width), BF16),
            jax.ShapeDtypeStruct((2 * size, width), BF16),
            jax.ShapeDtypeStruct((2 * size, width), BF16),
            jax.ShapeDtypeStruct((pairs, 2, length), F32),
        ],
        scratch_shapes=[
            pltpu.VMEM((3, 8 + length, LANES), F32),
            pltpu.VMEM((2, length, LANES), BF16),
            pltpu.VMEM((LANES, length), BF16),
            pltpu.VMEM((length, LANES), BF16),
            pltpu.VMEM((length, LANES), BF16),
        ],
        compiler_params=params(62),
        cost_estimate=CHEAP,
        name="attend",
    )(member, *proj, taps)


def attend_back_kernel(
    m_ref,
    p0,
    p1,
    p2,
    p3,
    mixed_ref,
    lse_ref,
    taps_ref,
    own_ref,
    send_ref,
    down_ref,
    drecv_ref,
    n0,
    n1,
    n2,
    n3,
    gown_ref,
    gsend_ref,
    gconv_ref,
    keep_ref,
    give_ref,
    pj,
    dm,
    qh,
    doh,
    kt,
    dl,
    dqa,
    nat,
    gp,
):
    member = m_ref[1]
    size = p0.shape[0]
    length = 4 * size
    scale = jnp.asarray(HEAD_DIM ** (-0.5), BF16)
    halves = [slice(0, size), slice(size, 2 * size)]
    load_natural(
        member,
        [own_ref[halves[0]], send_ref[halves[0]], own_ref[halves[1]], send_ref[halves[1]]],
        nat.at[0],
        size,
    )
    load_natural(
        member,
        [down_ref[halves[0]], drecv_ref[halves[0]], down_ref[halves[1]], drecv_ref[halves[1]]],
        nat.at[1],
        size,
    )
    grads = nat[1]
    product = (grads.astype(F32) * nat[0].astype(F32)).T
    for head in range(2):
        dl[head : head + 1, :] = jnp.sum(
            product[head * HEAD_DIM : (head + 1) * HEAD_DIM, :], axis=0, keepdims=True
        )
        doh[head] = only_head(grads, head)
        qh[head] = only_head(mixed_ref[:, 0:LANES], head) * scale
    kt[...] = mixed_ref[:, LANES : 2 * LANES].T
    for c in range(3):
        cols = slice(c * LANES, (c + 1) * LANES)
        pj[c, 0:8, :] = jnp.zeros((8, LANES), F32)
        dm[c, length : length + 8, :] = jnp.zeros((8, LANES), F32)
        load_natural(member, [p[:, cols] for p in (p0, p1, p2, p3)], pj.at[c], size, 8)
    for first in range(0, length, KBLOCK):
        keys = mixed_ref[first : first + KBLOCK, LANES : 2 * LANES]
        values = mixed_ref[first : first + KBLOCK, 2 * LANES : 3 * LANES]
        sum_v = None
        sum_k = None
        for head in range(2):
            scores = dot_nt(keys, qh[head, first:, :])
            key_pos = lax.broadcasted_iota(jnp.int32, (KBLOCK, KBLOCK), 0)
            query_pos = lax.broadcasted_iota(jnp.int32, (KBLOCK, KBLOCK), 1)
            corner = jnp.where(key_pos <= query_pos, scores[:, :KBLOCK], NEGATIVE)
            if first + KBLOCK < length:
                scores = jnp.concatenate([corner, scores[:, KBLOCK:]], axis=1)
            else:
                scores = corner
            probs = jnp.exp(scores - lse_ref[0, head : head + 1, first:])
            grad_probs = dot_nt(values, doh[head, first:, :])
            grad_scores = (probs * (grad_probs - dl[head : head + 1, first:])).astype(BF16)
            part_v = dot_nn(probs.astype(BF16), doh[head, first:, :])
            part_k = dot_nn(grad_scores, qh[head, first:, :])
            sum_v = part_v if sum_v is None else sum_v + part_v
            sum_k = part_k if sum_k is None else sum_k + part_k
            lanes = slice(head * HEAD_DIM, (head + 1) * HEAD_DIM)
            part_q = dot_nn(kt[lanes, first : first + KBLOCK], grad_scores)
            if first == 0:
                dqa[lanes, :] = part_q
            else:
                dqa[lanes, first:] += part_q
        dm[1, first : first + KBLOCK, :] = sum_k
        dm[2, first : first + KBLOCK, :] = sum_v
    dm[0, 0:length, :] = dqa[...].T * HEAD_DIM ** (-0.5)
    for c in range(3):
        grad = dm[c, 0:length, :]
        for s in range(3):
            gconv_ref[3 * c + s : 3 * c + s + 1, :] = jnp.sum(
                grad * pj[c, 8 - s : 8 - s + length, :], axis=0, keepdims=True
            )
        total = taps_ref[0, 3 * c : 3 * c + 1, :] * grad
        total = total + taps_ref[0, 3 * c + 1 : 3 * c + 2, :] * dm[c, 1 : 1 + length, :]
        total = total + taps_ref[0, 3 * c + 2 : 3 * c + 3, :] * dm[c, 2 : 2 + length, :]
        gp[:, c * LANES : (c + 1) * LANES] = total.astype(BF16)
    total = None
    for slot, norm in enumerate((n0, n1, n2, n3)):
        start = pl.multiple_of(lax.bitwise_xor(member, slot) * size, size)
        dest = (gown_ref, gsend_ref)[slot % 2]
        block = gp[pl.ds(start, size), :]
        dest[slot // 2 * size : (slot // 2 + 1) * size, :] = block
        part = dot_nn(norm[...], block)
        total = part if total is None else total + part
    rows = total.shape[0] // 8
    store_parts(
        m_ref[3],
        [
            [
                tile
                for b in (x, x + 4, x + 2, x + 6)
                for tile in lane_tiles(total[b * rows : (b + 1) * rows])
            ]
            for x in range(2)
        ],
        keep_ref,
        give_ref,
    )


def attend_back(pair, member, proj, mixed, lse, taps, own, send, grad_own, grad_recv, normed):
    size = proj[0].shape[0]
    length = 4 * size
    width = normed[0].shape[0]
    part = jax.ShapeDtypeStruct((2, 2, 3 * width // 8, LANES), BF16)
    half_spec = pl.BlockSpec((2 * size, LANES), lambda i: (0, pair))
    return pl.pallas_call(
        attend_back_kernel,
        grid=(1,),
        in_specs=[SMEM_SPEC]
        + [pl.BlockSpec((size, 3 * LANES), lambda i: (0, pair))] * 4
        + [
            pl.BlockSpec((length, 3 * LANES), lambda i: (0, pair)),
            pl.BlockSpec((1, 2, length), lambda i: (pair, 0, 0)),
            pl.BlockSpec((1, 16, LANES), lambda i: (pair, 0, 0)),
        ]
        + [half_spec] * 4
        + [pl.BlockSpec((width, size), lambda i: (0, 0))] * 4,
        out_specs=[
            pl.BlockSpec((2 * size, 3 * LANES), lambda i: (0, 0)),
            pl.BlockSpec((2 * size, 3 * LANES), lambda i: (0, 0)),
            pl.BlockSpec((16, LANES), lambda i: (0, 0)),
            pl.BlockSpec(part.shape, lambda i: (0, 0, 0, 0)),
            pl.BlockSpec(part.shape, lambda i: (0, 0, 0, 0)),
        ],
        out_shape=[
            jax.ShapeDtypeStruct((2 * size, 3 * LANES), BF16),
            jax.ShapeDtypeStruct((2 * size, 3 * LANES), BF16),
            jax.ShapeDtypeStruct((16, LANES), F32),
            part,
            part,
        ],
        scratch_shapes=[
            pltpu.VMEM((3, 8 + length, LANES), F32),
            pltpu.VMEM((3, 8 + length, LANES), F32),
            pltpu.VMEM((2, length, LANES), BF16),
            pltpu.VMEM((2, length, LANES), BF16),
            pltpu.VMEM((LANES, length), BF16),
            pltpu.VMEM((8, length), F32),
            pltpu.VMEM((LANES, length), F32),
            pltpu.VMEM((2, length, LANES), BF16),
            pltpu.VMEM((length, 3 * LANES), BF16),
        ],
        compiler_params=params(62),
        cost_estimate=CHEAP,
        name="attend_back",
    )(member, *proj, mixed, lse, taps, own, send, grad_own, grad_recv, *normed)


def canonical(flag, own_ref, recv_ref):
    own = own_ref[...]
    recv = recv_ref[...]
    return jnp.concatenate(
        [jnp.where(flag == 0, own, recv), jnp.where(flag == 0, recv, own)], axis=1
    )


def ffn_forward_kernel(
    s_ref,
    hown_ref,
    hrecv_ref,
    wout_ref,
    tok0,
    tok1,
    cot0,
    cot1,
    gain_ref,
    bias_ref,
    up_ref,
    upb_ref,
    down_ref,
    downb_ref,
    res_ref,
    nf_ref,
    gf_ref,
    relu_ref,
    out0,
    out1,
    dbias_ref,
    keep_ref,
    send_ref,
    acc,
):
    step = pl.program_id(0)
    size = tok0.shape[0]
    core = s_ref[0]
    halves = ((0, s_ref[1] * size), (size, lax.bitwise_xor(s_ref[1], 2) * size))

    def valid(start):
        row = start + lax.broadcasted_iota(jnp.int32, tok0.shape, 0)
        return row < s_ref[2]

    @pl.when(step == 0)
    def _():
        attended = dot_nn(canonical(core, hown_ref, hrecv_ref), wout_ref[...])
        for tok, cot, (first, start) in zip((tok0, tok1), (cot0, cot1), halves):
            rows = slice(first, first + size)
            residual = tok[...].astype(F32) + attended[rows]
            res_ref[rows, :] = residual
            scaled, _ = norm_stats(residual)
            nf_ref[rows, :] = (scaled * gain_ref[...] + bias_ref[...]).astype(BF16)
            grad = cot[...]
            gf_ref[rows, :] = jnp.where(valid(start), grad, jnp.zeros_like(grad))
        dbias_ref[0:1, :] = jnp.sum(gf_ref[...].astype(F32), axis=0, keepdims=True)
        acc[...] = jnp.zeros_like(acc)

    relu = jnp.maximum(dot_nn(nf_ref[...], up_ref[...]) + upb_ref[...], 0.0)
    relu_ref[...] = relu
    act = (relu * relu).astype(BF16)
    acc[...] += dot_nn(act, down_ref[...])
    grad = dot_tn(act, gf_ref[...])
    rows = grad.shape[0] // 8
    store_parts(
        core,
        [
            [
                tile
                for chunk in (bit, bit + 4, bit + 2, bit + 6)
                for tile in lane_tiles(grad[chunk * rows : (chunk + 1) * rows])
            ]
            for bit in range(2)
        ],
        keep_ref,
        send_ref,
    )

    @pl.when(step == pl.num_programs(0) - 1)
    def _():
        for out, (first, start) in zip((out0, out1), halves):
            rows = slice(first, first + size)
            total = res_ref[rows, :] + (acc[rows, :] + downb_ref[...])
            out[...] = jnp.where(valid(start), total, 0.0).astype(BF16).reshape(out.shape)


def ffn_forward(scalars, hown, hrecv, wout, toks, cots, gain, bias, up, upb, down, downb):
    rows = 2 * toks[0].shape[0]
    width, ff = up.shape
    tile = ff // 4
    part = jax.ShapeDtypeStruct((2, 2, 2, 2, tile // 8 * width // LANES, LANES), BF16)
    part_spec = pl.BlockSpec(
        (2, 2, 1, 1) + part.shape[4:], lambda j, _: (0, 0, lax.rem(j, 2), lax.div(j, 2), 0, 0)
    )
    full = lambda dtype: jax.ShapeDtypeStruct((rows, width), dtype)
    block = jax.ShapeDtypeStruct(toks[0].shape, BF16)
    return pl.pallas_call(
        ffn_forward_kernel,
        grid_spec=pltpu.PrefetchScalarGridSpec(
            num_scalar_prefetch=1,
            grid=(4,),
            in_specs=[still(a) for a in (hown, hrecv, wout, *toks, *cots, gain, bias)]
            + [
                pl.BlockSpec((width, tile), lambda j, _: (0, j)),
                pl.BlockSpec((1, tile), lambda j, _: (0, j)),
                pl.BlockSpec((tile, width), lambda j, _: (j, 0)),
                still(downb),
            ],
            out_specs=[once((rows, width), lambda j, _: (0, 0))] * 3
            + [
                pl.BlockSpec((rows, tile), lambda j, _: (0, j)),
                once((1,) + block.shape, lambda j, s: (s[4], 0, 0)),
                once(block.shape, lambda j, _: (0, 0)),
                pl.BlockSpec((8, width), lambda j, _: (0, 0)),
                part_spec,
                part_spec,
            ],
            scratch_shapes=[pltpu.VMEM((rows, width), F32)],
        ),
        out_shape=[
            full(F32),
            full(BF16),
            full(BF16),
            jax.ShapeDtypeStruct((rows, ff), F32),
            jax.ShapeDtypeStruct((2,) + block.shape, BF16),
            block,
            jax.ShapeDtypeStruct((8, width), F32),
            part,
            part,
        ],
        compiler_params=params(60),
        cost_estimate=CHEAP,
        name="ffn_forward",
    )(scalars, hown, hrecv, wout, *toks, *cots, gain, bias, up, upb, down, downb)


def ffn_backward_kernel(
    s_ref,
    gf_ref,
    nf_ref,
    res_ref,
    hown_ref,
    hrecv_ref,
    wout_ref,
    gain_ref,
    dbias_ref,
    relu_ref,
    up_ref,
    down_ref,
    gres_ref,
    gown_ref,
    gsend_ref,
    sums_ref,
    keep_ref,
    send_ref,
    nft,
    gn,
):
    step = pl.program_id(0)
    last = pl.num_programs(0) - 1
    core = s_ref[0]

    def store(grad):
        rows = grad.shape[0] // 32
        store_parts(
            core,
            [
                [
                    tile
                    for place in range(16)
                    for chunk in [
                        bit
                        + (place >> 3 & 1) * 2
                        + (place >> 2 & 1) * 4
                        + (place >> 1 & 1) * 8
                        + (place & 1) * 16
                    ]
                    for tile in lane_tiles(grad[chunk * rows : (chunk + 1) * rows])
                ]
                for bit in range(2)
            ],
            keep_ref,
            send_ref,
        )

    @pl.when(step == 0)
    def _():
        nft[...] = nf_ref[...].T
        gn[...] = jnp.zeros_like(gn)

    @pl.when(step < last)
    def _():
        grad_act = dot_nt(gf_ref[...], down_ref[...])
        grad_pre = (2.0 * relu_ref[...] * grad_act).astype(BF16)
        sums_ref[pl.ds(step, 1), :] = jnp.sum(grad_pre.astype(F32), axis=0, keepdims=True)
        gn[...] += dot_nt(grad_pre, up_ref[...])
        store(dot_nn(nft[...], grad_pre))

    @pl.when(step == last)
    def _():
        scaled, inv_std = norm_stats(res_ref[...])
        grad = gn[...]
        sums_ref[4:5, :] = jnp.sum(grad * scaled, axis=0, keepdims=True)
        sums_ref[5:6, :] = jnp.sum(grad, axis=0, keepdims=True)
        sums_ref[6:7, :] = dbias_ref[0:1, :]
        sums_ref[7:8, :] = jnp.zeros_like(sums_ref[7:8, :])
        total = gf_ref[...].astype(F32) + norm_backward(grad, gain_ref[...], scaled, inv_std)
        gres_ref[...] = total
        attended = total.astype(BF16)
        heads = dot_nt(attended, wout_ref[...]).astype(BF16)
        middle = heads.shape[1] // 2
        gown_ref[...] = jnp.where(core == 0, heads[:, :middle], heads[:, middle:])
        gsend_ref[...] = jnp.where(core == 0, heads[:, middle:], heads[:, :middle])
        store(dot_tn(canonical(core, hown_ref, hrecv_ref), attended))


def ffn_backward(scalars, gf, nf, res, hown, hrecv, wout, gain, dbias, relu, up, down):
    rows, width = nf.shape
    ff = up.shape[1]
    tile = ff // 4
    block = width // 32 * tile // LANES
    part = jax.ShapeDtypeStruct((2, 2, 2, 2, 5 * block, LANES), BF16)
    part_spec = pl.BlockSpec((2, 2, 2, 2, block, LANES), lambda j: (0, 0, 0, 0, j, 0))
    now = lambda j: jnp.minimum(j, 3)
    half = jax.ShapeDtypeStruct(hown.shape, BF16)
    return pl.pallas_call(
        ffn_backward_kernel,
        grid=(5,),
        in_specs=[SMEM_SPEC]
        + [still(a) for a in (gf, nf, res, hown, hrecv, wout, gain, dbias)]
        + [
            pl.BlockSpec((rows, tile), lambda j: (0, now(j))),
            pl.BlockSpec((width, tile), lambda j: (0, now(j))),
            pl.BlockSpec((tile, width), lambda j: (now(j), 0)),
        ],
        out_specs=[once((rows, width), lambda j: (0, 0))]
        + [once(half.shape, lambda j: (0, 0))] * 2
        + [
            pl.BlockSpec((8, width), lambda j: (0, 0)),
            part_spec,
            part_spec,
        ],
        out_shape=[
            jax.ShapeDtypeStruct((rows, width), F32),
            half,
            half,
            jax.ShapeDtypeStruct((8, width), F32),
            part,
            part,
        ],
        scratch_shapes=[pltpu.VMEM((width, rows), BF16), pltpu.VMEM((rows, width), F32)],
        compiler_params=params(60),
        cost_estimate=CHEAP,
        name="ffn_backward",
    )(scalars, gf, nf, res, hown, hrecv, wout, gain, dbias, relu, up, down)


def input_grad_kernel(
    final, s_ref, o0, o1, o2, r0, r1, r2, w_ref, x_ref, gres_ref, gain_ref, *refs
):
    out_ref, sums_ref, buf = refs[-3:]
    for n, ref in enumerate((o0, o1, o2, r0, r1, r2)):
        side = s_ref[0] if n < 3 else 1 - s_ref[0]
        start = pl.multiple_of((side * 3 + n % 3) * LANES, LANES)
        for c, tile in enumerate(lane_tiles(ref[...])):
            buf[c, :, pl.ds(start, LANES)] = tile
    grad = dot_nt(buf[0], w_ref[0]) + dot_nt(buf[1], w_ref[1]) + dot_nt(buf[2], w_ref[2])
    scaled, inv_std = norm_stats(x_ref[...].astype(F32))
    first = 17 if final else 0

    @pl.when(pl.program_id(0) == 0)
    def _():
        sums_ref[...] = jnp.zeros_like(sums_ref)
        if final:
            early_ref, before_ref, *convs = refs[:-3]
            sums_ref[0:8, :] = early_ref[...]
            sums_ref[first : first + 2, :] = before_ref[0:2, :]
            for n, conv in enumerate(convs):
                start = pl.multiple_of((s_ref[0] * 3 + n) * LANES, LANES)
                sums_ref[8:17, pl.ds(start, LANES)] = conv[0:9, :]

    sums_ref[first : first + 1, :] += jnp.sum(grad * scaled, axis=0, keepdims=True)
    sums_ref[first + 1 : first + 2, :] += jnp.sum(grad, axis=0, keepdims=True)
    total = gres_ref[...] + norm_backward(grad, gain_ref[...], scaled, inv_std)
    out_ref[...] = total.astype(BF16).reshape(out_ref.shape)


def input_grad(slot, scalars, owns, recvs, weights, x, grad_residual, gain, small=()):
    rows, width = x.shape
    tile = rows // 2
    final = len(small) > 0
    part = pl.BlockSpec((tile, 3 * LANES), lambda i, _: (2 * slot + i, 0))
    if final:
        out_spec = pl.BlockSpec((1, tile, width), lambda i, s: (s[4], i, 0))
        out = jax.ShapeDtypeStruct((2, rows, width), BF16)
    else:
        out_spec = pl.BlockSpec((tile, width), lambda i, _: (i, 0))
        out = jax.ShapeDtypeStruct((rows, width), BF16)
    sums = jax.ShapeDtypeStruct((24 if final else 8, width), F32)
    return pl.pallas_call(
        functools.partial(input_grad_kernel, final),
        grid_spec=pltpu.PrefetchScalarGridSpec(
            num_scalar_prefetch=1,
            grid=(2,),
            in_specs=[part] * 6
            + [
                still(weights),
                pl.BlockSpec((tile, width), lambda i, _: (i, 0)),
                pl.BlockSpec((tile, width), lambda i, _: (2 * slot + i, 0)),
                still(gain),
            ]
            + [still(a) for a in small],
            out_specs=[out_spec, pl.BlockSpec(sums.shape, lambda i, _: (0, 0))],
            scratch_shapes=[pltpu.VMEM((3, tile, width), BF16)],
        ),
        out_shape=[out, sums],
        compiler_params=params(62),
        cost_estimate=CHEAP,
        name="input_grad",
    )(scalars, *owns, *recvs, weights, x, grad_residual, gain, *small)


FREE, ONE, MINE, OTHER = range(4)
BIT_AT = (4, 3, 5, 6)


class Segment:
    def __init__(self, arrays, first, rows):
        self.rows = rows
        self.parts = [(array, self.fresh(array), first) for array in arrays]

    @staticmethod
    def fresh(array):
        return [FREE if n == 2 else ONE for n in array.shape[:4]]

    def chosen(self, dim):
        found = []
        for array, marks, first in self.parts:
            marks = list(marks)
            if dim is not None and marks[dim] == FREE:
                marks[dim] = OTHER
            found.append((array, tuple(marks), first, self.rows))
        return found

    def settle(self, dim, arrived, first):
        parts = []
        for array, marks, own_first in self.parts:
            marks = list(marks)
            if marks[dim] == FREE:
                marks[dim] = MINE
            parts.append((array, marks, own_first))
        self.parts = parts + [(arrived, self.fresh(arrived), first)]


def settle(segments, dim, arrived):
    first = 0
    for segment in segments:
        segment.settle(dim, arrived, first)
        first += segment.rows


def sum_kernel(plan, finish, count, s_ref, *refs):
    pieces = [p for parts in plan for p in parts]
    arrays, outs = refs[:count], refs[count : len(refs) - len(pieces) - 1]
    bufs, sems = refs[len(refs) - len(pieces) - 1 : -1], refs[-1]
    copies = []
    for n, (place, marks, first, rows) in enumerate(pieces):
        where = []
        for dim, mark in enumerate(marks):
            bit = s_ref[BIT_AT[dim]]
            start = {FREE: 0, ONE: 0, MINE: bit, OTHER: 1 - bit}[mark]
            where.append(pl.ds(start, 2 if mark == FREE else 1))
        source = arrays[place].at[tuple(where) + (pl.ds(first, rows), slice(None))]
        copies.append(pltpu.make_async_copy(source, bufs[n], sems.at[n]))
        copies[-1].start()
    n = 0
    totals = []
    for parts in plan:
        for copy in copies[n : n + len(parts)]:
            copy.wait()
        own = bufs[n : n + len(parts)]
        n += len(parts)

        def total(lead, rows, own=own):
            value = None
            for buf in own:
                piece = buf[lead + (rows, slice(None))].astype(F32)
                value = piece if value is None else value + piece
            return value

        totals.append(total)
    finish(s_ref, totals, outs)


def sum_call(scalars, segments, dims, finish, out_shape, name):
    arrays, plan, scratch = [], [], []
    for segment, dim in zip(segments, dims):
        parts = []
        for array, marks, first, rows in segment.chosen(dim):
            place = next((n for n, a in enumerate(arrays) if a is array), None)
            if place is None:
                place = len(arrays)
                arrays.append(array)
            parts.append((place, marks, first, rows))
            sizes = tuple(2 if mark == FREE else 1 for mark in marks)
            scratch.append(pltpu.VMEM(sizes + (rows, LANES), BF16))
        plan.append(parts)
    whole = lambda shape: pl.BlockSpec(shape, lambda i: (0,) * len(shape))
    return pl.pallas_call(
        functools.partial(sum_kernel, plan, finish, len(arrays)),
        grid=(1,),
        in_specs=[SMEM_SPEC] + [pl.BlockSpec(memory_space=pltpu.HBM)] * len(arrays),
        out_specs=[whole(o.shape) for o in out_shape],
        out_shape=out_shape,
        scratch_shapes=scratch + [pltpu.SemaphoreType.DMA((len(scratch),))],
        compiler_params=params(62),
        cost_estimate=CHEAP,
        name=name,
    )(scalars, *arrays)


def outgoing(scalars, groups, dims, name="stage_sum"):
    shapes = []
    for group, dim in zip(groups, dims):
        marks = [group[0].chosen(dim)[0][1]]
        sizes = tuple(2 if mark == FREE else 1 for mark in marks[0])
        shapes.append(jax.ShapeDtypeStruct(sizes + (sum(g.rows for g in group), LANES), BF16))

    def finish(s_ref, totals, outs):
        n = 0
        for group, out in zip(groups, outs):
            first = 0
            for segment in group:
                for lead in itertools.product(*[range(size) for size in out.shape[:4]]):
                    for row in range(0, segment.rows, 48):
                        value = totals[n](lead, slice(row, row + 48))
                        out[lead + (slice(first + row, first + row + 48), slice(None))] = (
                            value.astype(BF16)
                        )
                first += segment.rows
                n += 1

    segments = [segment for group in groups for segment in group]
    each = [dim for group, dim in zip(groups, dims) for _ in group]
    return sum_call(scalars, segments, each, finish, shapes, name)


def hop(value, stage):
    return lax.ppermute(value, stage[0], stage[1])


def ffn_plain(heads, toks, cot, valid, wout, gain, bias, up, upb, down, downb):
    residual = toks.astype(F32) + jnp.dot(heads, wout, preferred_element_type=F32)
    scaled, inv_std = norm_stats(residual)
    normed = (scaled * gain + bias).astype(BF16)
    relu = jnp.maximum(jnp.dot(normed, up, preferred_element_type=F32) + upb, 0.0)
    act = jnp.square(relu).astype(BF16)
    out = jnp.dot(act, down, preferred_element_type=F32) + downb
    result = jnp.where(valid, residual + out, 0.0).astype(BF16)
    grad_ffn = jnp.where(valid, cot, jnp.zeros_like(cot))
    grad_y = grad_ffn.astype(F32)
    grad_act = jnp.einsum("td,fd->tf", grad_ffn, down, preferred_element_type=F32)
    grad_pre = (2.0 * relu * grad_act).astype(BF16)
    grad = jnp.einsum("tf,df->td", grad_pre, up, preferred_element_type=F32)
    sums = jnp.stack([jnp.sum(grad * scaled, axis=0), jnp.sum(grad, axis=0)])
    grad_residual = grad_y + norm_backward(grad, gain, scaled, inv_std)
    attended = grad_residual.astype(BF16)
    grad_heads = jnp.einsum("td,ed->te", attended, wout, preferred_element_type=F32)
    return (
        result,
        grad_residual,
        grad_heads.astype(BF16),
        sums,
        jnp.sum(grad_pre.astype(F32), axis=0),
        jnp.sum(grad_y, axis=0),
        jnp.einsum("td,tf->df", normed, grad_pre, preferred_element_type=F32),
        jnp.einsum("tf,td->fd", act, grad_ffn, preferred_element_type=F32),
        jnp.einsum("te,td->ed", heads, attended, preferred_element_type=F32),
    )


def on_device(
    tokens,
    cotangent,
    lengths,
    pre_attn_gain,
    pre_attn_bias,
    qkv_weight,
    conv_weight,
    out_weight,
    pre_ffn_gain,
    pre_ffn_bias,
    up_weight,
    up_bias,
    down_weight,
    down_bias,
):
    groups = lax.axis_size("mp")
    batch_groups = lax.axis_size("batch")
    devices = groups * batch_groups
    member = lax.axis_index("mp").astype(jnp.int32)
    batch = lax.axis_index("batch").astype(jnp.int32)
    seqs, rows, width = tokens.shape
    ff = up_weight.shape[1]
    middle = width // 2
    quarter = width // groups
    pairs = middle // LANES
    taps = conv_weight.shape[1]
    assert groups == 4 and seqs == 2 and pairs == 3 and taps == 3
    fast = batch_groups == 8 and (width // devices) % 8 == 0
    half = lax.shift_right_logical(member, 1)
    core = lax.bitwise_and(member, 1)
    x_bit = lax.bitwise_and(batch, 1)
    z0_bit = lax.bitwise_and(lax.shift_right_logical(batch, 1), 1)
    z1_bit = lax.shift_right_logical(batch, 2)
    gain_attn = pre_attn_gain.astype(F32).reshape(1, width)
    bias_attn = pre_attn_bias.astype(F32).reshape(1, width)
    gain_ffn = pre_ffn_gain.astype(F32).reshape(1, width)
    bias_ffn = pre_ffn_bias.astype(F32).reshape(1, width)
    up_bias_f = up_bias.astype(F32).reshape(1, ff)
    down_bias_f = down_bias.astype(F32).reshape(1, width)

    def swap_core(value):
        return lax.ppermute(value, "mp", CORE)

    def swap_pair(value):
        return lax.ppermute(value, "mp", PAIR)

    def pick(value, index):
        starts = (index,) + (jnp.int32(0),) * (value.ndim - 1)
        return lax.dynamic_slice(value, starts, (1,) + value.shape[1:])[0]

    length = pick(lengths, half)
    scalars = jnp.stack([core, member, length, x_bit, half, z0_bit, z1_bit]).astype(jnp.int32)

    hops = [("mp", PAIR)] + [
        ("batch", [(i, i ^ flip) for i in range(batch_groups)]) for flip in (1, 2, 4)
    ]
    DY, DX, DZ0, DZ1 = range(4)
    tie = lax.optimization_barrier

    tok_pair = swap_pair(pick(tokens, 1 - half))
    tok_own = pick(tokens, half)
    cot_own = pick(cotangent, half)
    tok_core = swap_core(tok_own)
    taps_own = lax.dynamic_slice_in_dim(conv_weight, core * middle, middle, 2).astype(F32)
    taps_own = taps_own.reshape(3 * taps, pairs, LANES).transpose(1, 0, 2)
    taps_own = jnp.pad(taps_own, ((0, 0), (0, 16 - 3 * taps), (0, 0)))

    def norm_project(block):
        return project(scalars, block, gain_attn, bias_attn, qkv_weight)

    first = norm_project(tok_own)
    prepared = (cot_own, pick(cotangent, 1 - half), taps_own, gain_ffn, bias_ffn, up_bias_f, down_bias_f)
    tok_core, prepared = tie((tok_core, prepared))
    cot_own, cot_send, taps_own, gain_ffn, bias_ffn, up_bias_f, down_bias_f = prepared
    second = norm_project(tok_core)
    tok_pair, first, second = tie((tok_pair, first, second))
    tok_cross = swap_core(tok_pair)
    third = norm_project(tok_pair)
    tok_cross, third = tie((tok_cross, third))
    fourth = norm_project(tok_cross)
    cot_send, fourth = tie((cot_send, fourth))
    cot_pair = swap_pair(cot_send)
    normed, proj = zip(first, second, third, fourth)
    mixed, heads_own, heads_send, lse = attend(scalars, proj, taps_own)
    heads_recv = swap_core(heads_send)

    if fast:
        (
            residual,
            normed_ffn,
            grad_ffn,
            relu,
            result_all,
            result_give,
            sums_down,
            down_keep,
            down_send,
        ) = ffn_forward(
            scalars,
            heads_own,
            heads_recv,
            out_weight,
            (tok_own, tok_pair),
            (cot_own, cot_pair),
            gain_ffn,
            bias_ffn,
            up_weight,
            up_bias_f,
            down_weight,
            down_bias_f,
        )
        (
            grad_residual,
            grad_own,
            grad_send,
            early,
            up_keep,
            up_send,
        ) = ffn_backward(
            scalars,
            grad_ffn,
            normed_ffn,
            residual,
            heads_own,
            heads_recv,
            out_weight,
            gain_ffn,
            sums_down,
            relu,
            up_weight,
            down_weight,
        )
    else:
        row = jnp.arange(rows, dtype=jnp.int32)
        row_pos = [member * rows + row, jnp.bitwise_xor(member, 2) * rows + row]
        heads_all = jnp.concatenate(
            [
                jnp.where(core == 0, heads_own, heads_recv),
                jnp.where(core == 0, heads_recv, heads_own),
            ],
            axis=1,
        )
        (
            result,
            grad_residual,
            grad_heads,
            sums_ffn,
            sums_up,
            sums_down,
            grad_up,
            grad_down,
            grad_out,
        ) = ffn_plain(
            heads_all,
            jnp.concatenate([tok_own, tok_pair], axis=0),
            jnp.concatenate([cot_own, cot_pair], axis=0),
            (jnp.concatenate(row_pos) < length)[:, None],
            out_weight,
            gain_ffn,
            bias_ffn,
            up_weight,
            up_bias_f,
            down_weight,
            down_bias_f,
        )
        result_all, result_give = jnp.stack([result[:rows]] * 2), result[rows:]
        early = [sums_up.reshape(ff // width, width), sums_ffn, sums_down[None]]
        early = jnp.concatenate(early + [jnp.zeros((1, width), F32)], axis=0)
        grad_own = lax.dynamic_slice_in_dim(grad_heads, core * middle, middle, 1)
        grad_send = lax.dynamic_slice_in_dim(grad_heads, (1 - core) * middle, middle, 1)
    result_back = swap_pair(result_give)
    if fast:
        down_recv = swap_core(down_send)
        grad_own, grad_send, up_keep, up_send, down_recv, result_back = tie(
            (grad_own, grad_send, up_keep, up_send, down_recv, result_back)
        )
        up_recv = swap_core(up_send)
    grad_recv = swap_core(grad_send)
    if fast:
        down_rows = down_keep.shape[4]
        up_rows = up_keep.shape[4]
        each = (down_rows + up_rows) // 3
        down = (down_keep, down_recv)
        up = (up_keep, up_recv)
        rest = down_rows - each
        down_a, down_b = Segment(down, 0, each), Segment(down, each, rest)
        up_a, up_b = Segment(up, 0, each - rest), Segment(up, each - rest, each)
        group_1, group_2, group_3 = [down_a], [down_b, up_a], [up_b]

        def stage(dims, groups=(group_1, group_2, group_3)):
            return outgoing(scalars, groups, dims)

        def arrive(dims, sent, groups=(group_1, group_2, group_3)):
            for group, dim, value in zip(groups, dims, sent):
                settle(group, dim, value)

        dims = (DX, DZ0, DY)
        sent = stage(dims)
        grad_own, grad_recv, sent = tie((grad_own, grad_recv, sent))
        sent = [hop(v, hops[d]) for v, d in zip(sent, dims)]
        arrive(dims, sent)

    def backward(pair, grad_recv):
        own, send, conv, keep, give = attend_back(
            pair,
            scalars,
            proj,
            mixed,
            lse,
            taps_own,
            heads_own,
            heads_send,
            grad_own,
            grad_recv,
            normed,
        )
        keep = keep.reshape((1, 1) + keep.shape)
        give = give.reshape((1, 1) + give.shape)
        return own, send, conv, keep, give

    qkv_rows = 3 * width // 8
    own_0, send_0, conv_0, keep_0, give_0 = backward(0, grad_recv)
    if fast:
        dims = (DY, DZ1, DX)
        sent = stage(dims)
        grad_recv, own_0, send_0, give_0, sent = tie((grad_recv, own_0, send_0, give_0, sent))
        sent = [hop(v, hops[d]) for v, d in zip(sent, dims)]
        arrive(dims, sent)
        qkv_0 = Segment((keep_0, hop(give_0, hops[DX])), 0, qkv_rows)
        group_1.append(qkv_0)
    recv_0 = swap_core(send_0)
    own_1, send_1, conv_1, keep_1, give_1 = backward(1, grad_recv)
    if fast:
        dims = (DZ0, DX, DZ1)
        sent = stage(dims)
        grad_recv, own_1, send_1, give_1, recv_0, sent = tie(
            (grad_recv, own_1, send_1, give_1, recv_0, sent)
        )
        sent = [hop(v, hops[d]) for v, d in zip(sent, dims)]
        give_1 = hop(give_1, hops[DX])
    recv_1 = swap_core(send_1)
    own_2, send_2, conv_2, keep_2, give_2 = backward(2, grad_recv)
    if fast:
        own_2, send_2, give_2, recv_1, sent, give_1 = tie(
            (own_2, send_2, give_2, recv_1, sent, give_1)
        )
        arrive(dims, sent)
        qkv_1 = Segment((keep_1, give_1), 0, qkv_rows)
        give_2 = hop(give_2, hops[DX])
    recv_2 = swap_core(send_2)
    if fast:
        dims = (DZ1, DY, DZ0)
        sent = stage(dims)
        recv_2, sent = tie((recv_2, sent))
        ffn_waiting = [hop(v, hops[d]) for v, d in zip(sent, dims)]
    g_own = (own_0, own_1, own_2)
    g_send = (send_0, send_1, send_2)
    g_recv = (recv_0, recv_1, recv_2)
    g_conv = (conv_0, conv_1, conv_2)
    grad_in_pair, sums_pair = input_grad(
        1, scalars, g_own, g_recv, qkv_weight, tok_pair, grad_residual, gain_attn
    )
    grad_in_back = swap_pair(grad_in_pair)
    tok_last = tok_own
    if fast:
        give_2, sums_pair = tie((give_2, sums_pair))
        qkv_2 = Segment((keep_2, give_2), 0, qkv_rows)
        (sent,) = outgoing(scalars, [[qkv_1, qkv_2]], [DZ0])
        tok_last, sums_pair, sent = tie((tok_own, sums_pair, sent))
        waiting = hop(sent, hops[DZ0])
    tokens_grad, small = input_grad(
        0,
        scalars,
        g_own,
        g_recv,
        qkv_weight,
        tok_last,
        grad_residual,
        gain_attn,
        (early, sums_pair) + g_conv,
    )

    def place(both, other):
        return lax.dynamic_update_slice(both, other[None], (1 - half, 0, 0))

    result_all = place(result_all, result_back)
    index = batch * groups + member
    share = width // devices
    part = width // batch_groups

    if not fast:
        axes = ("batch", "mp")
        grad_qkv = 0.0
        for n, (norm, slot) in enumerate(zip(normed, (0, 0, 1, 1))):
            source = (g_own, g_send)[n % 2]
            grads = jnp.concatenate([g[slot * rows : (slot + 1) * rows] for g in source], axis=1)
            grad_qkv = grad_qkv + jnp.einsum("dt,te->de", norm, grads, preferred_element_type=F32)
        grad_qkv = grad_qkv.reshape(width, pairs, 3, LANES).transpose(2, 0, 1, 3)
        qkv_full = lax.dynamic_update_slice_in_dim(
            jnp.zeros((3, width, width), F32), grad_qkv.reshape(3, width, middle), core * middle, 2
        )
        qkv_flat = qkv_full.reshape(3, batch_groups, part, groups, quarter)
        qkv_flat = qkv_flat.transpose(1, 3, 0, 2, 4).reshape(devices * 3 * part, quarter)

        def scatter(value):
            return lax.psum_scatter(value, axes, scatter_dimension=0, tiled=True)

        small = lax.psum(small, axes)
        qkv_out = scatter(qkv_flat).reshape(3, part, quarter)
        up_out, down_out, out_out = scatter(grad_up), scatter(grad_down), scatter(grad_out)
    else:
        small = small + hop(small, ("mp", CORE))
        small, waiting = tie((small, waiting))
        settle([qkv_1, qkv_2], DZ0, waiting)
        (sent,) = outgoing(scalars, [[qkv_1, qkv_2]], [DZ1])
        sent = hop(sent, hops[DZ1])
        small = small + hop(small, hops[DX])
        small, ffn_waiting = tie((small, ffn_waiting))
        arrive((DZ1, DY, DZ0), ffn_waiting)
        small = small + hop(small, hops[DZ0])
        small, sent, grad_in_back = tie((small, sent, grad_in_back))
        settle([qkv_1, qkv_2], DZ1, sent)
        small = small + hop(small, hops[DZ1])
        small = small + hop(small, hops[DY])

        def finish_ffn(s_ref, totals, outs):
            whole = [total((0,) * 4, slice(None)) for total in totals]
            downs = jnp.concatenate(whole[0:2], axis=0)
            ups = jnp.concatenate(whole[2:4], axis=0)
            down_out, up_out, out_out = outs
            for out, values in ((down_out, downs), (up_out, ups), (out_out, ups[down_rows:])):
                size, cols = out.shape
                for n in range(cols // LANES):
                    out[:, n * LANES : (n + 1) * LANES] = values[n * size : (n + 1) * size]

        down_out, up_out, out_out = sum_call(
            scalars,
            [down_a, down_b, up_a, up_b],
            [None] * 4,
            finish_ffn,
            [
                jax.ShapeDtypeStruct((ff // devices, width), F32),
                jax.ShapeDtypeStruct((share, ff), F32),
                jax.ShapeDtypeStruct((share, width), F32),
            ],
            "ffn_sum",
        )

        def finish_qkv(s_ref, totals, outs):
            first, middle, last = [total((0,) * 4, slice(None)) for total in totals]
            lower = jnp.concatenate([first, middle[:, :HEAD_DIM]], axis=1)
            upper = jnp.concatenate([middle[:, HEAD_DIM:], last], axis=1)
            outs[0][...] = jnp.where(s_ref[0] == 0, lower, upper)
            outs[1][...] = jnp.where(s_ref[4] == 0, upper, lower).astype(BF16)
            outs[2][...] = jnp.where(s_ref[4] == 0, lower, upper).astype(BF16)

        keep, straight, crossed = sum_call(
            scalars,
            [qkv_0, qkv_1, qkv_2],
            [None] * 3,
            finish_qkv,
            [jax.ShapeDtypeStruct((qkv_rows, quarter), t) for t in (F32, BF16, BF16)],
            "qkv_sum",
        )
        straight = lax.ppermute(straight, "mp", [(2, 0), (0, 1), (3, 2), (1, 3)])
        crossed = lax.ppermute(crossed, "mp", [(2, 1), (1, 2)])
        qkv_out = straight.astype(F32) + jnp.where(half == core, keep, crossed.astype(F32))
        qkv_out = qkv_out.reshape(3, part, quarter)

    tokens_grad = place(tokens_grad, grad_in_back)
    up_bias_out = pick(small[: ff // width].reshape(devices, ff // devices), index)
    mine = pick(small.reshape(24, devices, share).transpose(1, 0, 2), index)
    return (
        result_all,
        tokens_grad,
        mine[17],
        mine[18],
        qkv_out,
        mine[8:17].reshape(3, taps, share),
        out_out,
        mine[4],
        mine[5],
        up_out,
        up_bias_out,
        down_out,
        mine[6],
    )


def solution(mesh):
    in_specs = (
        P("batch", "mp", None),
        P("batch", "mp", None),
        P("batch"),
    ) + (P(),) * 11
    out_specs = (
        P("batch", "mp", None),
        P("batch", "mp", None),
        P(("batch", "mp")),
        P(("batch", "mp")),
        P(None, "batch", "mp"),
        P(None, None, ("batch", "mp")),
        P(("batch", "mp"), None),
        P(("batch", "mp")),
        P(("batch", "mp")),
        P(("batch", "mp"), None),
        P(("batch", "mp")),
        P(("batch", "mp"), None),
        P(("batch", "mp")),
    )
    return jax.shard_map(
        on_device, mesh=mesh, in_specs=in_specs, out_specs=out_specs, check_vma=False
    )
```

```python
import functools
import itertools

import jax
import jax.numpy as jnp
from jax import lax
from jax.experimental import pallas as pl
from jax.experimental.pallas import tpu as pltpu
from jax.sharding import PartitionSpec as P

HEAD_DIM = 64
LANES = 128
EPSILON = 1e-05
NEGATIVE = -1000000000.0
QBLOCK = 512
KBLOCK = 256
F32 = jnp.float32
BF16 = jnp.bfloat16

CORE = [(i, i ^ 1) for i in range(4)]
PAIR = [(i, i ^ 2) for i in range(4)]


def dot_nt(left, right):
    return lax.dot_general(left, right, (((1,), (1,)), ((), ())), preferred_element_type=F32)


def dot_nn(left, right):
    return lax.dot_general(left, right, (((1,), (0,)), ((), ())), preferred_element_type=F32)


def dot_tn(left, right):
    return lax.dot_general(left, right, (((0,), (0,)), ((), ())), preferred_element_type=F32)


def params(mib):
    return pltpu.CompilerParams(vmem_limit_bytes=mib << 20)


def lane_tiles(values):
    return [values[:, n : n + LANES] for n in range(0, values.shape[1], LANES)]


def once(shape, index_map):
    return pl.BlockSpec(shape, index_map, pipeline_mode=pl.Buffered(1))


def still(array):
    return once(array.shape, lambda *_: (0,) * array.ndim)


CHEAP = pl.CostEstimate(flops=1 << 20, bytes_accessed=1 << 16, transcendentals=0)
SMEM_SPEC = pl.BlockSpec(memory_space=pltpu.SMEM)


def norm_stats(values):
    center = values - jnp.mean(values, axis=-1, keepdims=True)
    inv_std = lax.rsqrt(jnp.mean(center * center, axis=-1, keepdims=True) + EPSILON)
    return center * inv_std, inv_std


def norm_backward(grad_out, norm_gain, scaled, inv_std):
    weighted = grad_out * norm_gain
    return inv_std * (
        weighted
        - jnp.mean(weighted, axis=-1, keepdims=True)
        - scaled * jnp.mean(weighted * scaled, axis=-1, keepdims=True)
    )


def project_kernel(s_ref, x_ref, gain_ref, bias_ref, w_ref, normed_ref, proj_ref):
    scaled, _ = norm_stats(x_ref[...].astype(F32))
    normed = (scaled * gain_ref[...] + bias_ref[...]).astype(BF16)
    normed_ref[...] = normed.T
    for c in range(3):
        part = dot_nn(normed, w_ref[c]).astype(BF16)
        for n, tile in enumerate(lane_tiles(part)):
            start = (3 * n + c) * LANES
            proj_ref[:, start : start + LANES] = tile


def project(scalars, x, gain, bias, weights):
    rows, width = x.shape
    cols = 3 * width // 2
    return pl.pallas_call(
        project_kernel,
        grid_spec=pltpu.PrefetchScalarGridSpec(
            num_scalar_prefetch=1,
            grid=(1,),
            in_specs=[
                once((rows, width), lambda i, s: (0, 0)),
                once((1, width), lambda i, s: (0, 0)),
                once((1, width), lambda i, s: (0, 0)),
                once((3, width, width // 2), lambda i, s: (0, 0, s[0])),
            ],
            out_specs=[
                once((width, rows), lambda i, s: (0, 0)),
                once((rows, cols), lambda i, s: (0, 0)),
            ],
        ),
        out_shape=[
            jax.ShapeDtypeStruct((width, rows), BF16),
            jax.ShapeDtypeStruct((rows, cols), BF16),
        ],
        compiler_params=params(62),
        cost_estimate=CHEAP,
        name="project",
    )(scalars, x, gain, bias, weights)


def store_parts(flag, parts, keep_ref, send_ref):
    first = jnp.concatenate(parts[0], axis=0).astype(BF16)
    second = jnp.concatenate(parts[1], axis=0).astype(BF16)
    keep_ref[...] = jnp.where(flag == 0, first, second).reshape(keep_ref.shape)
    send_ref[...] = jnp.where(flag == 0, second, first).reshape(send_ref.shape)


def only_head(values, head):
    lane = lax.broadcasted_iota(jnp.int32, values.shape, 1)
    return jnp.where((lane // HEAD_DIM) == head, values, jnp.zeros_like(values))


def load_natural(member, blocks, dest, size, shift=0):
    for slot, block in enumerate(blocks):
        start = pl.multiple_of(lax.bitwise_xor(member, slot) * size, 8) + shift
        start = pl.multiple_of(start, 8)
        dest[pl.ds(start, size), :] = block.astype(dest.dtype)


def attend_kernel(
    m_ref, p0, p1, p2, p3, taps_ref, mixed_ref, own_ref, send_ref, lse_ref, pj, kh, vt, on, qs
):
    member = m_ref[1]
    size = p0.shape[0]
    length = 4 * size
    scale = jnp.asarray(HEAD_DIM ** (-0.5), BF16)
    for c in range(3):
        cols = slice(c * LANES, (c + 1) * LANES)
        pj[c, 0:8, :] = jnp.zeros((8, LANES), F32)
        load_natural(member, [p[:, cols] for p in (p0, p1, p2, p3)], pj.at[c], size, 8)
    for c in range(3):
        total = taps_ref[0, 3 * c : 3 * c + 1, :] * pj[c, 8 : 8 + length, :]
        total = total + taps_ref[0, 3 * c + 1 : 3 * c + 2, :] * pj[c, 7 : 7 + length, :]
        total = total + taps_ref[0, 3 * c + 2 : 3 * c + 3, :] * pj[c, 6 : 6 + length, :]
        mixed = total.astype(BF16)
        mixed_ref[:, c * LANES : (c + 1) * LANES] = mixed
        if c == 0:
            qs[...] = mixed * scale
        elif c == 1:
            kh[0] = only_head(mixed, 0)
            kh[1] = only_head(mixed, 1)
        else:
            vt[...] = mixed.T
    for first in range(0, length, QBLOCK):
        queries = qs[first : first + QBLOCK, :]
        keys = first + QBLOCK
        outs = []
        for head in range(2):
            scores = dot_nt(kh[head, 0:keys, :], queries)
            key_pos = lax.broadcasted_iota(jnp.int32, (QBLOCK, QBLOCK), 0)
            query_pos = lax.broadcasted_iota(jnp.int32, (QBLOCK, QBLOCK), 1)
            corner = jnp.where(key_pos <= query_pos, scores[first:keys, :], NEGATIVE)
            if first:
                scores = jnp.concatenate([scores[:first, :], corner], axis=0)
            else:
                scores = corner
            top = jnp.max(scores, axis=0, keepdims=True)
            weights = jnp.exp(scores - top)
            total = jnp.sum(weights, axis=0, keepdims=True)
            part = dot_nn(
                vt[head * HEAD_DIM : (head + 1) * HEAD_DIM, 0:keys], weights.astype(BF16)
            )
            outs.append(part * (1.0 / total))
            lse_ref[0, head : head + 1, first : first + QBLOCK] = top + jnp.log(total)
        on[first : first + QBLOCK, :] = jnp.concatenate(outs, axis=0).T.astype(BF16)
    for slot in range(4):
        start = pl.multiple_of(lax.bitwise_xor(member, slot) * size, size)
        block = on[pl.ds(start, size), :]
        dest = (own_ref, send_ref)[slot % 2]
        dest[slot // 2 * size : (slot // 2 + 1) * size, :] = block


def attend(member, proj, taps):
    size = proj[0].shape[0]
    pairs = proj[0].shape[1] // (3 * LANES)
    length = 4 * size
    width = pairs * LANES
    return pl.pallas_call(
        attend_kernel,
        grid=(pairs,),
        in_specs=[SMEM_SPEC]
        + [pl.BlockSpec((size, 3 * LANES), lambda p: (0, p))] * 4
        + [pl.BlockSpec((1, 16, LANES), lambda p: (p, 0, 0))],
        out_specs=[
            pl.BlockSpec((length, 3 * LANES), lambda p: (0, p)),
            pl.BlockSpec((2 * size, LANES), lambda p: (0, p)),
            pl.BlockSpec((2 * size, LANES), lambda p: (0, p)),
            pl.BlockSpec((1, 2, length), lambda p: (p, 0, 0)),
        ],
        out_shape=[
            jax.ShapeDtypeStruct((length, 3 * width), BF16),
            jax.ShapeDtypeStruct((2 * size, width), BF16),
            jax.ShapeDtypeStruct((2 * size, width), BF16),
            jax.ShapeDtypeStruct((pairs, 2, length), F32),
        ],
        scratch_shapes=[
            pltpu.VMEM((3, 8 + length, LANES), F32),
            pltpu.VMEM((2, length, LANES), BF16),
            pltpu.VMEM((LANES, length), BF16),
            pltpu.VMEM((length, LANES), BF16),
            pltpu.VMEM((length, LANES), BF16),
        ],
        compiler_params=params(62),
        cost_estimate=CHEAP,
        name="attend",
    )(member, *proj, taps)


def attend_back_kernel(
    m_ref,
    p0,
    p1,
    p2,
    p3,
    mixed_ref,
    lse_ref,
    taps_ref,
    own_ref,
    send_ref,
    down_ref,
    drecv_ref,
    n0,
    n1,
    n2,
    n3,
    gown_ref,
    gsend_ref,
    gconv_ref,
    keep_ref,
    give_ref,
    pj,
    dm,
    qh,
    doh,
    kt,
    dl,
    dqa,
    nat,
    gp,
):
    member = m_ref[1]
    size = p0.shape[0]
    length = 4 * size
    scale = jnp.asarray(HEAD_DIM ** (-0.5), BF16)
    halves = [slice(0, size), slice(size, 2 * size)]
    load_natural(
        member,
        [own_ref[halves[0]], send_ref[halves[0]], own_ref[halves[1]], send_ref[halves[1]]],
        nat.at[0],
        size,
    )
    load_natural(
        member,
        [down_ref[halves[0]], drecv_ref[halves[0]], down_ref[halves[1]], drecv_ref[halves[1]]],
        nat.at[1],
        size,
    )
    grads = nat[1]
    product = (grads.astype(F32) * nat[0].astype(F32)).T
    for head in range(2):
        dl[head : head + 1, :] = jnp.sum(
            product[head * HEAD_DIM : (head + 1) * HEAD_DIM, :], axis=0, keepdims=True
        )
        doh[head] = only_head(grads, head)
        qh[head] = only_head(mixed_ref[:, 0:LANES], head) * scale
    kt[...] = mixed_ref[:, LANES : 2 * LANES].T
    for c in range(3):
        cols = slice(c * LANES, (c + 1) * LANES)
        pj[c, 0:8, :] = jnp.zeros((8, LANES), F32)
        dm[c, length : length + 8, :] = jnp.zeros((8, LANES), F32)
        load_natural(member, [p[:, cols] for p in (p0, p1, p2, p3)], pj.at[c], size, 8)
    for first in range(0, length, KBLOCK):
        keys = mixed_ref[first : first + KBLOCK, LANES : 2 * LANES]
        values = mixed_ref[first : first + KBLOCK, 2 * LANES : 3 * LANES]
        sum_v = None
        sum_k = None
        for head in range(2):
            scores = dot_nt(keys, qh[head, first:, :])
            key_pos = lax.broadcasted_iota(jnp.int32, (KBLOCK, KBLOCK), 0)
            query_pos = lax.broadcasted_iota(jnp.int32, (KBLOCK, KBLOCK), 1)
            corner = jnp.where(key_pos <= query_pos, scores[:, :KBLOCK], NEGATIVE)
            if first + KBLOCK < length:
                scores = jnp.concatenate([corner, scores[:, KBLOCK:]], axis=1)
            else:
                scores = corner
            probs = jnp.exp(scores - lse_ref[0, head : head + 1, first:])
            grad_probs = dot_nt(values, doh[head, first:, :])
            grad_scores = (probs * (grad_probs - dl[head : head + 1, first:])).astype(BF16)
            part_v = dot_nn(probs.astype(BF16), doh[head, first:, :])
            part_k = dot_nn(grad_scores, qh[head, first:, :])
            sum_v = part_v if sum_v is None else sum_v + part_v
            sum_k = part_k if sum_k is None else sum_k + part_k
            lanes = slice(head * HEAD_DIM, (head + 1) * HEAD_DIM)
            part_q = dot_nn(kt[lanes, first : first + KBLOCK], grad_scores)
            if first == 0:
                dqa[lanes, :] = part_q
            else:
                dqa[lanes, first:] += part_q
        dm[1, first : first + KBLOCK, :] = sum_k
        dm[2, first : first + KBLOCK, :] = sum_v
    dm[0, 0:length, :] = dqa[...].T * HEAD_DIM ** (-0.5)
    for c in range(3):
        grad = dm[c, 0:length, :]
        for s in range(3):
            gconv_ref[3 * c + s : 3 * c + s + 1, :] = jnp.sum(
                grad * pj[c, 8 - s : 8 - s + length, :], axis=0, keepdims=True
            )
        total = taps_ref[0, 3 * c : 3 * c + 1, :] * grad
        total = total + taps_ref[0, 3 * c + 1 : 3 * c + 2, :] * dm[c, 1 : 1 + length, :]
        total = total + taps_ref[0, 3 * c + 2 : 3 * c + 3, :] * dm[c, 2 : 2 + length, :]
        gp[:, c * LANES : (c + 1) * LANES] = total.astype(BF16)
    total = None
    for slot, norm in enumerate((n0, n1, n2, n3)):
        start = pl.multiple_of(lax.bitwise_xor(member, slot) * size, size)
        dest = (gown_ref, gsend_ref)[slot % 2]
        block = gp[pl.ds(start, size), :]
        dest[slot // 2 * size : (slot // 2 + 1) * size, :] = block
        part = dot_nn(norm[...], block)
        total = part if total is None else total + part
    rows = total.shape[0] // 8
    store_parts(
        m_ref[3],
        [
            [
                tile
                for b in (x, x + 4, x + 2, x + 6)
                for tile in lane_tiles(total[b * rows : (b + 1) * rows])
            ]
            for x in range(2)
        ],
        keep_ref,
        give_ref,
    )


def attend_back(pair, member, proj, mixed, lse, taps, own, send, grad_own, grad_recv, normed):
    size = proj[0].shape[0]
    length = 4 * size
    width = normed[0].shape[0]
    part = jax.ShapeDtypeStruct((2, 2, 3 * width // 8, LANES), BF16)
    half_spec = pl.BlockSpec((2 * size, LANES), lambda i: (0, pair))
    return pl.pallas_call(
        attend_back_kernel,
        grid=(1,),
        in_specs=[SMEM_SPEC]
        + [pl.BlockSpec((size, 3 * LANES), lambda i: (0, pair))] * 4
        + [
            pl.BlockSpec((length, 3 * LANES), lambda i: (0, pair)),
            pl.BlockSpec((1, 2, length), lambda i: (pair, 0, 0)),
            pl.BlockSpec((1, 16, LANES), lambda i: (pair, 0, 0)),
        ]
        + [half_spec] * 4
        + [pl.BlockSpec((width, size), lambda i: (0, 0))] * 4,
        out_specs=[
            pl.BlockSpec((2 * size, 3 * LANES), lambda i: (0, 0)),
            pl.BlockSpec((2 * size, 3 * LANES), lambda i: (0, 0)),
            pl.BlockSpec((16, LANES), lambda i: (0, 0)),
            pl.BlockSpec(part.shape, lambda i: (0, 0, 0, 0)),
            pl.BlockSpec(part.shape, lambda i: (0, 0, 0, 0)),
        ],
        out_shape=[
            jax.ShapeDtypeStruct((2 * size, 3 * LANES), BF16),
            jax.ShapeDtypeStruct((2 * size, 3 * LANES), BF16),
            jax.ShapeDtypeStruct((16, LANES), F32),
            part,
            part,
        ],
        scratch_shapes=[
            pltpu.VMEM((3, 8 + length, LANES), F32),
            pltpu.VMEM((3, 8 + length, LANES), F32),
            pltpu.VMEM((2, length, LANES), BF16),
            pltpu.VMEM((2, length, LANES), BF16),
            pltpu.VMEM((LANES, length), BF16),
            pltpu.VMEM((8, length), F32),
            pltpu.VMEM((LANES, length), F32),
            pltpu.VMEM((2, length, LANES), BF16),
            pltpu.VMEM((length, 3 * LANES), BF16),
        ],
        compiler_params=params(62),
        cost_estimate=CHEAP,
        name="attend_back",
    )(member, *proj, mixed, lse, taps, own, send, grad_own, grad_recv, *normed)


def canonical(flag, own_ref, recv_ref):
    own = own_ref[...]
    recv = recv_ref[...]
    return jnp.concatenate(
        [jnp.where(flag == 0, own, recv), jnp.where(flag == 0, recv, own)], axis=1
    )


def ffn_kernel(
    s_ref,
    hown_ref,
    hrecv_ref,
    wout_ref,
    tok0,
    tok1,
    cot0,
    cot1,
    gain_ref,
    bias_ref,
    up_ref,
    upb_ref,
    down_ref,
    downb_ref,
    out0,
    out1,
    down_keep,
    down_send,
    gres_ref,
    gown_ref,
    gsend_ref,
    sums_ref,
    up_keep,
    up_send,
    relus,
    res,
    nf,
    nft,
    gf,
    acc,
):
    step = pl.program_id(0)
    size = tok0.shape[0]
    core = s_ref[0]
    halves = ((0, s_ref[1] * size), (size, lax.bitwise_xor(s_ref[1], 2) * size))

    def valid(start):
        row = start + lax.broadcasted_iota(jnp.int32, tok0.shape, 0)
        return row < s_ref[2]

    def store(grad):
        rows = grad.shape[0] // 32
        store_parts(
            core,
            [
                [
                    tile
                    for place in range(16)
                    for chunk in [
                        bit
                        + (place >> 3 & 1) * 2
                        + (place >> 2 & 1) * 4
                        + (place >> 1 & 1) * 8
                        + (place & 1) * 16
                    ]
                    for tile in lane_tiles(grad[chunk * rows : (chunk + 1) * rows])
                ]
                for bit in range(2)
            ],
            up_keep,
            up_send,
        )

    @pl.when(step == 0)
    def _():
        attended = dot_nn(canonical(core, hown_ref, hrecv_ref), wout_ref[...])
        for tok, cot, (first, start) in zip((tok0, tok1), (cot0, cot1), halves):
            rows = slice(first, first + size)
            residual = tok[...].astype(F32) + attended[rows]
            res[rows, :] = residual
            scaled, _ = norm_stats(residual)
            nf[rows, :] = (scaled * gain_ref[...] + bias_ref[...]).astype(BF16)
            grad = cot[...]
            gf[rows, :] = jnp.where(valid(start), grad, jnp.zeros_like(grad))
        sums_ref[6:7, :] = jnp.sum(gf[...].astype(F32), axis=0, keepdims=True)
        sums_ref[7:8, :] = jnp.zeros_like(sums_ref[7:8, :])
        acc[...] = jnp.zeros_like(acc)

    @pl.when(step < 4)
    def _():
        relu = jnp.maximum(dot_nn(nf[...], up_ref[...]) + upb_ref[...], 0.0)
        relus[step] = relu
        act = (relu * relu).astype(BF16)
        acc[...] += dot_nn(act, down_ref[...])
        grad = dot_tn(act, gf[...])
        rows = grad.shape[0] // 8
        store_parts(
            core,
            [
                [
                    tile
                    for chunk in (bit, bit + 4, bit + 2, bit + 6)
                    for tile in lane_tiles(grad[chunk * rows : (chunk + 1) * rows])
                ]
                for bit in range(2)
            ],
            down_keep,
            down_send,
        )

    @pl.when(step == 3)
    def _():
        for out, (first, start) in zip((out0, out1), halves):
            rows = slice(first, first + size)
            total = res[rows, :] + (acc[rows, :] + downb_ref[...])
            out[...] = jnp.where(valid(start), total, 0.0).astype(BF16).reshape(out.shape)
        nft[...] = nf[...].T
        acc[...] = jnp.zeros_like(acc)

    @pl.when((step >= 4) & (step < 8))
    def _():
        grad_act = dot_nt(gf[...], down_ref[...])
        grad_pre = (2.0 * relus[step - 4] * grad_act).astype(BF16)
        sums_ref[pl.ds(step - 4, 1), :] = jnp.sum(grad_pre.astype(F32), axis=0, keepdims=True)
        acc[...] += dot_nt(grad_pre, up_ref[...])
        store(dot_nn(nft[...], grad_pre))

    @pl.when(step == 8)
    def _():
        scaled, inv_std = norm_stats(res[...])
        grad = acc[...]
        sums_ref[4:5, :] = jnp.sum(grad * scaled, axis=0, keepdims=True)
        sums_ref[5:6, :] = jnp.sum(grad, axis=0, keepdims=True)
        total = gf[...].astype(F32) + norm_backward(grad, gain_ref[...], scaled, inv_std)
        gres_ref[...] = total
        attended = total.astype(BF16)
        heads = dot_nt(attended, wout_ref[...]).astype(BF16)
        middle = heads.shape[1] // 2
        gown_ref[...] = jnp.where(core == 0, heads[:, :middle], heads[:, middle:])
        gsend_ref[...] = jnp.where(core == 0, heads[:, middle:], heads[:, :middle])
        store(dot_tn(canonical(core, hown_ref, hrecv_ref), attended))


def ffn(scalars, hown, hrecv, wout, toks, cots, gain, bias, up, upb, down, downb):
    rows = 2 * toks[0].shape[0]
    width, ff = up.shape
    tile = ff // 4
    assert tile == width
    down_part = jax.ShapeDtypeStruct((2, 2, 2, 2, tile // 8 * width // LANES, LANES), BF16)
    block = width // 32 * tile // LANES
    up_part = jax.ShapeDtypeStruct((2, 2, 2, 2, 5 * block, LANES), BF16)

    def forward(j):
        return jnp.minimum(j, 3)

    def backward(j):
        return jnp.maximum(j - 4, 0)

    def either(j):
        return jnp.where(j < 4, j, jnp.minimum(j - 4, 3))

    down_spec = pl.BlockSpec(
        (2, 2, 1, 1) + down_part.shape[4:],
        lambda j, _: (0, 0, lax.rem(forward(j), 2), lax.div(forward(j), 2), 0, 0),
    )
    up_spec = pl.BlockSpec((2, 2, 2, 2, block, LANES), lambda j, _: (0, 0, 0, 0, backward(j), 0))
    token_block = jax.ShapeDtypeStruct(toks[0].shape, BF16)
    half = jax.ShapeDtypeStruct(hown.shape, BF16)
    return pl.pallas_call(
        ffn_kernel,
        grid_spec=pltpu.PrefetchScalarGridSpec(
            num_scalar_prefetch=1,
            grid=(9,),
            in_specs=[still(a) for a in (hown, hrecv, wout, *toks, *cots, gain, bias)]
            + [
                pl.BlockSpec((width, tile), lambda j, _: (0, either(j))),
                pl.BlockSpec((1, tile), lambda j, _: (0, forward(j))),
                pl.BlockSpec((tile, width), lambda j, _: (either(j), 0)),
                still(downb),
            ],
            out_specs=[
                once((1,) + token_block.shape, lambda j, s: (s[4], 0, 0)),
                once(token_block.shape, lambda j, _: (0, 0)),
                down_spec,
                down_spec,
                once((rows, width), lambda j, _: (0, 0)),
                once(half.shape, lambda j, _: (0, 0)),
                once(half.shape, lambda j, _: (0, 0)),
                pl.BlockSpec((8, width), lambda j, _: (0, 0)),
                up_spec,
                up_spec,
            ],
            scratch_shapes=[
                pltpu.VMEM((4, rows, tile), F32),
                pltpu.VMEM((rows, width), F32),
                pltpu.VMEM((rows, width), BF16),
                pltpu.VMEM((width, rows), BF16),
                pltpu.VMEM((rows, width), BF16),
                pltpu.VMEM((rows, width), F32),
            ],
        ),
        out_shape=[
            jax.ShapeDtypeStruct((2,) + token_block.shape, BF16),
            token_block,
            down_part,
            down_part,
            jax.ShapeDtypeStruct((rows, width), F32),
            half,
            half,
            jax.ShapeDtypeStruct((8, width), F32),
            up_part,
            up_part,
        ],
        compiler_params=params(63),
        cost_estimate=CHEAP,
        name="ffn",
    )(scalars, hown, hrecv, wout, *toks, *cots, gain, bias, up, upb, down, downb)


def input_grad_kernel(
    final, s_ref, o0, o1, o2, r0, r1, r2, w_ref, x_ref, gres_ref, gain_ref, *refs
):
    out_ref, sums_ref, buf = refs[-3:]
    for n, ref in enumerate((o0, o1, o2, r0, r1, r2)):
        side = s_ref[0] if n < 3 else 1 - s_ref[0]
        start = pl.multiple_of((side * 3 + n % 3) * LANES, LANES)
        for c, tile in enumerate(lane_tiles(ref[...])):
            buf[c, :, pl.ds(start, LANES)] = tile
    grad = dot_nt(buf[0], w_ref[0]) + dot_nt(buf[1], w_ref[1]) + dot_nt(buf[2], w_ref[2])
    scaled, inv_std = norm_stats(x_ref[...].astype(F32))
    first = 17 if final else 0

    @pl.when(pl.program_id(0) == 0)
    def _():
        sums_ref[...] = jnp.zeros_like(sums_ref)
        if final:
            early_ref, before_ref, *convs = refs[:-3]
            sums_ref[0:8, :] = early_ref[...]
            sums_ref[first : first + 2, :] = before_ref[0:2, :]
            for n, conv in enumerate(convs):
                start = pl.multiple_of((s_ref[0] * 3 + n) * LANES, LANES)
                sums_ref[8:17, pl.ds(start, LANES)] = conv[0:9, :]

    sums_ref[first : first + 1, :] += jnp.sum(grad * scaled, axis=0, keepdims=True)
    sums_ref[first + 1 : first + 2, :] += jnp.sum(grad, axis=0, keepdims=True)
    total = gres_ref[...] + norm_backward(grad, gain_ref[...], scaled, inv_std)
    out_ref[...] = total.astype(BF16).reshape(out_ref.shape)


def input_grad(slot, scalars, owns, recvs, weights, x, grad_residual, gain, small=()):
    rows, width = x.shape
    tile = rows // 2
    final = len(small) > 0
    part = pl.BlockSpec((tile, 3 * LANES), lambda i, _: (2 * slot + i, 0))
    if final:
        out_spec = pl.BlockSpec((1, tile, width), lambda i, s: (s[4], i, 0))
        out = jax.ShapeDtypeStruct((2, rows, width), BF16)
    else:
        out_spec = pl.BlockSpec((tile, width), lambda i, _: (i, 0))
        out = jax.ShapeDtypeStruct((rows, width), BF16)
    sums = jax.ShapeDtypeStruct((24 if final else 8, width), F32)
    return pl.pallas_call(
        functools.partial(input_grad_kernel, final),
        grid_spec=pltpu.PrefetchScalarGridSpec(
            num_scalar_prefetch=1,
            grid=(2,),
            in_specs=[part] * 6
            + [
                still(weights),
                pl.BlockSpec((tile, width), lambda i, _: (i, 0)),
                pl.BlockSpec((tile, width), lambda i, _: (2 * slot + i, 0)),
                still(gain),
            ]
            + [still(a) for a in small],
            out_specs=[out_spec, pl.BlockSpec(sums.shape, lambda i, _: (0, 0))],
            scratch_shapes=[pltpu.VMEM((3, tile, width), BF16)],
        ),
        out_shape=[out, sums],
        compiler_params=params(62),
        cost_estimate=CHEAP,
        name="input_grad",
    )(scalars, *owns, *recvs, weights, x, grad_residual, gain, *small)


FREE, ONE, MINE, OTHER = range(4)
BIT_AT = (4, 3, 5, 6)


class Segment:
    def __init__(self, arrays, first, rows):
        self.rows = rows
        self.parts = [(array, self.fresh(array), first) for array in arrays]

    @staticmethod
    def fresh(array):
        return [FREE if n == 2 else ONE for n in array.shape[:4]]

    def chosen(self, dim):
        found = []
        for array, marks, first in self.parts:
            marks = list(marks)
            if dim is not None and marks[dim] == FREE:
                marks[dim] = OTHER
            found.append((array, tuple(marks), first, self.rows))
        return found

    def settle(self, dim, arrived, first):
        parts = []
        for array, marks, own_first in self.parts:
            marks = list(marks)
            if marks[dim] == FREE:
                marks[dim] = MINE
            parts.append((array, marks, own_first))
        self.parts = parts + [(arrived, self.fresh(arrived), first)]


def settle(segments, dim, arrived):
    first = 0
    for segment in segments:
        segment.settle(dim, arrived, first)
        first += segment.rows


def sum_kernel(plan, finish, count, s_ref, *refs):
    pieces = [p for parts in plan for p in parts]
    arrays, outs = refs[:count], refs[count : len(refs) - len(pieces) - 1]
    bufs, sems = refs[len(refs) - len(pieces) - 1 : -1], refs[-1]
    copies = []
    for n, (place, marks, first, rows) in enumerate(pieces):
        where = []
        for dim, mark in enumerate(marks):
            bit = s_ref[BIT_AT[dim]]
            start = {FREE: 0, ONE: 0, MINE: bit, OTHER: 1 - bit}[mark]
            where.append(pl.ds(start, 2 if mark == FREE else 1))
        source = arrays[place].at[tuple(where) + (pl.ds(first, rows), slice(None))]
        copies.append(pltpu.make_async_copy(source, bufs[n], sems.at[n]))
        copies[-1].start()
    n = 0
    totals = []
    for parts in plan:
        for copy in copies[n : n + len(parts)]:
            copy.wait()
        own = bufs[n : n + len(parts)]
        n += len(parts)

        def total(lead, rows, own=own):
            value = None
            for buf in own:
                piece = buf[lead + (rows, slice(None))].astype(F32)
                value = piece if value is None else value + piece
            return value

        totals.append(total)
    finish(s_ref, totals, outs)


def sum_call(scalars, segments, dims, finish, out_shape, name):
    arrays, plan, scratch = [], [], []
    for segment, dim in zip(segments, dims):
        parts = []
        for array, marks, first, rows in segment.chosen(dim):
            place = next((n for n, a in enumerate(arrays) if a is array), None)
            if place is None:
                place = len(arrays)
                arrays.append(array)
            parts.append((place, marks, first, rows))
            sizes = tuple(2 if mark == FREE else 1 for mark in marks)
            scratch.append(pltpu.VMEM(sizes + (rows, LANES), BF16))
        plan.append(parts)
    whole = lambda shape: pl.BlockSpec(shape, lambda i: (0,) * len(shape))
    return pl.pallas_call(
        functools.partial(sum_kernel, plan, finish, len(arrays)),
        grid=(1,),
        in_specs=[SMEM_SPEC] + [pl.BlockSpec(memory_space=pltpu.HBM)] * len(arrays),
        out_specs=[whole(o.shape) for o in out_shape],
        out_shape=out_shape,
        scratch_shapes=scratch + [pltpu.SemaphoreType.DMA((len(scratch),))],
        compiler_params=params(62),
        cost_estimate=CHEAP,
        name=name,
    )(scalars, *arrays)


def outgoing(scalars, groups, dims, name="stage_sum"):
    shapes = []
    for group, dim in zip(groups, dims):
        marks = [group[0].chosen(dim)[0][1]]
        sizes = tuple(2 if mark == FREE else 1 for mark in marks[0])
        shapes.append(jax.ShapeDtypeStruct(sizes + (sum(g.rows for g in group), LANES), BF16))

    def finish(s_ref, totals, outs):
        n = 0
        for group, out in zip(groups, outs):
            first = 0
            for segment in group:
                for lead in itertools.product(*[range(size) for size in out.shape[:4]]):
                    for row in range(0, segment.rows, 48):
                        value = totals[n](lead, slice(row, row + 48))
                        out[lead + (slice(first + row, first + row + 48), slice(None))] = (
                            value.astype(BF16)
                        )
                first += segment.rows
                n += 1

    segments = [segment for group in groups for segment in group]
    each = [dim for group, dim in zip(groups, dims) for _ in group]
    return sum_call(scalars, segments, each, finish, shapes, name)


def hop(value, stage):
    return lax.ppermute(value, stage[0], stage[1])


def ffn_plain(heads, toks, cot, valid, wout, gain, bias, up, upb, down, downb):
    residual = toks.astype(F32) + jnp.dot(heads, wout, preferred_element_type=F32)
    scaled, inv_std = norm_stats(residual)
    normed = (scaled * gain + bias).astype(BF16)
    relu = jnp.maximum(jnp.dot(normed, up, preferred_element_type=F32) + upb, 0.0)
    act = jnp.square(relu).astype(BF16)
    out = jnp.dot(act, down, preferred_element_type=F32) + downb
    result = jnp.where(valid, residual + out, 0.0).astype(BF16)
    grad_ffn = jnp.where(valid, cot, jnp.zeros_like(cot))
    grad_y = grad_ffn.astype(F32)
    grad_act = jnp.einsum("td,fd->tf", grad_ffn, down, preferred_element_type=F32)
    grad_pre = (2.0 * relu * grad_act).astype(BF16)
    grad = jnp.einsum("tf,df->td", grad_pre, up, preferred_element_type=F32)
    sums = jnp.stack([jnp.sum(grad * scaled, axis=0), jnp.sum(grad, axis=0)])
    grad_residual = grad_y + norm_backward(grad, gain, scaled, inv_std)
    attended = grad_residual.astype(BF16)
    grad_heads = jnp.einsum("td,ed->te", attended, wout, preferred_element_type=F32)
    return (
        result,
        grad_residual,
        grad_heads.astype(BF16),
        sums,
        jnp.sum(grad_pre.astype(F32), axis=0),
        jnp.sum(grad_y, axis=0),
        jnp.einsum("td,tf->df", normed, grad_pre, preferred_element_type=F32),
        jnp.einsum("tf,td->fd", act, grad_ffn, preferred_element_type=F32),
        jnp.einsum("te,td->ed", heads, attended, preferred_element_type=F32),
    )


def on_device(
    tokens,
    cotangent,
    lengths,
    pre_attn_gain,
    pre_attn_bias,
    qkv_weight,
    conv_weight,
    out_weight,
    pre_ffn_gain,
    pre_ffn_bias,
    up_weight,
    up_bias,
    down_weight,
    down_bias,
):
    groups = lax.axis_size("mp")
    batch_groups = lax.axis_size("batch")
    devices = groups * batch_groups
    member = lax.axis_index("mp").astype(jnp.int32)
    batch = lax.axis_index("batch").astype(jnp.int32)
    seqs, rows, width = tokens.shape
    ff = up_weight.shape[1]
    middle = width // 2
    quarter = width // groups
    pairs = middle // LANES
    taps = conv_weight.shape[1]
    assert groups == 4 and seqs == 2 and pairs == 3 and taps == 3
    fast = batch_groups == 8 and (width // devices) % 8 == 0
    half = lax.shift_right_logical(member, 1)
    core = lax.bitwise_and(member, 1)
    x_bit = lax.bitwise_and(batch, 1)
    z0_bit = lax.bitwise_and(lax.shift_right_logical(batch, 1), 1)
    z1_bit = lax.shift_right_logical(batch, 2)
    gain_attn = pre_attn_gain.astype(F32).reshape(1, width)
    bias_attn = pre_attn_bias.astype(F32).reshape(1, width)
    gain_ffn = pre_ffn_gain.astype(F32).reshape(1, width)
    bias_ffn = pre_ffn_bias.astype(F32).reshape(1, width)
    up_bias_f = up_bias.astype(F32).reshape(1, ff)
    down_bias_f = down_bias.astype(F32).reshape(1, width)

    def swap_core(value):
        return lax.ppermute(value, "mp", CORE)

    def swap_pair(value):
        return lax.ppermute(value, "mp", PAIR)

    def pick(value, index):
        starts = (index,) + (jnp.int32(0),) * (value.ndim - 1)
        return lax.dynamic_slice(value, starts, (1,) + value.shape[1:])[0]

    length = pick(lengths, half)
    scalars = jnp.stack([core, member, length, x_bit, half, z0_bit, z1_bit]).astype(jnp.int32)

    hops = [("mp", PAIR)] + [
        ("batch", [(i, i ^ flip) for i in range(batch_groups)]) for flip in (1, 2, 4)
    ]
    DY, DX, DZ0, DZ1 = range(4)
    tie = lax.optimization_barrier

    tok_pair = swap_pair(pick(tokens, 1 - half))
    tok_own = pick(tokens, half)
    cot_own = pick(cotangent, half)
    tok_core = swap_core(tok_own)
    taps_own = lax.dynamic_slice_in_dim(conv_weight, core * middle, middle, 2).astype(F32)
    taps_own = taps_own.reshape(3 * taps, pairs, LANES).transpose(1, 0, 2)
    taps_own = jnp.pad(taps_own, ((0, 0), (0, 16 - 3 * taps), (0, 0)))

    def norm_project(block):
        return project(scalars, block, gain_attn, bias_attn, qkv_weight)

    first = norm_project(tok_own)
    prepared = (cot_own, pick(cotangent, 1 - half), taps_own, gain_ffn, bias_ffn, up_bias_f, down_bias_f)
    tok_core, prepared = tie((tok_core, prepared))
    cot_own, cot_send, taps_own, gain_ffn, bias_ffn, up_bias_f, down_bias_f = prepared
    second = norm_project(tok_core)
    tok_pair, first, second = tie((tok_pair, first, second))
    tok_cross = swap_core(tok_pair)
    third = norm_project(tok_pair)
    tok_cross, third = tie((tok_cross, third))
    fourth = norm_project(tok_cross)
    cot_send, fourth = tie((cot_send, fourth))
    cot_pair = swap_pair(cot_send)
    normed, proj = zip(first, second, third, fourth)
    mixed, heads_own, heads_send, lse = attend(scalars, proj, taps_own)
    heads_recv = swap_core(heads_send)

    if fast:
        (
            result_all,
            result_give,
            down_keep,
            down_send,
            grad_residual,
            grad_own,
            grad_send,
            early,
            up_keep,
            up_send,
        ) = ffn(
            scalars,
            heads_own,
            heads_recv,
            out_weight,
            (tok_own, tok_pair),
            (cot_own, cot_pair),
            gain_ffn,
            bias_ffn,
            up_weight,
            up_bias_f,
            down_weight,
            down_bias_f,
        )
    else:
        row = jnp.arange(rows, dtype=jnp.int32)
        row_pos = [member * rows + row, jnp.bitwise_xor(member, 2) * rows + row]
        heads_all = jnp.concatenate(
            [
                jnp.where(core == 0, heads_own, heads_recv),
                jnp.where(core == 0, heads_recv, heads_own),
            ],
            axis=1,
        )
        (
            result,
            grad_residual,
            grad_heads,
            sums_ffn,
            sums_up,
            sums_down,
            grad_up,
            grad_down,
            grad_out,
        ) = ffn_plain(
            heads_all,
            jnp.concatenate([tok_own, tok_pair], axis=0),
            jnp.concatenate([cot_own, cot_pair], axis=0),
            (jnp.concatenate(row_pos) < length)[:, None],
            out_weight,
            gain_ffn,
            bias_ffn,
            up_weight,
            up_bias_f,
            down_weight,
            down_bias_f,
        )
        result_all, result_give = jnp.stack([result[:rows]] * 2), result[rows:]
        early = [sums_up.reshape(ff // width, width), sums_ffn, sums_down[None]]
        early = jnp.concatenate(early + [jnp.zeros((1, width), F32)], axis=0)
        grad_own = lax.dynamic_slice_in_dim(grad_heads, core * middle, middle, 1)
        grad_send = lax.dynamic_slice_in_dim(grad_heads, (1 - core) * middle, middle, 1)
    grad_recv = swap_core(grad_send)
    if fast:
        down_recv = swap_core(down_send)
        grad_recv, down_recv, up_send = tie((grad_recv, down_recv, up_send))
        up_recv = swap_core(up_send)
        down_rows = down_keep.shape[4]
        up_rows = up_keep.shape[4]
        each = (down_rows + up_rows) // 3
        down = (down_keep, down_recv)
        up = (up_keep, up_recv)
        rest = down_rows - each
        down_a, down_b = Segment(down, 0, each), Segment(down, each, rest)
        up_a, up_b = Segment(up, 0, each - rest), Segment(up, each - rest, each)
        group_1, group_2, group_3 = [down_a], [down_b, up_a], [up_b]

        def stage(dims, groups=(group_1, group_2, group_3)):
            return outgoing(scalars, groups, dims)

        def arrive(dims, sent, groups=(group_1, group_2, group_3)):
            for group, dim, value in zip(groups, dims, sent):
                settle(group, dim, value)

        dims = (DX, DZ0, DY)
        sent = stage(dims[:1], (group_1,))
        sent, grad_recv, up_recv = tie((sent, grad_recv, up_recv))
        up_a.parts[1] = (up_recv,) + up_a.parts[1][1:]
        up_b.parts[1] = (up_recv,) + up_b.parts[1][1:]
        sent = list(sent) + list(stage(dims[1:], (group_2, group_3)))
        grad_own, grad_recv, sent = tie((grad_own, grad_recv, sent))
        sent = [hop(v, hops[d]) for v, d in zip(sent, dims)]
        arrive(dims, sent)

    def backward(pair, grad_recv):
        own, send, conv, keep, give = attend_back(
            pair,
            scalars,
            proj,
            mixed,
            lse,
            taps_own,
            heads_own,
            heads_send,
            grad_own,
            grad_recv,
            normed,
        )
        keep = keep.reshape((1, 1) + keep.shape)
        give = give.reshape((1, 1) + give.shape)
        return own, send, conv, keep, give

    qkv_rows = 3 * width // 8
    own_0, send_0, conv_0, keep_0, give_0 = backward(0, grad_recv)
    if fast:
        dims = (DY, DZ1, DX)
        sent = stage(dims)
        grad_recv, own_0, send_0, give_0, sent = tie((grad_recv, own_0, send_0, give_0, sent))
        sent = [hop(v, hops[d]) for v, d in zip(sent, dims)]
        arrive(dims, sent)
        qkv_0 = Segment((keep_0, hop(give_0, hops[DX])), 0, qkv_rows)
        group_1.append(qkv_0)
    recv_0 = swap_core(send_0)
    own_1, send_1, conv_1, keep_1, give_1 = backward(1, grad_recv)
    if fast:
        dims = (DZ0, DX, DZ1)
        sent = stage(dims)
        grad_recv, own_1, send_1, give_1, recv_0, result_give, sent = tie(
            (grad_recv, own_1, send_1, give_1, recv_0, result_give, sent)
        )
        sent = [hop(v, hops[d]) for v, d in zip(sent, dims)]
    result_back = swap_pair(result_give)
    recv_1 = swap_core(send_1)
    own_2, send_2, conv_2, keep_2, give_2 = backward(2, grad_recv)
    if fast:
        own_2, send_2, give_1, give_2, recv_1, result_back, sent = tie(
            (own_2, send_2, give_1, give_2, recv_1, result_back, sent)
        )
        arrive(dims, sent)
        give_1 = hop(give_1, hops[DX])
        give_2 = hop(give_2, hops[DX])
    recv_2 = swap_core(send_2)
    if fast:
        dims = (DZ1, DY, DZ0)
        sent = stage(dims)
        recv_2, sent = tie((recv_2, sent))
        ffn_waiting = [hop(v, hops[d]) for v, d in zip(sent, dims)]
    g_own = (own_0, own_1, own_2)
    g_send = (send_0, send_1, send_2)
    g_recv = (recv_0, recv_1, recv_2)
    g_conv = (conv_0, conv_1, conv_2)
    grad_in_pair, sums_pair = input_grad(
        1, scalars, g_own, g_recv, qkv_weight, tok_pair, grad_residual, gain_attn
    )
    grad_in_back = swap_pair(grad_in_pair)
    tok_last = tok_own
    if fast:
        give_1, give_2, sums_pair = tie((give_1, give_2, sums_pair))
        qkv_1 = Segment((keep_1, give_1), 0, qkv_rows)
        qkv_2 = Segment((keep_2, give_2), 0, qkv_rows)
        (sent,) = outgoing(scalars, [[qkv_1, qkv_2]], [DZ0])
        tok_last, sums_pair, sent = tie((tok_own, sums_pair, sent))
        waiting = hop(sent, hops[DZ0])
    tokens_grad, small = input_grad(
        0,
        scalars,
        g_own,
        g_recv,
        qkv_weight,
        tok_last,
        grad_residual,
        gain_attn,
        (early, sums_pair) + g_conv,
    )

    def place(both, other):
        return lax.dynamic_update_slice(both, other[None], (1 - half, 0, 0))

    result_all = place(result_all, result_back)
    index = batch * groups + member
    share = width // devices
    part = width // batch_groups

    if not fast:
        axes = ("batch", "mp")
        grad_qkv = 0.0
        for n, (norm, slot) in enumerate(zip(normed, (0, 0, 1, 1))):
            source = (g_own, g_send)[n % 2]
            grads = jnp.concatenate([g[slot * rows : (slot + 1) * rows] for g in source], axis=1)
            grad_qkv = grad_qkv + jnp.einsum("dt,te->de", norm, grads, preferred_element_type=F32)
        grad_qkv = grad_qkv.reshape(width, pairs, 3, LANES).transpose(2, 0, 1, 3)
        qkv_full = lax.dynamic_update_slice_in_dim(
            jnp.zeros((3, width, width), F32), grad_qkv.reshape(3, width, middle), core * middle, 2
        )
        qkv_flat = qkv_full.reshape(3, batch_groups, part, groups, quarter)
        qkv_flat = qkv_flat.transpose(1, 3, 0, 2, 4).reshape(devices * 3 * part, quarter)

        def scatter(value):
            return lax.psum_scatter(value, axes, scatter_dimension=0, tiled=True)

        small = lax.psum(small, axes)
        qkv_out = scatter(qkv_flat).reshape(3, part, quarter)
        up_out, down_out, out_out = scatter(grad_up), scatter(grad_down), scatter(grad_out)
    else:
        small = small + hop(small, ("mp", CORE))
        small, waiting = tie((small, waiting))
        settle([qkv_1, qkv_2], DZ0, waiting)
        (sent,) = outgoing(scalars, [[qkv_1, qkv_2]], [DZ1])
        sent = hop(sent, hops[DZ1])
        small = small + hop(small, hops[DX])
        small, ffn_waiting = tie((small, ffn_waiting))
        arrive((DZ1, DY, DZ0), ffn_waiting)
        small = small + hop(small, hops[DZ0])
        small, sent, grad_in_back = tie((small, sent, grad_in_back))
        settle([qkv_1, qkv_2], DZ1, sent)
        small = small + hop(small, hops[DZ1])
        small = small + hop(small, hops[DY])

        def finish_ffn(s_ref, totals, outs):
            whole = [total((0,) * 4, slice(None)) for total in totals]
            downs = jnp.concatenate(whole[0:2], axis=0)
            ups = jnp.concatenate(whole[2:4], axis=0)
            down_out, up_out, out_out = outs
            for out, values in ((down_out, downs), (up_out, ups), (out_out, ups[down_rows:])):
                size, cols = out.shape
                for n in range(cols // LANES):
                    out[:, n * LANES : (n + 1) * LANES] = values[n * size : (n + 1) * size]

        down_out, up_out, out_out = sum_call(
            scalars,
            [down_a, down_b, up_a, up_b],
            [None] * 4,
            finish_ffn,
            [
                jax.ShapeDtypeStruct((ff // devices, width), F32),
                jax.ShapeDtypeStruct((share, ff), F32),
                jax.ShapeDtypeStruct((share, width), F32),
            ],
            "ffn_sum",
        )

        def finish_qkv(s_ref, totals, outs):
            first, middle, last = [total((0,) * 4, slice(None)) for total in totals]
            lower = jnp.concatenate([first, middle[:, :HEAD_DIM]], axis=1)
            upper = jnp.concatenate([middle[:, HEAD_DIM:], last], axis=1)
            outs[0][...] = jnp.where(s_ref[0] == 0, lower, upper)
            outs[1][...] = jnp.where(s_ref[4] == 0, upper, lower).astype(BF16)
            outs[2][...] = jnp.where(s_ref[4] == 0, lower, upper).astype(BF16)

        keep, straight, crossed = sum_call(
            scalars,
            [qkv_0, qkv_1, qkv_2],
            [None] * 3,
            finish_qkv,
            [jax.ShapeDtypeStruct((qkv_rows, quarter), t) for t in (F32, BF16, BF16)],
            "qkv_sum",
        )
        straight = lax.ppermute(straight, "mp", [(2, 0), (0, 1), (3, 2), (1, 3)])
        crossed = lax.ppermute(crossed, "mp", [(2, 1), (1, 2)])
        qkv_out = straight.astype(F32) + jnp.where(half == core, keep, crossed.astype(F32))
        qkv_out = qkv_out.reshape(3, part, quarter)

    tokens_grad = place(tokens_grad, grad_in_back)
    up_bias_out = pick(small[: ff // width].reshape(devices, ff // devices), index)
    mine = pick(small.reshape(24, devices, share).transpose(1, 0, 2), index)
    return (
        result_all,
        tokens_grad,
        mine[17],
        mine[18],
        qkv_out,
        mine[8:17].reshape(3, taps, share),
        out_out,
        mine[4],
        mine[5],
        up_out,
        up_bias_out,
        down_out,
        mine[6],
    )


def solution(mesh):
    in_specs = (
        P("batch", "mp", None),
        P("batch", "mp", None),
        P("batch"),
    ) + (P(),) * 11
    out_specs = (
        P("batch", "mp", None),
        P("batch", "mp", None),
        P(("batch", "mp")),
        P(("batch", "mp")),
        P(None, "batch", "mp"),
        P(None, None, ("batch", "mp")),
        P(("batch", "mp"), None),
        P(("batch", "mp")),
        P(("batch", "mp")),
        P(("batch", "mp"), None),
        P(("batch", "mp")),
        P(("batch", "mp"), None),
        P(("batch", "mp")),
    )
    return jax.shard_map(
        on_device, mesh=mesh, in_specs=in_specs, out_specs=out_specs, check_vma=False
    )
```

```python
import functools
import itertools

import jax
import jax.numpy as jnp
from jax import lax
from jax.experimental import pallas as pl
from jax.experimental.pallas import tpu as pltpu
from jax.sharding import PartitionSpec as P

HEAD_DIM = 64
LANES = 128
EPSILON = 1e-05
NEGATIVE = -1000000000.0
QBLOCK = 512
KBLOCK = 256
F32 = jnp.float32
BF16 = jnp.bfloat16

CORE = [(i, i ^ 1) for i in range(4)]
PAIR = [(i, i ^ 2) for i in range(4)]


def dot_nt(left, right):
    return lax.dot_general(left, right, (((1,), (1,)), ((), ())), preferred_element_type=F32)


def dot_nn(left, right):
    return lax.dot_general(left, right, (((1,), (0,)), ((), ())), preferred_element_type=F32)


def dot_tn(left, right):
    return lax.dot_general(left, right, (((0,), (0,)), ((), ())), preferred_element_type=F32)


def params(mib):
    return pltpu.CompilerParams(vmem_limit_bytes=mib << 20)


def lane_tiles(values):
    return [values[:, n : n + LANES] for n in range(0, values.shape[1], LANES)]


def once(shape, index_map):
    return pl.BlockSpec(shape, index_map, pipeline_mode=pl.Buffered(1))


def still(array):
    return once(array.shape, lambda *_: (0,) * array.ndim)


CHEAP = pl.CostEstimate(flops=1 << 20, bytes_accessed=1 << 16, transcendentals=0)
SMEM_SPEC = pl.BlockSpec(memory_space=pltpu.SMEM)


def norm_stats(values):
    center = values - jnp.mean(values, axis=-1, keepdims=True)
    inv_std = lax.rsqrt(jnp.mean(center * center, axis=-1, keepdims=True) + EPSILON)
    return center * inv_std, inv_std


def norm_backward(grad_out, norm_gain, scaled, inv_std):
    weighted = grad_out * norm_gain
    return inv_std * (
        weighted
        - jnp.mean(weighted, axis=-1, keepdims=True)
        - scaled * jnp.mean(weighted * scaled, axis=-1, keepdims=True)
    )


def project_kernel(s_ref, x_ref, vec_ref, w_ref, normed_ref, proj_ref):
    scaled, _ = norm_stats(x_ref[...].astype(F32))
    normed = (scaled * vec_ref[0:1, :] + vec_ref[1:2, :]).astype(BF16)
    normed_ref[...] = normed.T
    for c in range(3):
        part = dot_nn(normed, w_ref[c]).astype(BF16)
        for n, tile in enumerate(lane_tiles(part)):
            start = (3 * n + c) * LANES
            proj_ref[:, start : start + LANES] = tile


def project(scalars, x, vectors, weights):
    rows, width = x.shape
    cols = 3 * width // 2
    return pl.pallas_call(
        project_kernel,
        grid_spec=pltpu.PrefetchScalarGridSpec(
            num_scalar_prefetch=1,
            grid=(1,),
            in_specs=[
                once((rows, width), lambda i, s: (0, 0)),
                still(vectors),
                once((3, width, width // 2), lambda i, s: (0, 0, s[0])),
            ],
            out_specs=[
                once((width, rows), lambda i, s: (0, 0)),
                once((rows, cols), lambda i, s: (0, 0)),
            ],
        ),
        out_shape=[
            jax.ShapeDtypeStruct((width, rows), BF16),
            jax.ShapeDtypeStruct((rows, cols), BF16),
        ],
        compiler_params=params(62),
        cost_estimate=CHEAP,
        name="project",
    )(scalars, x, vectors, weights)


def store_parts(flag, parts, keep_ref, send_ref):
    first = jnp.concatenate(parts[0], axis=0).astype(BF16)
    second = jnp.concatenate(parts[1], axis=0).astype(BF16)
    keep_ref[...] = jnp.where(flag == 0, first, second).reshape(keep_ref.shape)
    send_ref[...] = jnp.where(flag == 0, second, first).reshape(send_ref.shape)


def only_head(values, head):
    lane = lax.broadcasted_iota(jnp.int32, values.shape, 1)
    return jnp.where((lane // HEAD_DIM) == head, values, jnp.zeros_like(values))


def load_natural(member, blocks, dest, size, shift=0):
    for slot, block in enumerate(blocks):
        start = pl.multiple_of(lax.bitwise_xor(member, slot) * size, 8) + shift
        start = pl.multiple_of(start, 8)
        dest[pl.ds(start, size), :] = block.astype(dest.dtype)


def attend_kernel(
    m_ref, p0, p1, p2, p3, taps_ref, mixed_ref, own_ref, send_ref, lse_ref, pj, kh, vt, on, qs
):
    member = m_ref[1]
    size = p0.shape[0]
    length = 4 * size
    scale = jnp.asarray(HEAD_DIM ** (-0.5), BF16)
    for c in range(3):
        cols = slice(c * LANES, (c + 1) * LANES)
        pj[c, 0:8, :] = jnp.zeros((8, LANES), F32)
        load_natural(member, [p[:, cols] for p in (p0, p1, p2, p3)], pj.at[c], size, 8)
    for c in range(3):
        total = taps_ref[0, 3 * c : 3 * c + 1, :] * pj[c, 8 : 8 + length, :]
        total = total + taps_ref[0, 3 * c + 1 : 3 * c + 2, :] * pj[c, 7 : 7 + length, :]
        total = total + taps_ref[0, 3 * c + 2 : 3 * c + 3, :] * pj[c, 6 : 6 + length, :]
        mixed = total.astype(BF16)
        mixed_ref[:, c * LANES : (c + 1) * LANES] = mixed
        if c == 0:
            qs[...] = mixed * scale
        elif c == 1:
            kh[0] = only_head(mixed, 0)
            kh[1] = only_head(mixed, 1)
        else:
            vt[...] = mixed.T
    def scores_of(first, head):
        keys = first + QBLOCK
        scores = dot_nt(kh[head, 0:keys, :], qs[first:keys, :])
        key_pos = lax.broadcasted_iota(jnp.int32, (QBLOCK, QBLOCK), 0)
        query_pos = lax.broadcasted_iota(jnp.int32, (QBLOCK, QBLOCK), 1)
        corner = jnp.where(key_pos <= query_pos, scores[first:keys, :], NEGATIVE)
        return jnp.concatenate([scores[:first, :], corner], axis=0) if first else corner

    jobs = [(first, head) for first in reversed(range(0, length, QBLOCK)) for head in range(2)]
    ahead = 2
    ready = [scores_of(*job) for job in jobs[:ahead]]
    outs = []
    for n, (first, head) in enumerate(jobs):
        if n + ahead < len(jobs):
            ready.append(scores_of(*jobs[n + ahead]))
        scores = ready[n]
        keys = first + QBLOCK
        top = jnp.max(scores, axis=0, keepdims=True)
        weights = jnp.exp(scores - top)
        total = jnp.sum(weights, axis=0, keepdims=True)
        part = dot_nn(vt[head * HEAD_DIM : (head + 1) * HEAD_DIM, 0:keys], weights.astype(BF16))
        outs.append(part * (1.0 / total))
        lse_ref[0, head : head + 1, first:keys] = top + jnp.log(total)
        if head == 1:
            on[first:keys, :] = jnp.concatenate(outs, axis=0).T.astype(BF16)
            outs = []
    for slot in range(4):
        start = pl.multiple_of(lax.bitwise_xor(member, slot) * size, size)
        block = on[pl.ds(start, size), :]
        dest = (own_ref, send_ref)[slot % 2]
        dest[slot // 2 * size : (slot // 2 + 1) * size, :] = block


def attend(member, proj, taps):
    size = proj[0].shape[0]
    pairs = proj[0].shape[1] // (3 * LANES)
    length = 4 * size
    width = pairs * LANES
    return pl.pallas_call(
        attend_kernel,
        grid=(pairs,),
        in_specs=[SMEM_SPEC]
        + [pl.BlockSpec((size, 3 * LANES), lambda p: (0, p))] * 4
        + [pl.BlockSpec((1, 16, LANES), lambda p: (p, 0, 0))],
        out_specs=[
            pl.BlockSpec((length, 3 * LANES), lambda p: (0, p)),
            pl.BlockSpec((2 * size, LANES), lambda p: (0, p)),
            pl.BlockSpec((2 * size, LANES), lambda p: (0, p)),
            pl.BlockSpec((1, 2, length), lambda p: (p, 0, 0)),
        ],
        out_shape=[
            jax.ShapeDtypeStruct((length, 3 * width), BF16),
            jax.ShapeDtypeStruct((2 * size, width), BF16),
            jax.ShapeDtypeStruct((2 * size, width), BF16),
            jax.ShapeDtypeStruct((pairs, 2, length), F32),
        ],
        scratch_shapes=[
            pltpu.VMEM((3, 8 + length, LANES), F32),
            pltpu.VMEM((2, length, LANES), BF16),
            pltpu.VMEM((LANES, length), BF16),
            pltpu.VMEM((length, LANES), BF16),
            pltpu.VMEM((length, LANES), BF16),
        ],
        compiler_params=params(62),
        cost_estimate=CHEAP,
        name="attend",
    )(member, *proj, taps)


def attend_back_kernel(
    m_ref,
    p0,
    p1,
    p2,
    p3,
    mixed_ref,
    lse_ref,
    taps_ref,
    own_ref,
    send_ref,
    down_ref,
    drecv_ref,
    n0,
    n1,
    n2,
    n3,
    gown_ref,
    gsend_ref,
    gconv_ref,
    keep_ref,
    give_ref,
    pj,
    dm,
    qh,
    doh,
    kt,
    dl,
    dqa,
    nat,
    gp,
    nv,
    sems,
):
    member = m_ref[1]
    size = p0.shape[0]
    length = 4 * size
    scale = jnp.asarray(HEAD_DIM ** (-0.5), BF16)
    halves = [slice(0, size), slice(size, 2 * size)]
    copies = []
    for slot, norm in enumerate((n0, n1, n2, n3)):
        copies.append(pltpu.make_async_copy(norm, nv.at[slot], sems.at[slot]))
        copies[slot].start()
    load_natural(
        member,
        [own_ref[halves[0]], send_ref[halves[0]], own_ref[halves[1]], send_ref[halves[1]]],
        nat.at[0],
        size,
    )
    load_natural(
        member,
        [down_ref[halves[0]], drecv_ref[halves[0]], down_ref[halves[1]], drecv_ref[halves[1]]],
        nat.at[1],
        size,
    )
    grads = nat[1]
    product = (grads.astype(F32) * nat[0].astype(F32)).T
    for head in range(2):
        dl[head : head + 1, :] = jnp.sum(
            product[head * HEAD_DIM : (head + 1) * HEAD_DIM, :], axis=0, keepdims=True
        )
        doh[head] = only_head(grads, head)
        qh[head] = only_head(mixed_ref[:, 0:LANES], head) * scale
    kt[...] = mixed_ref[:, LANES : 2 * LANES].T
    for c in range(3):
        cols = slice(c * LANES, (c + 1) * LANES)
        pj[c, 0:8, :] = jnp.zeros((8, LANES), F32)
        dm[c, length : length + 8, :] = jnp.zeros((8, LANES), F32)
        load_natural(member, [p[:, cols] for p in (p0, p1, p2, p3)], pj.at[c], size, 8)
    def products(first, head):
        keys = mixed_ref[first : first + KBLOCK, LANES : 2 * LANES]
        values = mixed_ref[first : first + KBLOCK, 2 * LANES : 3 * LANES]
        scores = dot_nt(keys, qh[head, first:, :])
        key_pos = lax.broadcasted_iota(jnp.int32, (KBLOCK, KBLOCK), 0)
        query_pos = lax.broadcasted_iota(jnp.int32, (KBLOCK, KBLOCK), 1)
        corner = jnp.where(key_pos <= query_pos, scores[:, :KBLOCK], NEGATIVE)
        if first + KBLOCK < length:
            corner = jnp.concatenate([corner, scores[:, KBLOCK:]], axis=1)
        return corner, dot_nt(values, doh[head, first:, :])

    jobs = [(first, head) for first in range(0, length, KBLOCK) for head in range(2)]
    ahead = 1
    ready = [products(*job) for job in jobs[:ahead]]
    for n, (first, head) in enumerate(jobs):
        if n + ahead < len(jobs):
            ready.append(products(*jobs[n + ahead]))
        scores, grad_probs = ready[n]
        probs = jnp.exp(scores - lse_ref[0, head : head + 1, first:])
        grad_scores = (probs * (grad_probs - dl[head : head + 1, first:])).astype(BF16)
        part_v = dot_nn(probs.astype(BF16), doh[head, first:, :])
        part_k = dot_nn(grad_scores, qh[head, first:, :])
        lanes = slice(head * HEAD_DIM, (head + 1) * HEAD_DIM)
        part_q = dot_nn(kt[lanes, first : first + KBLOCK], grad_scores)
        if first == 0:
            dqa[lanes, :] = part_q
        else:
            dqa[lanes, first:] += part_q
        if head == 0:
            sum_v, sum_k = part_v, part_k
        else:
            dm[1, first : first + KBLOCK, :] = sum_k + part_k
            dm[2, first : first + KBLOCK, :] = sum_v + part_v
    dm[0, 0:length, :] = dqa[...].T * HEAD_DIM ** (-0.5)
    for c in range(3):
        grad = dm[c, 0:length, :]
        for s in range(3):
            gconv_ref[3 * c + s : 3 * c + s + 1, :] = jnp.sum(
                grad * pj[c, 8 - s : 8 - s + length, :], axis=0, keepdims=True
            )
        total = taps_ref[0, 3 * c : 3 * c + 1, :] * grad
        total = total + taps_ref[0, 3 * c + 1 : 3 * c + 2, :] * dm[c, 1 : 1 + length, :]
        total = total + taps_ref[0, 3 * c + 2 : 3 * c + 3, :] * dm[c, 2 : 2 + length, :]
        gp[:, c * LANES : (c + 1) * LANES] = total.astype(BF16)
    total = None
    for slot in range(4):
        copies[slot].wait()
        start = pl.multiple_of(lax.bitwise_xor(member, slot) * size, size)
        dest = (gown_ref, gsend_ref)[slot % 2]
        block = gp[pl.ds(start, size), :]
        dest[slot // 2 * size : (slot // 2 + 1) * size, :] = block
        part = dot_nn(nv[slot], block)
        total = part if total is None else total + part
    rows = total.shape[0] // 8
    store_parts(
        m_ref[3],
        [
            [
                tile
                for b in (x, x + 4, x + 2, x + 6)
                for tile in lane_tiles(total[b * rows : (b + 1) * rows])
            ]
            for x in range(2)
        ],
        keep_ref,
        give_ref,
    )


def attend_back(pair, member, proj, mixed, lse, taps, own, send, grad_own, grad_recv, normed):
    size = proj[0].shape[0]
    length = 4 * size
    width = normed[0].shape[0]
    part = jax.ShapeDtypeStruct((2, 2, 3 * width // 8, LANES), BF16)
    half_spec = pl.BlockSpec((2 * size, LANES), lambda i: (0, pair))
    return pl.pallas_call(
        attend_back_kernel,
        grid=(1,),
        in_specs=[SMEM_SPEC]
        + [pl.BlockSpec((size, 3 * LANES), lambda i: (0, pair))] * 4
        + [
            pl.BlockSpec((length, 3 * LANES), lambda i: (0, pair)),
            pl.BlockSpec((1, 2, length), lambda i: (pair, 0, 0)),
            pl.BlockSpec((1, 16, LANES), lambda i: (pair, 0, 0)),
        ]
        + [half_spec] * 4
        + [pl.BlockSpec(memory_space=pltpu.HBM)] * 4,
        out_specs=[
            pl.BlockSpec((2 * size, 3 * LANES), lambda i: (0, 0)),
            pl.BlockSpec((2 * size, 3 * LANES), lambda i: (0, 0)),
            pl.BlockSpec((16, LANES), lambda i: (0, 0)),
            pl.BlockSpec(part.shape, lambda i: (0, 0, 0, 0)),
            pl.BlockSpec(part.shape, lambda i: (0, 0, 0, 0)),
        ],
        out_shape=[
            jax.ShapeDtypeStruct((2 * size, 3 * LANES), BF16),
            jax.ShapeDtypeStruct((2 * size, 3 * LANES), BF16),
            jax.ShapeDtypeStruct((16, LANES), F32),
            part,
            part,
        ],
        scratch_shapes=[
            pltpu.VMEM((3, 8 + length, LANES), F32),
            pltpu.VMEM((3, 8 + length, LANES), F32),
            pltpu.VMEM((2, length, LANES), BF16),
            pltpu.VMEM((2, length, LANES), BF16),
            pltpu.VMEM((LANES, length), BF16),
            pltpu.VMEM((8, length), F32),
            pltpu.VMEM((LANES, length), F32),
            pltpu.VMEM((2, length, LANES), BF16),
            pltpu.VMEM((length, 3 * LANES), BF16),
            pltpu.VMEM((4, width, size), BF16),
            pltpu.SemaphoreType.DMA((4,)),
        ],
        compiler_params=params(62),
        cost_estimate=CHEAP,
        name="attend_back",
    )(member, *proj, mixed, lse, taps, own, send, grad_own, grad_recv, *normed)


def canonical(flag, own_ref, recv_ref):
    own = own_ref[...]
    recv = recv_ref[...]
    return jnp.concatenate(
        [jnp.where(flag == 0, own, recv), jnp.where(flag == 0, recv, own)], axis=1
    )


def ffn_kernel(
    s_ref,
    hown_ref,
    hrecv_ref,
    wout_ref,
    tok0,
    tok1,
    cot0,
    cot1,
    vec_ref,
    up_ref,
    down_ref,
    out0,
    out1,
    down_keep,
    down_send,
    gres_ref,
    gown_ref,
    gsend_ref,
    sums_ref,
    up_keep,
    up_send,
    relus,
    res,
    nf,
    nft,
    gf,
    acc,
):
    step = pl.program_id(0)
    size = tok0.shape[0]
    core = s_ref[0]
    halves = ((0, s_ref[1] * size), (size, lax.bitwise_xor(s_ref[1], 2) * size))

    def valid(start):
        row = start + lax.broadcasted_iota(jnp.int32, tok0.shape, 0)
        return row < s_ref[2]

    def store(grad):
        rows = grad.shape[0] // 32
        store_parts(
            core,
            [
                [
                    tile
                    for place in range(16)
                    for chunk in [
                        bit
                        + (place >> 3 & 1) * 2
                        + (place >> 2 & 1) * 4
                        + (place >> 1 & 1) * 8
                        + (place & 1) * 16
                    ]
                    for tile in lane_tiles(grad[chunk * rows : (chunk + 1) * rows])
                ]
                for bit in range(2)
            ],
            up_keep,
            up_send,
        )

    @pl.when(step == 0)
    def _():
        attended = dot_nn(canonical(core, hown_ref, hrecv_ref), wout_ref[...])
        for tok, cot, (first, start) in zip((tok0, tok1), (cot0, cot1), halves):
            rows = slice(first, first + size)
            residual = tok[...].astype(F32) + attended[rows]
            res[rows, :] = residual
            scaled, _ = norm_stats(residual)
            nf[rows, :] = (scaled * vec_ref[2:3, :] + vec_ref[3:4, :]).astype(BF16)
            grad = cot[...].reshape(tok.shape)
            gf[rows, :] = jnp.where(valid(start), grad, jnp.zeros_like(grad))
        sums_ref[6:7, :] = jnp.sum(gf[...].astype(F32), axis=0, keepdims=True)
        sums_ref[7:8, :] = jnp.zeros_like(sums_ref[7:8, :])
        acc[...] = jnp.zeros_like(acc)

    @pl.when(step < 4)
    def _():
        relu = jnp.maximum(dot_nn(nf[...], up_ref[...]) + vec_ref[pl.ds(5 + step, 1), :], 0.0)
        relus[step] = relu
        act = (relu * relu).astype(BF16)
        acc[...] += dot_nn(act, down_ref[...])
        grad = dot_tn(act, gf[...])
        rows = grad.shape[0] // 8
        store_parts(
            core,
            [
                [
                    tile
                    for chunk in (bit, bit + 4, bit + 2, bit + 6)
                    for tile in lane_tiles(grad[chunk * rows : (chunk + 1) * rows])
                ]
                for bit in range(2)
            ],
            down_keep,
            down_send,
        )

    @pl.when(step == 3)
    def _():
        for out, (first, start) in zip((out0, out1), halves):
            rows = slice(first, first + size)
            total = res[rows, :] + (acc[rows, :] + vec_ref[4:5, :])
            out[...] = jnp.where(valid(start), total, 0.0).astype(BF16).reshape(out.shape)
        nft[...] = nf[...].T
        acc[...] = jnp.zeros_like(acc)

    @pl.when((step >= 4) & (step < 8))
    def _():
        grad_act = dot_nt(gf[...], down_ref[...])
        grad_pre = (2.0 * relus[step - 4] * grad_act).astype(BF16)
        sums_ref[pl.ds(step - 4, 1), :] = jnp.sum(grad_pre.astype(F32), axis=0, keepdims=True)
        acc[...] += dot_nt(grad_pre, up_ref[...])
        store(dot_nn(nft[...], grad_pre))

    @pl.when(step == 8)
    def _():
        scaled, inv_std = norm_stats(res[...])
        grad = acc[...]
        sums_ref[4:5, :] = jnp.sum(grad * scaled, axis=0, keepdims=True)
        sums_ref[5:6, :] = jnp.sum(grad, axis=0, keepdims=True)
        total = gf[...].astype(F32) + norm_backward(grad, vec_ref[2:3, :], scaled, inv_std)
        gres_ref[...] = total
        attended = total.astype(BF16)
        heads = dot_nt(attended, wout_ref[...]).astype(BF16)
        middle = heads.shape[1] // 2
        gown_ref[...] = jnp.where(core == 0, heads[:, :middle], heads[:, middle:])
        gsend_ref[...] = jnp.where(core == 0, heads[:, middle:], heads[:, :middle])
        store(dot_tn(canonical(core, hown_ref, hrecv_ref), attended))


def ffn(scalars, hown, hrecv, wout, toks, cots, vectors, up, down):
    rows = 2 * toks[0].shape[0]
    width, ff = up.shape
    tile = ff // 4
    assert tile == width
    down_part = jax.ShapeDtypeStruct((2, 2, 2, 2, tile // 8 * width // LANES, LANES), BF16)
    block = width // 32 * tile // LANES
    up_part = jax.ShapeDtypeStruct((2, 2, 2, 2, 5 * block, LANES), BF16)

    def forward(j):
        return jnp.minimum(j, 3)

    def backward(j):
        return jnp.maximum(j - 4, 0)

    def either(j):
        return jnp.where(j < 4, j, jnp.minimum(j - 4, 3))

    down_spec = pl.BlockSpec(
        (2, 2, 1, 1) + down_part.shape[4:],
        lambda j, _: (0, 0, lax.rem(forward(j), 2), lax.div(forward(j), 2), 0, 0),
    )
    up_spec = pl.BlockSpec((2, 2, 2, 2, block, LANES), lambda j, _: (0, 0, 0, 0, backward(j), 0))
    token_block = jax.ShapeDtypeStruct(toks[0].shape, BF16)
    half = jax.ShapeDtypeStruct(hown.shape, BF16)
    return pl.pallas_call(
        ffn_kernel,
        grid_spec=pltpu.PrefetchScalarGridSpec(
            num_scalar_prefetch=1,
            grid=(9,),
            in_specs=[still(a) for a in (hown, hrecv, wout, *toks)]
            + [
                once((1,) + cots[0].shape[1:], lambda j, s: (s[4], 0, 0)),
                still(cots[1]),
                still(vectors),
                pl.BlockSpec((width, tile), lambda j, _: (0, either(j))),
                pl.BlockSpec((tile, width), lambda j, _: (either(j), 0)),
            ],
            out_specs=[
                once((1,) + token_block.shape, lambda j, s: (s[4], 0, 0)),
                once(token_block.shape, lambda j, _: (0, 0)),
                down_spec,
                down_spec,
                once((rows, width), lambda j, _: (0, 0)),
                once(half.shape, lambda j, _: (0, 0)),
                once(half.shape, lambda j, _: (0, 0)),
                pl.BlockSpec((8, width), lambda j, _: (0, 0)),
                up_spec,
                up_spec,
            ],
            scratch_shapes=[
                pltpu.VMEM((4, rows, tile), F32),
                pltpu.VMEM((rows, width), F32),
                pltpu.VMEM((rows, width), BF16),
                pltpu.VMEM((width, rows), BF16),
                pltpu.VMEM((rows, width), BF16),
                pltpu.VMEM((rows, width), F32),
            ],
        ),
        out_shape=[
            jax.ShapeDtypeStruct((2,) + token_block.shape, BF16),
            token_block,
            down_part,
            down_part,
            jax.ShapeDtypeStruct((rows, width), F32),
            half,
            half,
            jax.ShapeDtypeStruct((8, width), F32),
            up_part,
            up_part,
        ],
        compiler_params=params(63),
        cost_estimate=CHEAP,
        name="ffn",
    )(scalars, hown, hrecv, wout, *toks, *cots, vectors, up, down)


def input_grad_kernel(
    s_ref, o0, o1, o2, r0, r1, r2, w_ref, xp_ref, xo_ref, gres_ref, vec_ref, early_ref, *refs
):
    convs, (pair_ref, own_ref, sums_ref, buf) = refs[:3], refs[3:]
    step = pl.program_id(0)
    for n, ref in enumerate((o0, o1, o2, r0, r1, r2)):
        side = s_ref[0] if n < 3 else 1 - s_ref[0]
        start = pl.multiple_of((side * 3 + n % 3) * LANES, LANES)
        for c, tile in enumerate(lane_tiles(ref[...])):
            buf[c, :, pl.ds(start, LANES)] = tile
    grad = dot_nt(buf[0], w_ref[0]) + dot_nt(buf[1], w_ref[1]) + dot_nt(buf[2], w_ref[2])
    x = jnp.where(step < 2, xp_ref[...], xo_ref[...])
    scaled, inv_std = norm_stats(x.astype(F32))

    @pl.when(step == 0)
    def _():
        sums_ref[...] = jnp.zeros_like(sums_ref)
        sums_ref[0:8, :] = early_ref[...]
        for n, conv in enumerate(convs):
            start = pl.multiple_of((s_ref[0] * 3 + n) * LANES, LANES)
            sums_ref[8:17, pl.ds(start, LANES)] = conv[0:9, :]

    sums_ref[17:18, :] += jnp.sum(grad * scaled, axis=0, keepdims=True)
    sums_ref[18:19, :] += jnp.sum(grad, axis=0, keepdims=True)
    total = gres_ref[...] + norm_backward(grad, vec_ref[0:1, :], scaled, inv_std)
    total = total.astype(BF16)

    @pl.when(step < 2)
    def _():
        pair_ref[...] = total

    @pl.when(step >= 2)
    def _():
        own_ref[0] = total


def input_grad(scalars, owns, recvs, weights, x_pair, x_own, grad_residual, vectors, early, convs):
    rows, width = x_own.shape
    tile = rows // 2
    flipped = lambda i, _: (jnp.where(i < 2, i + 2, i - 2), 0)
    first = lambda i: jnp.minimum(i, 1)
    second = lambda i: jnp.maximum(i - 2, 0)
    return pl.pallas_call(
        input_grad_kernel,
        grid_spec=pltpu.PrefetchScalarGridSpec(
            num_scalar_prefetch=1,
            grid=(4,),
            in_specs=[pl.BlockSpec((tile, 3 * LANES), flipped)] * 6
            + [
                still(weights),
                pl.BlockSpec((tile, width), lambda i, _: (first(i), 0)),
                pl.BlockSpec((tile, width), lambda i, _: (second(i), 0)),
                pl.BlockSpec((tile, width), flipped),
                still(vectors),
                still(early),
            ]
            + [still(a) for a in convs],
            out_specs=[
                pl.BlockSpec((tile, width), lambda i, _: (first(i), 0)),
                pl.BlockSpec((1, tile, width), lambda i, s: (s[4], second(i), 0)),
                pl.BlockSpec((24, width), lambda i, _: (0, 0)),
            ],
            scratch_shapes=[pltpu.VMEM((3, tile, width), BF16)],
        ),
        out_shape=[
            jax.ShapeDtypeStruct((rows, width), BF16),
            jax.ShapeDtypeStruct((2, rows, width), BF16),
            jax.ShapeDtypeStruct((24, width), F32),
        ],
        compiler_params=params(62),
        cost_estimate=CHEAP,
        name="input_grad",
    )(
        scalars,
        *owns,
        *recvs,
        weights,
        x_pair,
        x_own,
        grad_residual,
        vectors,
        early,
        *convs,
    )


FREE, ONE, MINE, OTHER = range(4)
BIT_AT = (4, 3, 5, 6)


class Segment:
    def __init__(self, arrays, first, rows):
        self.rows = rows
        self.parts = [(array, self.fresh(array), first) for array in arrays]

    @staticmethod
    def fresh(array):
        return [FREE if n == 2 else ONE for n in array.shape[:4]]

    def chosen(self, dim):
        found = []
        for array, marks, first in self.parts:
            marks = list(marks)
            if dim is not None and marks[dim] == FREE:
                marks[dim] = OTHER
            found.append((array, tuple(marks), first, self.rows))
        return found

    def settle(self, dim, arrived, first):
        parts = []
        for array, marks, own_first in self.parts:
            marks = list(marks)
            if marks[dim] == FREE:
                marks[dim] = MINE
            parts.append((array, marks, own_first))
        self.parts = parts + [(arrived, self.fresh(arrived), first)]


def settle(segments, dim, arrived):
    first = 0
    for segment in segments:
        segment.settle(dim, arrived, first)
        first += segment.rows


def sum_kernel(plan, finish, count, s_ref, *refs):
    pieces = [p for parts in plan for p in parts]
    arrays, outs = refs[:count], refs[count : len(refs) - len(pieces) - 1]
    bufs, sems = refs[len(refs) - len(pieces) - 1 : -1], refs[-1]
    copies = []
    for n, (place, marks, first, rows) in enumerate(pieces):
        where = []
        for dim, mark in enumerate(marks):
            bit = s_ref[BIT_AT[dim]]
            start = {FREE: 0, ONE: 0, MINE: bit, OTHER: 1 - bit}[mark]
            where.append(pl.ds(start, 2 if mark == FREE else 1))
        source = arrays[place].at[tuple(where) + (pl.ds(first, rows), slice(None))]
        copies.append(pltpu.make_async_copy(source, bufs[n], sems.at[n]))
        copies[-1].start()
    n = 0
    totals = []
    for parts in plan:
        for copy in copies[n : n + len(parts)]:
            copy.wait()
        own = bufs[n : n + len(parts)]
        n += len(parts)

        def total(lead, rows, own=own):
            value = None
            for buf in own:
                piece = buf[lead + (rows, slice(None))].astype(F32)
                value = piece if value is None else value + piece
            return value

        totals.append(total)
    finish(s_ref, totals, outs)


def sum_call(scalars, segments, dims, finish, out_shape, name):
    arrays, plan, scratch = [], [], []
    for segment, dim in zip(segments, dims):
        parts = []
        for array, marks, first, rows in segment.chosen(dim):
            place = next((n for n, a in enumerate(arrays) if a is array), None)
            if place is None:
                place = len(arrays)
                arrays.append(array)
            parts.append((place, marks, first, rows))
            sizes = tuple(2 if mark == FREE else 1 for mark in marks)
            scratch.append(pltpu.VMEM(sizes + (rows, LANES), BF16))
        plan.append(parts)
    whole = lambda shape: pl.BlockSpec(shape, lambda i: (0,) * len(shape))
    return pl.pallas_call(
        functools.partial(sum_kernel, plan, finish, len(arrays)),
        grid=(1,),
        in_specs=[SMEM_SPEC] + [pl.BlockSpec(memory_space=pltpu.HBM)] * len(arrays),
        out_specs=[whole(o.shape) for o in out_shape],
        out_shape=out_shape,
        scratch_shapes=scratch + [pltpu.SemaphoreType.DMA((len(scratch),))],
        compiler_params=params(62),
        cost_estimate=CHEAP,
        name=name,
    )(scalars, *arrays)


def outgoing(scalars, groups, dims, name="stage_sum"):
    shapes = []
    for group, dim in zip(groups, dims):
        marks = [group[0].chosen(dim)[0][1]]
        sizes = tuple(2 if mark == FREE else 1 for mark in marks[0])
        shapes.append(jax.ShapeDtypeStruct(sizes + (sum(g.rows for g in group), LANES), BF16))

    def finish(s_ref, totals, outs):
        n = 0
        for group, out in zip(groups, outs):
            first = 0
            for segment in group:
                for lead in itertools.product(*[range(size) for size in out.shape[:4]]):
                    for row in range(0, segment.rows, 48):
                        value = totals[n](lead, slice(row, row + 48))
                        out[lead + (slice(first + row, first + row + 48), slice(None))] = (
                            value.astype(BF16)
                        )
                first += segment.rows
                n += 1

    segments = [segment for group in groups for segment in group]
    each = [dim for group, dim in zip(groups, dims) for _ in group]
    return sum_call(scalars, segments, each, finish, shapes, name)


def hop(value, stage):
    return lax.ppermute(value, stage[0], stage[1])


def ffn_plain(heads, toks, cot, valid, wout, gain, bias, up, upb, down, downb):
    residual = toks.astype(F32) + jnp.dot(heads, wout, preferred_element_type=F32)
    scaled, inv_std = norm_stats(residual)
    normed = (scaled * gain + bias).astype(BF16)
    relu = jnp.maximum(jnp.dot(normed, up, preferred_element_type=F32) + upb, 0.0)
    act = jnp.square(relu).astype(BF16)
    out = jnp.dot(act, down, preferred_element_type=F32) + downb
    result = jnp.where(valid, residual + out, 0.0).astype(BF16)
    grad_ffn = jnp.where(valid, cot, jnp.zeros_like(cot))
    grad_y = grad_ffn.astype(F32)
    grad_act = jnp.einsum("td,fd->tf", grad_ffn, down, preferred_element_type=F32)
    grad_pre = (2.0 * relu * grad_act).astype(BF16)
    grad = jnp.einsum("tf,df->td", grad_pre, up, preferred_element_type=F32)
    sums = jnp.stack([jnp.sum(grad * scaled, axis=0), jnp.sum(grad, axis=0)])
    grad_residual = grad_y + norm_backward(grad, gain, scaled, inv_std)
    attended = grad_residual.astype(BF16)
    grad_heads = jnp.einsum("td,ed->te", attended, wout, preferred_element_type=F32)
    return (
        result,
        grad_residual,
        grad_heads.astype(BF16),
        sums,
        jnp.sum(grad_pre.astype(F32), axis=0),
        jnp.sum(grad_y, axis=0),
        jnp.einsum("td,tf->df", normed, grad_pre, preferred_element_type=F32),
        jnp.einsum("tf,td->fd", act, grad_ffn, preferred_element_type=F32),
        jnp.einsum("te,td->ed", heads, attended, preferred_element_type=F32),
    )


def on_device(
    tokens,
    cotangent,
    lengths,
    pre_attn_gain,
    pre_attn_bias,
    qkv_weight,
    conv_weight,
    out_weight,
    pre_ffn_gain,
    pre_ffn_bias,
    up_weight,
    up_bias,
    down_weight,
    down_bias,
):
    groups = lax.axis_size("mp")
    batch_groups = lax.axis_size("batch")
    devices = groups * batch_groups
    member = lax.axis_index("mp").astype(jnp.int32)
    batch = lax.axis_index("batch").astype(jnp.int32)
    seqs, rows, width = tokens.shape
    ff = up_weight.shape[1]
    middle = width // 2
    quarter = width // groups
    pairs = middle // LANES
    taps = conv_weight.shape[1]
    assert groups == 4 and seqs == 2 and pairs == 3 and taps == 3
    fast = batch_groups == 8 and (width // devices) % 8 == 0
    half = lax.shift_right_logical(member, 1)
    core = lax.bitwise_and(member, 1)
    x_bit = lax.bitwise_and(batch, 1)
    z0_bit = lax.bitwise_and(lax.shift_right_logical(batch, 1), 1)
    z1_bit = lax.shift_right_logical(batch, 2)
    vectors = (pre_attn_gain, pre_attn_bias, pre_ffn_gain, pre_ffn_bias, down_bias, up_bias)
    vectors = jnp.concatenate(vectors).astype(F32).reshape(5 + ff // width, width)

    def swap_core(value):
        return lax.ppermute(value, "mp", CORE)

    def swap_pair(value):
        return lax.ppermute(value, "mp", PAIR)

    def pick(value, index):
        starts = (index,) + (jnp.int32(0),) * (value.ndim - 1)
        return lax.dynamic_slice(value, starts, (1,) + value.shape[1:])[0]

    length = pick(lengths, half)
    scalars = jnp.stack([core, member, length, x_bit, half, z0_bit, z1_bit]).astype(jnp.int32)

    hops = [("mp", PAIR)] + [
        ("batch", [(i, i ^ flip) for i in range(batch_groups)]) for flip in (1, 2, 4)
    ]
    DY, DX, DZ0, DZ1 = range(4)
    tie = lax.optimization_barrier

    tok_pair = swap_pair(pick(tokens, 1 - half))
    tok_own = pick(tokens, half)
    tok_core = swap_core(tok_own)
    taps_own = lax.dynamic_slice_in_dim(conv_weight, core * middle, middle, 2).astype(F32)
    taps_own = taps_own.reshape(3 * taps, pairs, LANES).transpose(1, 0, 2)
    taps_own = jnp.pad(taps_own, ((0, 0), (0, 16 - 3 * taps), (0, 0)))

    def norm_project(block):
        return project(scalars, block, vectors, qkv_weight)

    first = norm_project(tok_own)
    tok_core, cot_send, taps_own = tie((tok_core, pick(cotangent, 1 - half), taps_own))
    second = norm_project(tok_core)
    tok_pair, first, second = tie((tok_pair, first, second))
    tok_cross = swap_core(tok_pair)
    third = norm_project(tok_pair)
    tok_cross, third = tie((tok_cross, third))
    fourth = norm_project(tok_cross)
    cot_send, fourth = tie((cot_send, fourth))
    cot_pair = swap_pair(cot_send)
    normed, proj = zip(first, second, third, fourth)
    mixed, heads_own, heads_send, lse = attend(scalars, proj, taps_own)
    heads_recv = swap_core(heads_send)

    if fast:
        (
            result_all,
            result_give,
            down_keep,
            down_send,
            grad_residual,
            grad_own,
            grad_send,
            early,
            up_keep,
            up_send,
        ) = ffn(
            scalars,
            heads_own,
            heads_recv,
            out_weight,
            (tok_own, tok_pair),
            (cotangent, cot_pair),
            vectors,
            up_weight,
            down_weight,
        )
    else:
        row = jnp.arange(rows, dtype=jnp.int32)
        row_pos = [member * rows + row, jnp.bitwise_xor(member, 2) * rows + row]
        heads_all = jnp.concatenate(
            [
                jnp.where(core == 0, heads_own, heads_recv),
                jnp.where(core == 0, heads_recv, heads_own),
            ],
            axis=1,
        )
        (
            result,
            grad_residual,
            grad_heads,
            sums_ffn,
            sums_up,
            sums_down,
            grad_up,
            grad_down,
            grad_out,
        ) = ffn_plain(
            heads_all,
            jnp.concatenate([tok_own, tok_pair], axis=0),
            jnp.concatenate([pick(cotangent, half), cot_pair], axis=0),
            (jnp.concatenate(row_pos) < length)[:, None],
            out_weight,
            vectors[2:3],
            vectors[3:4],
            up_weight,
            vectors[5:].reshape(1, ff),
            down_weight,
            vectors[4:5],
        )
        result_all, result_give = jnp.stack([result[:rows]] * 2), result[rows:]
        early = [sums_up.reshape(ff // width, width), sums_ffn, sums_down[None]]
        early = jnp.concatenate(early + [jnp.zeros((1, width), F32)], axis=0)
        grad_own = lax.dynamic_slice_in_dim(grad_heads, core * middle, middle, 1)
        grad_send = lax.dynamic_slice_in_dim(grad_heads, (1 - core) * middle, middle, 1)
    grad_recv = swap_core(grad_send)
    if fast:
        down_recv = swap_core(down_send)
        grad_recv, down_recv, up_send = tie((grad_recv, down_recv, up_send))
        up_recv = swap_core(up_send)
        down_rows = down_keep.shape[4]
        up_rows = up_keep.shape[4]
        each = (down_rows + up_rows) // 3
        down = (down_keep, down_recv)
        up = (up_keep, up_recv)
        rest = down_rows - each
        down_a, down_b = Segment(down, 0, each), Segment(down, each, rest)
        up_a, up_b = Segment(up, 0, each - rest), Segment(up, each - rest, each)
        group_1, group_2, group_3 = [down_a], [down_b, up_a], [up_b]

        def stage(dims, groups=(group_1, group_2, group_3)):
            return outgoing(scalars, groups, dims)

        def arrive(dims, sent, groups=(group_1, group_2, group_3)):
            for group, dim, value in zip(groups, dims, sent):
                settle(group, dim, value)

        dims = (DX, DZ0, DY)
        sent = stage(dims[:1], (group_1,))
        sent, grad_recv, up_recv = tie((sent, grad_recv, up_recv))
        up_a.parts[1] = (up_recv,) + up_a.parts[1][1:]
        up_b.parts[1] = (up_recv,) + up_b.parts[1][1:]
        sent = list(sent) + list(stage(dims[1:], (group_2, group_3)))
        grad_own, grad_recv, sent = tie((grad_own, grad_recv, sent))
        sent = [hop(v, hops[d]) for v, d in zip(sent, dims)]
        arrive(dims, sent)

    def backward(pair, grad_recv):
        own, send, conv, keep, give = attend_back(
            pair,
            scalars,
            proj,
            mixed,
            lse,
            taps_own,
            heads_own,
            heads_send,
            grad_own,
            grad_recv,
            normed,
        )
        keep = keep.reshape((1, 1) + keep.shape)
        give = give.reshape((1, 1) + give.shape)
        return own, send, conv, keep, give

    qkv_rows = 3 * width // 8
    own_0, send_0, conv_0, keep_0, give_0 = backward(0, grad_recv)
    if fast:
        dims = (DY, DZ1, DX)
        sent = stage(dims)
        grad_recv, own_0, send_0, give_0, sent = tie((grad_recv, own_0, send_0, give_0, sent))
        sent = [hop(v, hops[d]) for v, d in zip(sent, dims)]
        arrive(dims, sent)
        qkv_0 = Segment((keep_0, hop(give_0, hops[DX])), 0, qkv_rows)
        group_1.append(qkv_0)
    recv_0 = swap_core(send_0)
    own_1, send_1, conv_1, keep_1, give_1 = backward(1, grad_recv)
    if fast:
        dims = (DZ0, DX, DZ1)
        sent = stage(dims)
        grad_recv, own_1, send_1, give_1, recv_0, result_give, sent = tie(
            (grad_recv, own_1, send_1, give_1, recv_0, result_give, sent)
        )
        sent = [hop(v, hops[d]) for v, d in zip(sent, dims)]
    result_back = swap_pair(result_give)
    recv_1 = swap_core(send_1)
    own_2, send_2, conv_2, keep_2, give_2 = backward(2, grad_recv)
    if fast:
        own_2, send_2, give_1, give_2, recv_1, result_back, sent = tie(
            (own_2, send_2, give_1, give_2, recv_1, result_back, sent)
        )
        arrive(dims, sent)
        give_1 = hop(give_1, hops[DX])
        give_2 = hop(give_2, hops[DX])
    recv_2 = swap_core(send_2)
    if fast:
        dims = (DZ1, DY, DZ0)
        sent = stage(dims)
        recv_2, sent = tie((recv_2, sent))
        ffn_waiting = [hop(v, hops[d]) for v, d in zip(sent, dims)]
    g_own = (own_0, own_1, own_2)
    g_send = (send_0, send_1, send_2)
    g_recv = (recv_0, recv_1, recv_2)
    g_conv = (conv_0, conv_1, conv_2)
    grad_in_pair, tokens_grad, small = input_grad(
        scalars,
        g_own,
        g_recv,
        qkv_weight,
        tok_pair,
        tok_own,
        grad_residual,
        vectors,
        early,
        g_conv,
    )
    grad_in_back = swap_pair(grad_in_pair)

    def place(both, other):
        return lax.dynamic_update_slice(both, other[None], (1 - half, 0, 0))

    result_all = place(result_all, result_back)
    index = batch * groups + member
    share = width // devices
    part = width // batch_groups

    if not fast:
        axes = ("batch", "mp")
        grad_qkv = 0.0
        for n, (norm, slot) in enumerate(zip(normed, (0, 0, 1, 1))):
            source = (g_own, g_send)[n % 2]
            grads = jnp.concatenate([g[slot * rows : (slot + 1) * rows] for g in source], axis=1)
            grad_qkv = grad_qkv + jnp.einsum("dt,te->de", norm, grads, preferred_element_type=F32)
        grad_qkv = grad_qkv.reshape(width, pairs, 3, LANES).transpose(2, 0, 1, 3)
        qkv_full = lax.dynamic_update_slice_in_dim(
            jnp.zeros((3, width, width), F32), grad_qkv.reshape(3, width, middle), core * middle, 2
        )
        qkv_flat = qkv_full.reshape(3, batch_groups, part, groups, quarter)
        qkv_flat = qkv_flat.transpose(1, 3, 0, 2, 4).reshape(devices * 3 * part, quarter)

        def scatter(value):
            return lax.psum_scatter(value, axes, scatter_dimension=0, tiled=True)

        small = lax.psum(small, axes)
        qkv_out = scatter(qkv_flat).reshape(3, part, quarter)
        up_out, down_out, out_out = scatter(grad_up), scatter(grad_down), scatter(grad_out)
    else:
        give_1, give_2, small, ffn_waiting = tie((give_1, give_2, small, ffn_waiting))
        arrive((DZ1, DY, DZ0), ffn_waiting)
        qkv_1 = Segment((keep_1, give_1), 0, qkv_rows)
        qkv_2 = Segment((keep_2, give_2), 0, qkv_rows)
        (sent,) = outgoing(scalars, [[qkv_1, qkv_2]], [DZ0])
        small = small + hop(small, ("mp", CORE))
        small, sent = tie((small, sent))
        waiting = hop(sent, hops[DZ0])
        small = small + hop(small, hops[DX])
        small, waiting = tie((small, waiting))
        settle([qkv_1, qkv_2], DZ0, waiting)
        (sent,) = outgoing(scalars, [[qkv_1, qkv_2]], [DZ1])
        sent = hop(sent, hops[DZ1])
        small = small + hop(small, hops[DZ0])
        small = small + hop(small, hops[DZ1])
        small, sent, grad_in_back = tie((small, sent, grad_in_back))
        settle([qkv_1, qkv_2], DZ1, sent)
        small = small + hop(small, hops[DY])

        def finish_ffn(s_ref, totals, outs):
            whole = [total((0,) * 4, slice(None)) for total in totals]
            downs = jnp.concatenate(whole[0:2], axis=0)
            ups = jnp.concatenate(whole[2:4], axis=0)
            down_out, up_out, out_out = outs
            for out, values in ((down_out, downs), (up_out, ups), (out_out, ups[down_rows:])):
                size, cols = out.shape
                for n in range(cols // LANES):
                    out[:, n * LANES : (n + 1) * LANES] = values[n * size : (n + 1) * size]

        down_out, up_out, out_out = sum_call(
            scalars,
            [down_a, down_b, up_a, up_b],
            [None] * 4,
            finish_ffn,
            [
                jax.ShapeDtypeStruct((ff // devices, width), F32),
                jax.ShapeDtypeStruct((share, ff), F32),
                jax.ShapeDtypeStruct((share, width), F32),
            ],
            "ffn_sum",
        )

        def finish_qkv(s_ref, totals, outs):
            first, middle, last = [total((0,) * 4, slice(None)) for total in totals]
            lower = jnp.concatenate([first, middle[:, :HEAD_DIM]], axis=1)
            upper = jnp.concatenate([middle[:, HEAD_DIM:], last], axis=1)
            outs[0][...] = jnp.where(s_ref[0] == 0, lower, upper)
            outs[1][...] = jnp.where(s_ref[4] == 0, upper, lower).astype(BF16)
            outs[2][...] = jnp.where(s_ref[4] == 0, lower, upper).astype(BF16)

        keep, straight, crossed = sum_call(
            scalars,
            [qkv_0, qkv_1, qkv_2],
            [None] * 3,
            finish_qkv,
            [jax.ShapeDtypeStruct((qkv_rows, quarter), t) for t in (F32, BF16, BF16)],
            "qkv_sum",
        )
        straight = lax.ppermute(straight, "mp", [(2, 0), (0, 1), (3, 2), (1, 3)])
        crossed = lax.ppermute(crossed, "mp", [(2, 1), (1, 2)])
        qkv_out = straight.astype(F32) + jnp.where(half == core, keep, crossed.astype(F32))
        qkv_out = qkv_out.reshape(3, part, quarter)

    tokens_grad = place(tokens_grad, grad_in_back)
    up_bias_out = pick(small[: ff // width].reshape(devices, ff // devices), index)
    mine = pick(small.reshape(24, devices, share).transpose(1, 0, 2), index)
    return (
        result_all,
        tokens_grad,
        mine[17],
        mine[18],
        qkv_out,
        mine[8:17].reshape(3, taps, share),
        out_out,
        mine[4],
        mine[5],
        up_out,
        up_bias_out,
        down_out,
        mine[6],
    )


def solution(mesh):
    in_specs = (
        P("batch", "mp", None),
        P("batch", "mp", None),
        P("batch"),
    ) + (P(),) * 11
    out_specs = (
        P("batch", "mp", None),
        P("batch", "mp", None),
        P(("batch", "mp")),
        P(("batch", "mp")),
        P(None, "batch", "mp"),
        P(None, None, ("batch", "mp")),
        P(("batch", "mp"), None),
        P(("batch", "mp")),
        P(("batch", "mp")),
        P(("batch", "mp"), None),
        P(("batch", "mp")),
        P(("batch", "mp"), None),
        P(("batch", "mp")),
    )
    return jax.shard_map(
        on_device, mesh=mesh, in_specs=in_specs, out_specs=out_specs, check_vma=False
    )
```

```python
import functools
import itertools

import jax
import jax.numpy as jnp
from jax import lax
from jax.experimental import pallas as pl
from jax.experimental.pallas import tpu as pltpu
from jax.sharding import PartitionSpec as P

HEAD_DIM = 64
LANES = 128
EPSILON = 1e-05
NEGATIVE = -1000000000.0
QBLOCK = 512
KBLOCK = 256
F32 = jnp.float32
BF16 = jnp.bfloat16

CORE = [(i, i ^ 1) for i in range(4)]
PAIR = [(i, i ^ 2) for i in range(4)]


def dot_nt(left, right):
    return lax.dot_general(left, right, (((1,), (1,)), ((), ())), preferred_element_type=F32)


def dot_nn(left, right):
    return lax.dot_general(left, right, (((1,), (0,)), ((), ())), preferred_element_type=F32)


def dot_tn(left, right):
    return lax.dot_general(left, right, (((0,), (0,)), ((), ())), preferred_element_type=F32)


def params(mib):
    return pltpu.CompilerParams(vmem_limit_bytes=mib << 20)


def lane_tiles(values):
    return [values[:, n : n + LANES] for n in range(0, values.shape[1], LANES)]


def once(shape, index_map):
    return pl.BlockSpec(shape, index_map, pipeline_mode=pl.Buffered(1))


def still(array):
    return once(array.shape, lambda *_: (0,) * array.ndim)


CHEAP = pl.CostEstimate(flops=1 << 20, bytes_accessed=1 << 16, transcendentals=0)
BUSY = pl.CostEstimate(flops=2048 << 20, bytes_accessed=2 << 20, transcendentals=0)
SMEM_SPEC = pl.BlockSpec(memory_space=pltpu.SMEM)


def norm_stats(values):
    center = values - jnp.mean(values, axis=-1, keepdims=True)
    inv_std = lax.rsqrt(jnp.mean(center * center, axis=-1, keepdims=True) + EPSILON)
    return center * inv_std, inv_std


def norm_backward(grad_out, norm_gain, scaled, inv_std):
    weighted = grad_out * norm_gain
    return inv_std * (
        weighted
        - jnp.mean(weighted, axis=-1, keepdims=True)
        - scaled * jnp.mean(weighted * scaled, axis=-1, keepdims=True)
    )


def project_kernel(s_ref, x_ref, vec_ref, w_ref, normed_ref, proj_ref):
    scaled, _ = norm_stats(x_ref[...].astype(F32))
    normed = (scaled * vec_ref[0:1, :] + vec_ref[1:2, :]).astype(BF16)
    normed_ref[...] = normed.T
    for c in range(3):
        part = dot_nn(normed, w_ref[c]).astype(BF16)
        for n, tile in enumerate(lane_tiles(part)):
            start = (3 * n + c) * LANES
            proj_ref[:, start : start + LANES] = tile


def project(scalars, x, vectors, weights):
    rows, width = x.shape
    cols = 3 * width // 2
    return pl.pallas_call(
        project_kernel,
        grid_spec=pltpu.PrefetchScalarGridSpec(
            num_scalar_prefetch=1,
            grid=(1,),
            in_specs=[
                once((rows, width), lambda i, s: (0, 0)),
                still(vectors),
                once((3, width, width // 2), lambda i, s: (0, 0, s[0])),
            ],
            out_specs=[
                once((width, rows), lambda i, s: (0, 0)),
                once((rows, cols), lambda i, s: (0, 0)),
            ],
        ),
        out_shape=[
            jax.ShapeDtypeStruct((width, rows), BF16),
            jax.ShapeDtypeStruct((rows, cols), BF16),
        ],
        compiler_params=params(62),
        cost_estimate=CHEAP,
        name="project",
    )(scalars, x, vectors, weights)


def store_parts(flag, parts, keep_ref, send_ref):
    first = jnp.concatenate(parts[0], axis=0).astype(BF16)
    second = jnp.concatenate(parts[1], axis=0).astype(BF16)
    keep_ref[...] = jnp.where(flag == 0, first, second).reshape(keep_ref.shape)
    send_ref[...] = jnp.where(flag == 0, second, first).reshape(send_ref.shape)


def only_head(values, head):
    lane = lax.broadcasted_iota(jnp.int32, values.shape, 1)
    return jnp.where((lane // HEAD_DIM) == head, values, jnp.zeros_like(values))


def load_natural(member, blocks, dest, size, shift=0):
    for slot, block in enumerate(blocks):
        start = pl.multiple_of(lax.bitwise_xor(member, slot) * size, 8) + shift
        start = pl.multiple_of(start, 8)
        dest[pl.ds(start, size), :] = block.astype(dest.dtype)


def attend_kernel(
    m_ref, p0, p1, p2, p3, taps_ref, mixed_ref, own_ref, send_ref, lse_ref, pj, kh, vt, on, qs
):
    member = m_ref[1]
    size = p0.shape[0]
    length = 4 * size
    scale = jnp.asarray(HEAD_DIM ** (-0.5), BF16)
    for c in range(3):
        cols = slice(c * LANES, (c + 1) * LANES)
        pj[c, 0:8, :] = jnp.zeros((8, LANES), F32)
        load_natural(member, [p[:, cols] for p in (p0, p1, p2, p3)], pj.at[c], size, 8)
    for c in range(3):
        total = taps_ref[0, 3 * c : 3 * c + 1, :] * pj[c, 8 : 8 + length, :]
        total = total + taps_ref[0, 3 * c + 1 : 3 * c + 2, :] * pj[c, 7 : 7 + length, :]
        total = total + taps_ref[0, 3 * c + 2 : 3 * c + 3, :] * pj[c, 6 : 6 + length, :]
        mixed = total.astype(BF16)
        mixed_ref[:, c * LANES : (c + 1) * LANES] = mixed
        if c == 0:
            qs[...] = mixed * scale
        elif c == 1:
            kh[0] = only_head(mixed, 0)
            kh[1] = only_head(mixed, 1)
        else:
            vt[...] = mixed.T
    def scores_of(first, head):
        keys = first + QBLOCK
        scores = dot_nt(kh[head, 0:keys, :], qs[first:keys, :])
        key_pos = lax.broadcasted_iota(jnp.int32, (QBLOCK, QBLOCK), 0)
        query_pos = lax.broadcasted_iota(jnp.int32, (QBLOCK, QBLOCK), 1)
        corner = jnp.where(key_pos <= query_pos, scores[first:keys, :], NEGATIVE)
        return jnp.concatenate([scores[:first, :], corner], axis=0) if first else corner

    jobs = [(first, head) for first in reversed(range(0, length, QBLOCK)) for head in range(2)]
    ahead = 2
    ready = [scores_of(*job) for job in jobs[:ahead]]
    outs = []
    for n, (first, head) in enumerate(jobs):
        if n + ahead < len(jobs):
            ready.append(scores_of(*jobs[n + ahead]))
        scores = ready[n]
        keys = first + QBLOCK
        top = jnp.max(scores, axis=0, keepdims=True)
        weights = jnp.exp(scores - top)
        total = jnp.sum(weights, axis=0, keepdims=True)
        part = dot_nn(vt[head * HEAD_DIM : (head + 1) * HEAD_DIM, 0:keys], weights.astype(BF16))
        outs.append(part * (1.0 / total))
        lse_ref[0, head : head + 1, first:keys] = top + jnp.log(total)
        if head == 1:
            on[first:keys, :] = jnp.concatenate(outs, axis=0).T.astype(BF16)
            outs = []
    for slot in range(4):
        start = pl.multiple_of(lax.bitwise_xor(member, slot) * size, size)
        block = on[pl.ds(start, size), :]
        dest = (own_ref, send_ref)[slot % 2]
        dest[slot // 2 * size : (slot // 2 + 1) * size, :] = block


def attend(member, proj, taps):
    size = proj[0].shape[0]
    pairs = proj[0].shape[1] // (3 * LANES)
    length = 4 * size
    width = pairs * LANES
    return pl.pallas_call(
        attend_kernel,
        grid=(pairs,),
        in_specs=[SMEM_SPEC]
        + [pl.BlockSpec((size, 3 * LANES), lambda p: (0, p))] * 4
        + [pl.BlockSpec((1, 16, LANES), lambda p: (p, 0, 0))],
        out_specs=[
            pl.BlockSpec((length, 3 * LANES), lambda p: (0, p)),
            pl.BlockSpec((2 * size, LANES), lambda p: (0, p)),
            pl.BlockSpec((2 * size, LANES), lambda p: (0, p)),
            pl.BlockSpec((1, 2, length), lambda p: (p, 0, 0)),
        ],
        out_shape=[
            jax.ShapeDtypeStruct((length, 3 * width), BF16),
            jax.ShapeDtypeStruct((2 * size, width), BF16),
            jax.ShapeDtypeStruct((2 * size, width), BF16),
            jax.ShapeDtypeStruct((pairs, 2, length), F32),
        ],
        scratch_shapes=[
            pltpu.VMEM((3, 8 + length, LANES), F32),
            pltpu.VMEM((2, length, LANES), BF16),
            pltpu.VMEM((LANES, length), BF16),
            pltpu.VMEM((length, LANES), BF16),
            pltpu.VMEM((length, LANES), BF16),
        ],
        compiler_params=params(62),
        cost_estimate=CHEAP,
        name="attend",
    )(member, *proj, taps)


def attend_back_kernel(
    m_ref,
    p0,
    p1,
    p2,
    p3,
    mixed_ref,
    lse_ref,
    taps_ref,
    own_ref,
    send_ref,
    down_ref,
    drecv_ref,
    n0,
    n1,
    n2,
    n3,
    gown_ref,
    gsend_ref,
    gconv_ref,
    keep_ref,
    give_ref,
    pj,
    dm,
    qh,
    doh,
    kt,
    dl,
    dqa,
    nat,
    gp,
    nv,
    sems,
):
    member = m_ref[1]
    size = p0.shape[0]
    length = 4 * size
    scale = jnp.asarray(HEAD_DIM ** (-0.5), BF16)
    halves = [slice(0, size), slice(size, 2 * size)]
    copies = []
    for slot, norm in enumerate((n0, n1, n2, n3)):
        copies.append(pltpu.make_async_copy(norm, nv.at[slot], sems.at[slot]))
        copies[slot].start()
    load_natural(
        member,
        [own_ref[halves[0]], send_ref[halves[0]], own_ref[halves[1]], send_ref[halves[1]]],
        nat.at[0],
        size,
    )
    load_natural(
        member,
        [down_ref[halves[0]], drecv_ref[halves[0]], down_ref[halves[1]], drecv_ref[halves[1]]],
        nat.at[1],
        size,
    )
    grads = nat[1]
    product = (grads.astype(F32) * nat[0].astype(F32)).T
    for head in range(2):
        dl[head : head + 1, :] = jnp.sum(
            product[head * HEAD_DIM : (head + 1) * HEAD_DIM, :], axis=0, keepdims=True
        )
        doh[head] = only_head(grads, head)
        qh[head] = only_head(mixed_ref[:, 0:LANES], head) * scale
    kt[...] = mixed_ref[:, LANES : 2 * LANES].T
    for c in range(3):
        cols = slice(c * LANES, (c + 1) * LANES)
        pj[c, 0:8, :] = jnp.zeros((8, LANES), F32)
        dm[c, length : length + 8, :] = jnp.zeros((8, LANES), F32)
        load_natural(member, [p[:, cols] for p in (p0, p1, p2, p3)], pj.at[c], size, 8)
    def products(first, head):
        keys = mixed_ref[first : first + KBLOCK, LANES : 2 * LANES]
        values = mixed_ref[first : first + KBLOCK, 2 * LANES : 3 * LANES]
        scores = dot_nt(keys, qh[head, first:, :])
        key_pos = lax.broadcasted_iota(jnp.int32, (KBLOCK, KBLOCK), 0)
        query_pos = lax.broadcasted_iota(jnp.int32, (KBLOCK, KBLOCK), 1)
        corner = jnp.where(key_pos <= query_pos, scores[:, :KBLOCK], NEGATIVE)
        if first + KBLOCK < length:
            corner = jnp.concatenate([corner, scores[:, KBLOCK:]], axis=1)
        return corner, dot_nt(values, doh[head, first:, :])

    jobs = [(first, head) for first in range(0, length, KBLOCK) for head in range(2)]
    ahead = 1
    ready = [products(*job) for job in jobs[:ahead]]
    for n, (first, head) in enumerate(jobs):
        if n + ahead < len(jobs):
            ready.append(products(*jobs[n + ahead]))
        scores, grad_probs = ready[n]
        probs = jnp.exp(scores - lse_ref[0, head : head + 1, first:])
        grad_scores = (probs * (grad_probs - dl[head : head + 1, first:])).astype(BF16)
        part_v = dot_nn(probs.astype(BF16), doh[head, first:, :])
        part_k = dot_nn(grad_scores, qh[head, first:, :])
        lanes = slice(head * HEAD_DIM, (head + 1) * HEAD_DIM)
        part_q = dot_nn(kt[lanes, first : first + KBLOCK], grad_scores)
        if first == 0:
            dqa[lanes, :] = part_q
        else:
            dqa[lanes, first:] += part_q
        if head == 0:
            sum_v, sum_k = part_v, part_k
        else:
            dm[1, first : first + KBLOCK, :] = sum_k + part_k
            dm[2, first : first + KBLOCK, :] = sum_v + part_v
    dm[0, 0:length, :] = dqa[...].T * HEAD_DIM ** (-0.5)
    for c in range(3):
        grad = dm[c, 0:length, :]
        for s in range(3):
            gconv_ref[3 * c + s : 3 * c + s + 1, :] = jnp.sum(
                grad * pj[c, 8 - s : 8 - s + length, :], axis=0, keepdims=True
            )
        total = taps_ref[0, 3 * c : 3 * c + 1, :] * grad
        total = total + taps_ref[0, 3 * c + 1 : 3 * c + 2, :] * dm[c, 1 : 1 + length, :]
        total = total + taps_ref[0, 3 * c + 2 : 3 * c + 3, :] * dm[c, 2 : 2 + length, :]
        gp[:, c * LANES : (c + 1) * LANES] = total.astype(BF16)
    total = None
    for slot in range(4):
        copies[slot].wait()
        start = pl.multiple_of(lax.bitwise_xor(member, slot) * size, size)
        dest = (gown_ref, gsend_ref)[slot % 2]
        block = gp[pl.ds(start, size), :]
        dest[slot // 2 * size : (slot // 2 + 1) * size, :] = block
        part = dot_nn(nv[slot], block)
        total = part if total is None else total + part
    rows = total.shape[0] // 8
    store_parts(
        m_ref[3],
        [
            [
                tile
                for b in (x, x + 4, x + 2, x + 6)
                for tile in lane_tiles(total[b * rows : (b + 1) * rows])
            ]
            for x in range(2)
        ],
        keep_ref,
        give_ref,
    )


def attend_back(pair, member, proj, mixed, lse, taps, own, send, grad_own, grad_recv, normed):
    size = proj[0].shape[0]
    length = 4 * size
    width = normed[0].shape[0]
    part = jax.ShapeDtypeStruct((2, 2, 3 * width // 8, LANES), BF16)
    half_spec = pl.BlockSpec((2 * size, LANES), lambda i: (0, pair))
    return pl.pallas_call(
        attend_back_kernel,
        grid=(1,),
        in_specs=[SMEM_SPEC]
        + [pl.BlockSpec((size, 3 * LANES), lambda i: (0, pair))] * 4
        + [
            pl.BlockSpec((length, 3 * LANES), lambda i: (0, pair)),
            pl.BlockSpec((1, 2, length), lambda i: (pair, 0, 0)),
            pl.BlockSpec((1, 16, LANES), lambda i: (pair, 0, 0)),
        ]
        + [half_spec] * 4
        + [pl.BlockSpec(memory_space=pltpu.HBM)] * 4,
        out_specs=[
            pl.BlockSpec((2 * size, 3 * LANES), lambda i: (0, 0)),
            pl.BlockSpec((2 * size, 3 * LANES), lambda i: (0, 0)),
            pl.BlockSpec((16, LANES), lambda i: (0, 0)),
            pl.BlockSpec(part.shape, lambda i: (0, 0, 0, 0)),
            pl.BlockSpec(part.shape, lambda i: (0, 0, 0, 0)),
        ],
        out_shape=[
            jax.ShapeDtypeStruct((2 * size, 3 * LANES), BF16),
            jax.ShapeDtypeStruct((2 * size, 3 * LANES), BF16),
            jax.ShapeDtypeStruct((16, LANES), F32),
            part,
            part,
        ],
        scratch_shapes=[
            pltpu.VMEM((3, 8 + length, LANES), F32),
            pltpu.VMEM((3, 8 + length, LANES), F32),
            pltpu.VMEM((2, length, LANES), BF16),
            pltpu.VMEM((2, length, LANES), BF16),
            pltpu.VMEM((LANES, length), BF16),
            pltpu.VMEM((8, length), F32),
            pltpu.VMEM((LANES, length), F32),
            pltpu.VMEM((2, length, LANES), BF16),
            pltpu.VMEM((length, 3 * LANES), BF16),
            pltpu.VMEM((4, width, size), BF16),
            pltpu.SemaphoreType.DMA((4,)),
        ],
        compiler_params=params(62),
        cost_estimate=CHEAP,
        name="attend_back",
    )(member, *proj, mixed, lse, taps, own, send, grad_own, grad_recv, *normed)


def canonical(flag, own_ref, recv_ref):
    own = own_ref[...]
    recv = recv_ref[...]
    return jnp.concatenate(
        [jnp.where(flag == 0, own, recv), jnp.where(flag == 0, recv, own)], axis=1
    )


def ffn_kernel(
    s_ref,
    hown_ref,
    hrecv_ref,
    wout_ref,
    tok0,
    tok1,
    cot0,
    cot1,
    vec_ref,
    up_ref,
    down_ref,
    out0,
    out1,
    down_keep,
    down_send,
    gres_ref,
    gown_ref,
    gsend_ref,
    sums_ref,
    up_keep,
    up_send,
    relus,
    res,
    nf,
    nft,
    gf,
    acc,
):
    step = pl.program_id(0)
    size = tok0.shape[0]
    core = s_ref[0]
    halves = ((0, s_ref[1] * size), (size, lax.bitwise_xor(s_ref[1], 2) * size))

    def valid(start):
        row = start + lax.broadcasted_iota(jnp.int32, tok0.shape, 0)
        return row < s_ref[2]

    def store(grad):
        rows = grad.shape[0] // 32
        store_parts(
            core,
            [
                [
                    tile
                    for place in range(16)
                    for chunk in [
                        bit
                        + (place >> 3 & 1) * 2
                        + (place >> 2 & 1) * 4
                        + (place >> 1 & 1) * 8
                        + (place & 1) * 16
                    ]
                    for tile in lane_tiles(grad[chunk * rows : (chunk + 1) * rows])
                ]
                for bit in range(2)
            ],
            up_keep,
            up_send,
        )

    @pl.when(step == 0)
    def _():
        attended = dot_nn(canonical(core, hown_ref, hrecv_ref), wout_ref[...])
        for tok, cot, (first, start) in zip((tok0, tok1), (cot0, cot1), halves):
            rows = slice(first, first + size)
            residual = tok[...].astype(F32) + attended[rows]
            res[rows, :] = residual
            scaled, _ = norm_stats(residual)
            nf[rows, :] = (scaled * vec_ref[2:3, :] + vec_ref[3:4, :]).astype(BF16)
            grad = cot[...].reshape(tok.shape)
            gf[rows, :] = jnp.where(valid(start), grad, jnp.zeros_like(grad))
        sums_ref[6:7, :] = jnp.sum(gf[...].astype(F32), axis=0, keepdims=True)
        sums_ref[7:8, :] = jnp.zeros_like(sums_ref[7:8, :])
        acc[...] = jnp.zeros_like(acc)

    @pl.when(step < 4)
    def _():
        relu = jnp.maximum(dot_nn(nf[...], up_ref[...]) + vec_ref[pl.ds(5 + step, 1), :], 0.0)
        relus[step] = relu
        act = (relu * relu).astype(BF16)
        acc[...] += dot_nn(act, down_ref[...])
        grad = dot_tn(act, gf[...])
        rows = grad.shape[0] // 8
        store_parts(
            core,
            [
                [
                    tile
                    for chunk in (bit, bit + 4, bit + 2, bit + 6)
                    for tile in lane_tiles(grad[chunk * rows : (chunk + 1) * rows])
                ]
                for bit in range(2)
            ],
            down_keep,
            down_send,
        )

    @pl.when(step == 3)
    def _():
        for out, (first, start) in zip((out0, out1), halves):
            rows = slice(first, first + size)
            total = res[rows, :] + (acc[rows, :] + vec_ref[4:5, :])
            out[...] = jnp.where(valid(start), total, 0.0).astype(BF16).reshape(out.shape)
        nft[...] = nf[...].T
        acc[...] = jnp.zeros_like(acc)

    @pl.when((step >= 4) & (step < 8))
    def _():
        grad_act = dot_nt(gf[...], down_ref[...])
        grad_pre = (2.0 * relus[step - 4] * grad_act).astype(BF16)
        sums_ref[pl.ds(step - 4, 1), :] = jnp.sum(grad_pre.astype(F32), axis=0, keepdims=True)
        acc[...] += dot_nt(grad_pre, up_ref[...])
        store(dot_nn(nft[...], grad_pre))

    @pl.when(step == 8)
    def _():
        scaled, inv_std = norm_stats(res[...])
        grad = acc[...]
        sums_ref[4:5, :] = jnp.sum(grad * scaled, axis=0, keepdims=True)
        sums_ref[5:6, :] = jnp.sum(grad, axis=0, keepdims=True)
        total = gf[...].astype(F32) + norm_backward(grad, vec_ref[2:3, :], scaled, inv_std)
        gres_ref[...] = total
        attended = total.astype(BF16)
        heads = dot_nt(attended, wout_ref[...]).astype(BF16)
        middle = heads.shape[1] // 2
        gown_ref[...] = jnp.where(core == 0, heads[:, :middle], heads[:, middle:])
        gsend_ref[...] = jnp.where(core == 0, heads[:, middle:], heads[:, :middle])
        store(dot_tn(canonical(core, hown_ref, hrecv_ref), attended))


def ffn(scalars, hown, hrecv, wout, toks, cots, vectors, up, down):
    rows = 2 * toks[0].shape[0]
    width, ff = up.shape
    tile = ff // 4
    assert tile == width
    down_part = jax.ShapeDtypeStruct((2, 2, 2, 2, tile // 8 * width // LANES, LANES), BF16)
    block = width // 32 * tile // LANES
    up_part = jax.ShapeDtypeStruct((2, 2, 2, 2, 5 * block, LANES), BF16)

    def forward(j):
        return jnp.minimum(j, 3)

    def backward(j):
        return jnp.maximum(j - 4, 0)

    def either(j):
        return jnp.where(j < 4, j, jnp.minimum(j - 4, 3))

    down_spec = pl.BlockSpec(
        (2, 2, 1, 1) + down_part.shape[4:],
        lambda j, _: (0, 0, lax.rem(forward(j), 2), lax.div(forward(j), 2), 0, 0),
    )
    up_spec = pl.BlockSpec((2, 2, 2, 2, block, LANES), lambda j, _: (0, 0, 0, 0, backward(j), 0))
    token_block = jax.ShapeDtypeStruct(toks[0].shape, BF16)
    half = jax.ShapeDtypeStruct(hown.shape, BF16)
    return pl.pallas_call(
        ffn_kernel,
        grid_spec=pltpu.PrefetchScalarGridSpec(
            num_scalar_prefetch=1,
            grid=(9,),
            in_specs=[still(a) for a in (hown, hrecv, wout, *toks)]
            + [
                once((1,) + cots[0].shape[1:], lambda j, s: (s[4], 0, 0)),
                still(cots[1]),
                still(vectors),
                pl.BlockSpec((width, tile), lambda j, _: (0, either(j))),
                pl.BlockSpec((tile, width), lambda j, _: (either(j), 0)),
            ],
            out_specs=[
                once((1,) + token_block.shape, lambda j, s: (s[4], 0, 0)),
                once(token_block.shape, lambda j, _: (0, 0)),
                down_spec,
                down_spec,
                once((rows, width), lambda j, _: (0, 0)),
                once(half.shape, lambda j, _: (0, 0)),
                once(half.shape, lambda j, _: (0, 0)),
                pl.BlockSpec((8, width), lambda j, _: (0, 0)),
                up_spec,
                up_spec,
            ],
            scratch_shapes=[
                pltpu.VMEM((4, rows, tile), F32),
                pltpu.VMEM((rows, width), F32),
                pltpu.VMEM((rows, width), BF16),
                pltpu.VMEM((width, rows), BF16),
                pltpu.VMEM((rows, width), BF16),
                pltpu.VMEM((rows, width), F32),
            ],
        ),
        out_shape=[
            jax.ShapeDtypeStruct((2,) + token_block.shape, BF16),
            token_block,
            down_part,
            down_part,
            jax.ShapeDtypeStruct((rows, width), F32),
            half,
            half,
            jax.ShapeDtypeStruct((8, width), F32),
            up_part,
            up_part,
        ],
        compiler_params=params(63),
        cost_estimate=CHEAP,
        name="ffn",
    )(scalars, hown, hrecv, wout, *toks, *cots, vectors, up, down)


def input_grad_kernel(
    s_ref, o0, o1, o2, r0, r1, r2, w_ref, xp_ref, xo_ref, gres_ref, vec_ref, early_ref, *refs
):
    convs, (pair_ref, own_ref, sums_ref, buf) = refs[:3], refs[3:]
    step = pl.program_id(0)
    for n, ref in enumerate((o0, o1, o2, r0, r1, r2)):
        side = s_ref[0] if n < 3 else 1 - s_ref[0]
        start = pl.multiple_of((side * 3 + n % 3) * LANES, LANES)
        for c, tile in enumerate(lane_tiles(ref[...])):
            buf[c, :, pl.ds(start, LANES)] = tile
    grad = dot_nt(buf[0], w_ref[0]) + dot_nt(buf[1], w_ref[1]) + dot_nt(buf[2], w_ref[2])
    x = jnp.where(step < 2, xp_ref[...], xo_ref[...])
    scaled, inv_std = norm_stats(x.astype(F32))

    @pl.when(step == 0)
    def _():
        sums_ref[...] = jnp.zeros_like(sums_ref)
        sums_ref[0:8, :] = early_ref[...]
        for n, conv in enumerate(convs):
            start = pl.multiple_of((s_ref[0] * 3 + n) * LANES, LANES)
            sums_ref[8:17, pl.ds(start, LANES)] = conv[0:9, :]

    sums_ref[17:18, :] += jnp.sum(grad * scaled, axis=0, keepdims=True)
    sums_ref[18:19, :] += jnp.sum(grad, axis=0, keepdims=True)
    total = gres_ref[...] + norm_backward(grad, vec_ref[0:1, :], scaled, inv_std)
    total = total.astype(BF16)

    @pl.when(step < 2)
    def _():
        pair_ref[...] = total

    @pl.when(step >= 2)
    def _():
        own_ref[0] = total


def input_grad(scalars, owns, recvs, weights, x_pair, x_own, grad_residual, vectors, early, convs):
    rows, width = x_own.shape
    tile = rows // 2
    flipped = lambda i, _: (jnp.where(i < 2, i + 2, i - 2), 0)
    first = lambda i: jnp.minimum(i, 1)
    second = lambda i: jnp.maximum(i - 2, 0)
    return pl.pallas_call(
        input_grad_kernel,
        grid_spec=pltpu.PrefetchScalarGridSpec(
            num_scalar_prefetch=1,
            grid=(4,),
            in_specs=[pl.BlockSpec((tile, 3 * LANES), flipped)] * 6
            + [
                still(weights),
                pl.BlockSpec((tile, width), lambda i, _: (first(i), 0)),
                pl.BlockSpec((tile, width), lambda i, _: (second(i), 0)),
                pl.BlockSpec((tile, width), flipped),
                still(vectors),
                still(early),
            ]
            + [still(a) for a in convs],
            out_specs=[
                pl.BlockSpec((tile, width), lambda i, _: (first(i), 0)),
                pl.BlockSpec((1, tile, width), lambda i, s: (s[4], second(i), 0)),
                pl.BlockSpec((24, width), lambda i, _: (0, 0)),
            ],
            scratch_shapes=[pltpu.VMEM((3, tile, width), BF16)],
        ),
        out_shape=[
            jax.ShapeDtypeStruct((rows, width), BF16),
            jax.ShapeDtypeStruct((2, rows, width), BF16),
            jax.ShapeDtypeStruct((24, width), F32),
        ],
        compiler_params=params(62),
        cost_estimate=CHEAP,
        name="input_grad",
    )(
        scalars,
        *owns,
        *recvs,
        weights,
        x_pair,
        x_own,
        grad_residual,
        vectors,
        early,
        *convs,
    )


FREE, ONE, MINE, OTHER = range(4)
BIT_AT = (4, 3, 5, 6)


class Segment:
    def __init__(self, arrays, first, rows):
        self.rows = rows
        self.parts = [(array, self.fresh(array), first) for array in arrays]

    @staticmethod
    def fresh(array):
        return [FREE if n == 2 else ONE for n in array.shape[:4]]

    def chosen(self, dim):
        found = []
        for array, marks, first in self.parts:
            marks = list(marks)
            if dim is not None and marks[dim] == FREE:
                marks[dim] = OTHER
            found.append((array, tuple(marks), first, self.rows))
        return found

    def settle(self, dim, arrived, first):
        parts = []
        for array, marks, own_first in self.parts:
            marks = list(marks)
            if marks[dim] == FREE:
                marks[dim] = MINE
            parts.append((array, marks, own_first))
        self.parts = parts + [(arrived, self.fresh(arrived), first)]


def settle(segments, dim, arrived):
    first = 0
    for segment in segments:
        segment.settle(dim, arrived, first)
        first += segment.rows


def sum_kernel(plan, finish, count, made, s_ref, *refs):
    pieces = [p for parts in plan for p in parts]
    arrays, outs, bufs = refs[:count], refs[count : count + made], refs[count + made : -1]
    sems = refs[-1]
    staged = bufs[len(pieces) :]
    results = []

    def send(n):
        if staged:
            copy = pltpu.make_async_copy(staged[n], outs[n], sems.at[len(pieces) + n])
            copy.start()
            results.append(copy)

    copies = []
    for n, (place, marks, first, rows) in enumerate(pieces):
        where = []
        for dim, mark in enumerate(marks):
            bit = s_ref[BIT_AT[dim]]
            start = {FREE: 0, ONE: 0, MINE: bit, OTHER: 1 - bit}[mark]
            where.append(pl.ds(start, 2 if mark == FREE else 1))
        source = arrays[place].at[tuple(where) + (pl.ds(first, rows), slice(None))]
        copies.append(pltpu.make_async_copy(source, bufs[n], sems.at[n]))
        copies[-1].start()
    n = 0
    totals = []
    for parts in plan:
        own = bufs[n : n + len(parts)]
        pending = copies[n : n + len(parts)]
        n += len(parts)

        def total(lead, rows, own=own, pending=pending):
            while pending:
                pending.pop(0).wait()
            value = None
            for buf in own:
                piece = buf[lead + (rows, slice(None))].astype(F32)
                value = piece if value is None else value + piece
            return value

        totals.append(total)
    finish(s_ref, totals, staged or outs, send)
    for copy in results:
        copy.wait()


def sum_call(scalars, segments, dims, finish, out_shape, name, cost=BUSY, stream=False):
    arrays, plan, scratch = [], [], []
    for segment, dim in zip(segments, dims):
        parts = []
        for array, marks, first, rows in segment.chosen(dim):
            place = next((n for n, a in enumerate(arrays) if a is array), None)
            if place is None:
                place = len(arrays)
                arrays.append(array)
            parts.append((place, marks, first, rows))
            sizes = tuple(2 if mark == FREE else 1 for mark in marks)
            scratch.append(pltpu.VMEM(sizes + (rows, LANES), BF16))
        plan.append(parts)
    whole = lambda shape: pl.BlockSpec(shape, lambda i: (0,) * len(shape))
    sems = len(scratch)
    if stream:
        whole = lambda _: pl.BlockSpec(memory_space=pltpu.HBM)
        scratch += [pltpu.VMEM(o.shape, o.dtype) for o in out_shape]
        sems += len(out_shape)
    return pl.pallas_call(
        functools.partial(sum_kernel, plan, finish, len(arrays), len(out_shape)),
        grid=(1,),
        in_specs=[SMEM_SPEC] + [pl.BlockSpec(memory_space=pltpu.HBM)] * len(arrays),
        out_specs=[whole(o.shape) for o in out_shape],
        out_shape=out_shape,
        scratch_shapes=scratch + [pltpu.SemaphoreType.DMA((sems,))],
        compiler_params=params(62),
        cost_estimate=cost,
        name=name,
    )(scalars, *arrays)


def outgoing(scalars, groups, dims, cost=CHEAP):
    shapes = []
    for group, dim in zip(groups, dims):
        marks = [group[0].chosen(dim)[0][1]]
        sizes = tuple(2 if mark == FREE else 1 for mark in marks[0])
        shapes.append(jax.ShapeDtypeStruct(sizes + (sum(g.rows for g in group), LANES), BF16))

    def finish(s_ref, totals, outs, send):
        n = 0
        for place, (group, out) in enumerate(zip(groups, outs)):
            first = 0
            for segment in group:
                for lead in itertools.product(*[range(size) for size in out.shape[:4]]):
                    for row in range(0, segment.rows, 48):
                        value = totals[n](lead, slice(row, row + 48))
                        out[lead + (slice(first + row, first + row + 48), slice(None))] = (
                            value.astype(BF16)
                        )
                first += segment.rows
                n += 1
            send(place)

    segments = [segment for group in groups for segment in group]
    each = [dim for group, dim in zip(groups, dims) for _ in group]
    return sum_call(scalars, segments, each, finish, shapes, "stage_sum", cost, True)


def hop(value, stage):
    return lax.ppermute(value, stage[0], stage[1])


def ffn_plain(heads, toks, cot, valid, wout, gain, bias, up, upb, down, downb):
    residual = toks.astype(F32) + jnp.dot(heads, wout, preferred_element_type=F32)
    scaled, inv_std = norm_stats(residual)
    normed = (scaled * gain + bias).astype(BF16)
    relu = jnp.maximum(jnp.dot(normed, up, preferred_element_type=F32) + upb, 0.0)
    act = jnp.square(relu).astype(BF16)
    out = jnp.dot(act, down, preferred_element_type=F32) + downb
    result = jnp.where(valid, residual + out, 0.0).astype(BF16)
    grad_ffn = jnp.where(valid, cot, jnp.zeros_like(cot))
    grad_y = grad_ffn.astype(F32)
    grad_act = jnp.einsum("td,fd->tf", grad_ffn, down, preferred_element_type=F32)
    grad_pre = (2.0 * relu * grad_act).astype(BF16)
    grad = jnp.einsum("tf,df->td", grad_pre, up, preferred_element_type=F32)
    sums = jnp.stack([jnp.sum(grad * scaled, axis=0), jnp.sum(grad, axis=0)])
    grad_residual = grad_y + norm_backward(grad, gain, scaled, inv_std)
    attended = grad_residual.astype(BF16)
    grad_heads = jnp.einsum("td,ed->te", attended, wout, preferred_element_type=F32)
    return (
        result,
        grad_residual,
        grad_heads.astype(BF16),
        sums,
        jnp.sum(grad_pre.astype(F32), axis=0),
        jnp.sum(grad_y, axis=0),
        jnp.einsum("td,tf->df", normed, grad_pre, preferred_element_type=F32),
        jnp.einsum("tf,td->fd", act, grad_ffn, preferred_element_type=F32),
        jnp.einsum("te,td->ed", heads, attended, preferred_element_type=F32),
    )


def on_device(
    tokens,
    cotangent,
    lengths,
    pre_attn_gain,
    pre_attn_bias,
    qkv_weight,
    conv_weight,
    out_weight,
    pre_ffn_gain,
    pre_ffn_bias,
    up_weight,
    up_bias,
    down_weight,
    down_bias,
):
    groups = lax.axis_size("mp")
    batch_groups = lax.axis_size("batch")
    devices = groups * batch_groups
    member = lax.axis_index("mp").astype(jnp.int32)
    batch = lax.axis_index("batch").astype(jnp.int32)
    seqs, rows, width = tokens.shape
    ff = up_weight.shape[1]
    middle = width // 2
    quarter = width // groups
    pairs = middle // LANES
    taps = conv_weight.shape[1]
    assert groups == 4 and seqs == 2 and pairs == 3 and taps == 3
    fast = batch_groups == 8 and (width // devices) % 8 == 0
    half = lax.shift_right_logical(member, 1)
    core = lax.bitwise_and(member, 1)
    x_bit = lax.bitwise_and(batch, 1)
    z0_bit = lax.bitwise_and(lax.shift_right_logical(batch, 1), 1)
    z1_bit = lax.shift_right_logical(batch, 2)
    vectors = (pre_attn_gain, pre_attn_bias, pre_ffn_gain, pre_ffn_bias, down_bias, up_bias)
    vectors = jnp.concatenate(vectors).astype(F32).reshape(5 + ff // width, width)

    def swap_core(value):
        return lax.ppermute(value, "mp", CORE)

    def swap_pair(value):
        return lax.ppermute(value, "mp", PAIR)

    def pick(value, index):
        starts = (index,) + (jnp.int32(0),) * (value.ndim - 1)
        return lax.dynamic_slice(value, starts, (1,) + value.shape[1:])[0]

    length = pick(lengths, half)
    scalars = jnp.stack([core, member, length, x_bit, half, z0_bit, z1_bit]).astype(jnp.int32)

    hops = [("mp", PAIR)] + [
        ("batch", [(i, i ^ flip) for i in range(batch_groups)]) for flip in (1, 2, 4)
    ]
    DY, DX, DZ0, DZ1 = range(4)
    tie = lax.optimization_barrier

    tok_pair = swap_pair(pick(tokens, 1 - half))
    tok_own = pick(tokens, half)
    tok_core = swap_core(tok_own)
    taps_own = lax.dynamic_slice_in_dim(conv_weight, core * middle, middle, 2).astype(F32)
    taps_own = taps_own.reshape(3 * taps, pairs, LANES).transpose(1, 0, 2)
    taps_own = jnp.pad(taps_own, ((0, 0), (0, 16 - 3 * taps), (0, 0)))

    def norm_project(block):
        return project(scalars, block, vectors, qkv_weight)

    first = norm_project(tok_own)
    tok_core, cot_send, taps_own = tie((tok_core, pick(cotangent, 1 - half), taps_own))
    second = norm_project(tok_core)
    tok_pair, first, second = tie((tok_pair, first, second))
    tok_cross = swap_core(tok_pair)
    third = norm_project(tok_pair)
    tok_cross, third = tie((tok_cross, third))
    fourth = norm_project(tok_cross)
    cot_send, fourth = tie((cot_send, fourth))
    cot_pair = swap_pair(cot_send)
    normed, proj = zip(first, second, third, fourth)
    mixed, heads_own, heads_send, lse = attend(scalars, proj, taps_own)
    heads_recv = swap_core(heads_send)

    if fast:
        (
            result_all,
            result_give,
            down_keep,
            down_send,
            grad_residual,
            grad_own,
            grad_send,
            early,
            up_keep,
            up_send,
        ) = ffn(
            scalars,
            heads_own,
            heads_recv,
            out_weight,
            (tok_own, tok_pair),
            (cotangent, cot_pair),
            vectors,
            up_weight,
            down_weight,
        )
    else:
        row = jnp.arange(rows, dtype=jnp.int32)
        row_pos = [member * rows + row, jnp.bitwise_xor(member, 2) * rows + row]
        heads_all = jnp.concatenate(
            [
                jnp.where(core == 0, heads_own, heads_recv),
                jnp.where(core == 0, heads_recv, heads_own),
            ],
            axis=1,
        )
        (
            result,
            grad_residual,
            grad_heads,
            sums_ffn,
            sums_up,
            sums_down,
            grad_up,
            grad_down,
            grad_out,
        ) = ffn_plain(
            heads_all,
            jnp.concatenate([tok_own, tok_pair], axis=0),
            jnp.concatenate([pick(cotangent, half), cot_pair], axis=0),
            (jnp.concatenate(row_pos) < length)[:, None],
            out_weight,
            vectors[2:3],
            vectors[3:4],
            up_weight,
            vectors[5:].reshape(1, ff),
            down_weight,
            vectors[4:5],
        )
        result_all, result_give = jnp.stack([result[:rows]] * 2), result[rows:]
        early = [sums_up.reshape(ff // width, width), sums_ffn, sums_down[None]]
        early = jnp.concatenate(early + [jnp.zeros((1, width), F32)], axis=0)
        grad_own = lax.dynamic_slice_in_dim(grad_heads, core * middle, middle, 1)
        grad_send = lax.dynamic_slice_in_dim(grad_heads, (1 - core) * middle, middle, 1)
    grad_recv = swap_core(grad_send)
    if fast:
        down_recv = swap_core(down_send)
        grad_recv, down_recv, up_send = tie((grad_recv, down_recv, up_send))
        up_recv = swap_core(up_send)
        down_rows = down_keep.shape[4]
        up_rows = up_keep.shape[4]
        each = (down_rows + up_rows) // 3
        down = (down_keep, down_recv)
        up = (up_keep, up_recv)
        rest = down_rows - each
        down_a, down_b = Segment(down, 0, each), Segment(down, each, rest)
        up_a, up_b = Segment(up, 0, each - rest), Segment(up, each - rest, each)
        group_1, group_2, group_3 = [down_a], [down_b, up_a], [up_b]

        def stage(dims, groups=(group_1, group_2, group_3)):
            return outgoing(scalars, groups, dims)

        def arrive(dims, sent, groups=(group_1, group_2, group_3)):
            for group, dim, value in zip(groups, dims, sent):
                settle(group, dim, value)

        dims = (DX, DZ0, DY)
        sent = stage(dims[:1], (group_1,))
        sent, grad_recv, up_recv = tie((sent, grad_recv, up_recv))
        up_a.parts[1] = (up_recv,) + up_a.parts[1][1:]
        up_b.parts[1] = (up_recv,) + up_b.parts[1][1:]
        sent = list(sent) + list(stage(dims[1:], (group_2, group_3)))
        grad_own, grad_recv, sent = tie((grad_own, grad_recv, sent))
        sent = [hop(v, hops[d]) for v, d in zip(sent, dims)]
        arrive(dims, sent)

    def backward(pair, grad_recv):
        own, send, conv, keep, give = attend_back(
            pair,
            scalars,
            proj,
            mixed,
            lse,
            taps_own,
            heads_own,
            heads_send,
            grad_own,
            grad_recv,
            normed,
        )
        keep = keep.reshape((1, 1) + keep.shape)
        give = give.reshape((1, 1) + give.shape)
        return own, send, conv, keep, give

    qkv_rows = 3 * width // 8
    own_0, send_0, conv_0, keep_0, give_0 = backward(0, grad_recv)
    if fast:
        dims = (DY, DZ1, DX)
        sent = stage(dims)
        grad_recv, own_0, send_0, give_0, sent = tie((grad_recv, own_0, send_0, give_0, sent))
        sent = [hop(v, hops[d]) for v, d in zip(sent, dims)]
        arrive(dims, sent)
        qkv_0 = Segment((keep_0, hop(give_0, hops[DX])), 0, qkv_rows)
        group_1.append(qkv_0)
    recv_0 = swap_core(send_0)
    own_1, send_1, conv_1, keep_1, give_1 = backward(1, grad_recv)
    if fast:
        dims = (DZ0, DX, DZ1)
        sent = stage(dims)
        grad_recv, own_1, send_1, give_1, recv_0, result_give, sent = tie(
            (grad_recv, own_1, send_1, give_1, recv_0, result_give, sent)
        )
        sent = [hop(v, hops[d]) for v, d in zip(sent, dims)]
    result_back = swap_pair(result_give)
    recv_1 = swap_core(send_1)
    own_2, send_2, conv_2, keep_2, give_2 = backward(2, grad_recv)
    if fast:
        own_2, send_2, give_1, give_2, recv_1, result_back, sent = tie(
            (own_2, send_2, give_1, give_2, recv_1, result_back, sent)
        )
        arrive(dims, sent)
        give_1 = hop(give_1, hops[DX])
        give_2 = hop(give_2, hops[DX])
    recv_2 = swap_core(send_2)
    if fast:
        dims = (DZ1, DY, DZ0)
        sent = stage(dims)
        recv_2, sent = tie((recv_2, sent))
        ffn_waiting = [hop(v, hops[d]) for v, d in zip(sent, dims)]
    g_own = (own_0, own_1, own_2)
    g_send = (send_0, send_1, send_2)
    g_recv = (recv_0, recv_1, recv_2)
    g_conv = (conv_0, conv_1, conv_2)
    grad_in_pair, tokens_grad, small = input_grad(
        scalars,
        g_own,
        g_recv,
        qkv_weight,
        tok_pair,
        tok_own,
        grad_residual,
        vectors,
        early,
        g_conv,
    )
    grad_in_back = swap_pair(grad_in_pair)

    def place(both, other):
        return lax.dynamic_update_slice(both, other[None], (1 - half, 0, 0))

    result_all = place(result_all, result_back)
    index = batch * groups + member
    share = width // devices
    part = width // batch_groups

    if not fast:
        axes = ("batch", "mp")
        grad_qkv = 0.0
        for n, (norm, slot) in enumerate(zip(normed, (0, 0, 1, 1))):
            source = (g_own, g_send)[n % 2]
            grads = jnp.concatenate([g[slot * rows : (slot + 1) * rows] for g in source], axis=1)
            grad_qkv = grad_qkv + jnp.einsum("dt,te->de", norm, grads, preferred_element_type=F32)
        grad_qkv = grad_qkv.reshape(width, pairs, 3, LANES).transpose(2, 0, 1, 3)
        qkv_full = lax.dynamic_update_slice_in_dim(
            jnp.zeros((3, width, width), F32), grad_qkv.reshape(3, width, middle), core * middle, 2
        )
        qkv_flat = qkv_full.reshape(3, batch_groups, part, groups, quarter)
        qkv_flat = qkv_flat.transpose(1, 3, 0, 2, 4).reshape(devices * 3 * part, quarter)

        def scatter(value):
            return lax.psum_scatter(value, axes, scatter_dimension=0, tiled=True)

        small = lax.psum(small, axes)
        qkv_out = scatter(qkv_flat).reshape(3, part, quarter)
        up_out, down_out, out_out = scatter(grad_up), scatter(grad_down), scatter(grad_out)
    else:
        give_1, give_2, small, ffn_waiting = tie((give_1, give_2, small, ffn_waiting))
        arrive((DZ1, DY, DZ0), ffn_waiting)
        qkv_1 = Segment((keep_1, give_1), 0, qkv_rows)
        qkv_2 = Segment((keep_2, give_2), 0, qkv_rows)
        (sent,) = outgoing(scalars, [[qkv_1, qkv_2]], [DZ0])
        small = small + hop(small, ("mp", CORE))
        small, sent = tie((small, sent))
        waiting = hop(sent, hops[DZ0])
        small = small + hop(small, hops[DX])
        def finish_ffn(s_ref, totals, outs, send):
            whole = [total((0,) * 4, slice(None)) for total in totals]
            downs = jnp.concatenate(whole[0:2], axis=0)
            ups = jnp.concatenate(whole[2:4], axis=0)
            down_out, up_out, out_out = outs
            for out, values in ((down_out, downs), (up_out, ups), (out_out, ups[down_rows:])):
                size, cols = out.shape
                for n in range(cols // LANES):
                    out[:, n * LANES : (n + 1) * LANES] = values[n * size : (n + 1) * size]

        down_out, up_out, out_out = sum_call(
            scalars,
            [down_a, down_b, up_a, up_b],
            [None] * 4,
            finish_ffn,
            [
                jax.ShapeDtypeStruct((ff // devices, width), F32),
                jax.ShapeDtypeStruct((share, ff), F32),
                jax.ShapeDtypeStruct((share, width), F32),
            ],
            "ffn_sum",
        )

        small, waiting, result_all, down_out, up_out, out_out = tie(
            (small, waiting, result_all, down_out, up_out, out_out)
        )
        settle([qkv_1, qkv_2], DZ0, waiting)
        (sent,) = outgoing(scalars, [[qkv_1, qkv_2]], [DZ1], BUSY)
        sent = hop(sent, hops[DZ1])
        small = small + hop(small, hops[DZ0])
        small = small + hop(small, hops[DZ1])
        small, sent, grad_in_back = tie((small, sent, grad_in_back))
        settle([qkv_1, qkv_2], DZ1, sent)
        small = small + hop(small, hops[DY])

        def finish_qkv(s_ref, totals, outs, send):
            first, middle, last = [total((0,) * 4, slice(None)) for total in totals]
            lower = jnp.concatenate([first, middle[:, :HEAD_DIM]], axis=1)
            upper = jnp.concatenate([middle[:, HEAD_DIM:], last], axis=1)
            outs[0][...] = jnp.where(s_ref[0] == 0, lower, upper)
            outs[1][...] = jnp.where(s_ref[4] == 0, upper, lower).astype(BF16)
            outs[2][...] = jnp.where(s_ref[4] == 0, lower, upper).astype(BF16)

        keep, straight, crossed = sum_call(
            scalars,
            [qkv_0, qkv_1, qkv_2],
            [None] * 3,
            finish_qkv,
            [jax.ShapeDtypeStruct((qkv_rows, quarter), t) for t in (F32, BF16, BF16)],
            "qkv_sum",
        )
        straight = lax.ppermute(straight, "mp", [(2, 0), (0, 1), (3, 2), (1, 3)])
        crossed = lax.ppermute(crossed, "mp", [(2, 1), (1, 2)])
        qkv_out = straight.astype(F32) + jnp.where(half == core, keep, crossed.astype(F32))
        qkv_out = qkv_out.reshape(3, part, quarter)

    tokens_grad = place(tokens_grad, grad_in_back)
    up_bias_out = pick(small[: ff // width].reshape(devices, ff // devices), index)
    mine = pick(small.reshape(24, devices, share).transpose(1, 0, 2), index)
    return (
        result_all,
        tokens_grad,
        mine[17],
        mine[18],
        qkv_out,
        mine[8:17].reshape(3, taps, share),
        out_out,
        mine[4],
        mine[5],
        up_out,
        up_bias_out,
        down_out,
        mine[6],
    )


def solution(mesh):
    in_specs = (
        P("batch", "mp", None),
        P("batch", "mp", None),
        P("batch"),
    ) + (P(),) * 11
    out_specs = (
        P("batch", "mp", None),
        P("batch", "mp", None),
        P(("batch", "mp")),
        P(("batch", "mp")),
        P(None, "batch", "mp"),
        P(None, None, ("batch", "mp")),
        P(("batch", "mp"), None),
        P(("batch", "mp")),
        P(("batch", "mp")),
        P(("batch", "mp"), None),
        P(("batch", "mp")),
        P(("batch", "mp"), None),
        P(("batch", "mp")),
    )
    return jax.shard_map(
        on_device, mesh=mesh, in_specs=in_specs, out_specs=out_specs, check_vma=False
    )
```

```python
import functools
import itertools

import jax
import jax.numpy as jnp
from jax import lax
from jax.experimental import pallas as pl
from jax.experimental.pallas import tpu as pltpu
from jax.sharding import PartitionSpec as P

HEAD_DIM = 64
LANES = 128
EPSILON = 1e-05
NEGATIVE = -1000000000.0
QBLOCK = 512
KBLOCK = 256
F32 = jnp.float32
BF16 = jnp.bfloat16

CORE = [(i, i ^ 1) for i in range(4)]
PAIR = [(i, i ^ 2) for i in range(4)]


def dot_nt(left, right):
    return lax.dot_general(left, right, (((1,), (1,)), ((), ())), preferred_element_type=F32)


def dot_nn(left, right):
    return lax.dot_general(left, right, (((1,), (0,)), ((), ())), preferred_element_type=F32)


def dot_tn(left, right):
    return lax.dot_general(left, right, (((0,), (0,)), ((), ())), preferred_element_type=F32)


def params(mib):
    return pltpu.CompilerParams(vmem_limit_bytes=mib << 20)


def lane_tiles(values):
    return [values[:, n : n + LANES] for n in range(0, values.shape[1], LANES)]


def once(shape, index_map):
    return pl.BlockSpec(shape, index_map, pipeline_mode=pl.Buffered(1))


def still(array):
    return once(array.shape, lambda *_: (0,) * array.ndim)


CHEAP = pl.CostEstimate(flops=1 << 20, bytes_accessed=1 << 16, transcendentals=0)
BUSY = pl.CostEstimate(flops=2048 << 20, bytes_accessed=2 << 20, transcendentals=0)
SMEM_SPEC = pl.BlockSpec(memory_space=pltpu.SMEM)


def norm_stats(values):
    center = values - jnp.mean(values, axis=-1, keepdims=True)
    inv_std = lax.rsqrt(jnp.mean(center * center, axis=-1, keepdims=True) + EPSILON)
    return center * inv_std, inv_std


def norm_backward(grad_out, norm_gain, scaled, inv_std):
    weighted = grad_out * norm_gain
    return inv_std * (
        weighted
        - jnp.mean(weighted, axis=-1, keepdims=True)
        - scaled * jnp.mean(weighted * scaled, axis=-1, keepdims=True)
    )


def project_kernel(s_ref, x_ref, vec_ref, w_ref, normed_ref, proj_ref):
    scaled, _ = norm_stats(x_ref[...].astype(F32))
    normed = (scaled * vec_ref[0:1, :] + vec_ref[1:2, :]).astype(BF16)
    normed_ref[...] = normed.T
    for c in range(3):
        part = dot_nn(normed, w_ref[c]).astype(BF16)
        for n, tile in enumerate(lane_tiles(part)):
            start = (3 * n + c) * LANES
            proj_ref[:, start : start + LANES] = tile


def project(scalars, x, vectors, weights):
    rows, width = x.shape
    cols = 3 * width // 2
    return pl.pallas_call(
        project_kernel,
        grid_spec=pltpu.PrefetchScalarGridSpec(
            num_scalar_prefetch=1,
            grid=(1,),
            in_specs=[
                once((rows, width), lambda i, s: (0, 0)),
                still(vectors),
                once((3, width, width // 2), lambda i, s: (0, 0, s[0])),
            ],
            out_specs=[
                once((width, rows), lambda i, s: (0, 0)),
                once((rows, cols), lambda i, s: (0, 0)),
            ],
        ),
        out_shape=[
            jax.ShapeDtypeStruct((width, rows), BF16),
            jax.ShapeDtypeStruct((rows, cols), BF16),
        ],
        compiler_params=params(62),
        cost_estimate=CHEAP,
        name="project",
    )(scalars, x, vectors, weights)


def store_parts(flag, parts, keep_ref, send_ref):
    first = jnp.concatenate(parts[0], axis=0).astype(BF16)
    second = jnp.concatenate(parts[1], axis=0).astype(BF16)
    keep_ref[...] = jnp.where(flag == 0, first, second).reshape(keep_ref.shape)
    send_ref[...] = jnp.where(flag == 0, second, first).reshape(send_ref.shape)


def only_head(values, head):
    lane = lax.broadcasted_iota(jnp.int32, values.shape, 1)
    return jnp.where((lane // HEAD_DIM) == head, values, jnp.zeros_like(values))


def load_natural(member, blocks, dest, size, shift=0):
    for slot, block in enumerate(blocks):
        start = pl.multiple_of(lax.bitwise_xor(member, slot) * size, 8) + shift
        start = pl.multiple_of(start, 8)
        dest[pl.ds(start, size), :] = block.astype(dest.dtype)


def attend_kernel(
    m_ref, p0, p1, p2, p3, taps_ref, mixed_ref, own_ref, send_ref, lse_ref, pj, kh, vt, on, qs
):
    member = m_ref[1]
    size = p0.shape[0]
    length = 4 * size
    scale = jnp.asarray(HEAD_DIM ** (-0.5), BF16)
    for c in range(3):
        cols = slice(c * LANES, (c + 1) * LANES)
        pj[c, 0:8, :] = jnp.zeros((8, LANES), F32)
        load_natural(member, [p[:, cols] for p in (p0, p1, p2, p3)], pj.at[c], size, 8)
    for c in range(3):
        total = taps_ref[0, 3 * c : 3 * c + 1, :] * pj[c, 8 : 8 + length, :]
        total = total + taps_ref[0, 3 * c + 1 : 3 * c + 2, :] * pj[c, 7 : 7 + length, :]
        total = total + taps_ref[0, 3 * c + 2 : 3 * c + 3, :] * pj[c, 6 : 6 + length, :]
        mixed = total.astype(BF16)
        mixed_ref[:, c * LANES : (c + 1) * LANES] = mixed
        if c == 0:
            qs[...] = mixed * scale
        elif c == 1:
            kh[0] = only_head(mixed, 0)
            kh[1] = only_head(mixed, 1)
        else:
            vt[...] = mixed.T
    def scores_of(first, head):
        keys = first + QBLOCK
        scores = dot_nt(kh[head, 0:keys, :], qs[first:keys, :])
        key_pos = lax.broadcasted_iota(jnp.int32, (QBLOCK, QBLOCK), 0)
        query_pos = lax.broadcasted_iota(jnp.int32, (QBLOCK, QBLOCK), 1)
        corner = jnp.where(key_pos <= query_pos, scores[first:keys, :], NEGATIVE)
        return jnp.concatenate([scores[:first, :], corner], axis=0) if first else corner

    jobs = [(first, head) for first in reversed(range(0, length, QBLOCK)) for head in range(2)]
    ahead = 2
    ready = [scores_of(*job) for job in jobs[:ahead]]
    outs = []
    for n, (first, head) in enumerate(jobs):
        if n + ahead < len(jobs):
            ready.append(scores_of(*jobs[n + ahead]))
        scores = ready[n]
        keys = first + QBLOCK
        top = jnp.max(scores, axis=0, keepdims=True)
        weights = jnp.exp(scores - top)
        total = jnp.sum(weights, axis=0, keepdims=True)
        part = dot_nn(vt[head * HEAD_DIM : (head + 1) * HEAD_DIM, 0:keys], weights.astype(BF16))
        outs.append(part * (1.0 / total))
        lse_ref[0, head : head + 1, first:keys] = top + jnp.log(total)
        if head == 1:
            on[first:keys, :] = jnp.concatenate(outs, axis=0).T.astype(BF16)
            outs = []
    for slot in range(4):
        start = pl.multiple_of(lax.bitwise_xor(member, slot) * size, size)
        block = on[pl.ds(start, size), :]
        dest = (own_ref, send_ref)[slot % 2]
        dest[slot // 2 * size : (slot // 2 + 1) * size, :] = block


def attend(member, proj, taps):
    size = proj[0].shape[0]
    pairs = proj[0].shape[1] // (3 * LANES)
    length = 4 * size
    width = pairs * LANES
    return pl.pallas_call(
        attend_kernel,
        grid=(pairs,),
        in_specs=[SMEM_SPEC]
        + [pl.BlockSpec((size, 3 * LANES), lambda p: (0, p))] * 4
        + [pl.BlockSpec((1, 16, LANES), lambda p: (p, 0, 0))],
        out_specs=[
            pl.BlockSpec((length, 3 * LANES), lambda p: (0, p)),
            pl.BlockSpec((2 * size, LANES), lambda p: (0, p)),
            pl.BlockSpec((2 * size, LANES), lambda p: (0, p)),
            pl.BlockSpec((1, 2, length), lambda p: (p, 0, 0)),
        ],
        out_shape=[
            jax.ShapeDtypeStruct((length, 3 * width), BF16),
            jax.ShapeDtypeStruct((2 * size, width), BF16),
            jax.ShapeDtypeStruct((2 * size, width), BF16),
            jax.ShapeDtypeStruct((pairs, 2, length), F32),
        ],
        scratch_shapes=[
            pltpu.VMEM((3, 8 + length, LANES), F32),
            pltpu.VMEM((2, length, LANES), BF16),
            pltpu.VMEM((LANES, length), BF16),
            pltpu.VMEM((length, LANES), BF16),
            pltpu.VMEM((length, LANES), BF16),
        ],
        compiler_params=params(62),
        cost_estimate=CHEAP,
        name="attend",
    )(member, *proj, taps)


def attend_back_kernel(
    m_ref,
    p0,
    p1,
    p2,
    p3,
    mixed_ref,
    lse_ref,
    taps_ref,
    own_ref,
    send_ref,
    down_ref,
    drecv_ref,
    n0,
    n1,
    n2,
    n3,
    gown_ref,
    gsend_ref,
    gconv_ref,
    keep_ref,
    give_ref,
    pj,
    dm,
    qh,
    doh,
    kt,
    dl,
    dqa,
    nat,
    gp,
    nv,
    sems,
):
    member = m_ref[1]
    size = p0.shape[0]
    length = 4 * size
    scale = jnp.asarray(HEAD_DIM ** (-0.5), BF16)
    halves = [slice(0, size), slice(size, 2 * size)]
    copies = []
    for slot, norm in enumerate((n0, n1, n2, n3)):
        copies.append(pltpu.make_async_copy(norm, nv.at[slot], sems.at[slot]))
        copies[slot].start()
    load_natural(
        member,
        [own_ref[halves[0]], send_ref[halves[0]], own_ref[halves[1]], send_ref[halves[1]]],
        nat.at[0],
        size,
    )
    load_natural(
        member,
        [down_ref[halves[0]], drecv_ref[halves[0]], down_ref[halves[1]], drecv_ref[halves[1]]],
        nat.at[1],
        size,
    )
    grads = nat[1]
    product = (grads.astype(F32) * nat[0].astype(F32)).T
    for head in range(2):
        dl[head : head + 1, :] = jnp.sum(
            product[head * HEAD_DIM : (head + 1) * HEAD_DIM, :], axis=0, keepdims=True
        )
        doh[head] = only_head(grads, head)
        qh[head] = only_head(mixed_ref[:, 0:LANES], head) * scale
    kt[...] = mixed_ref[:, LANES : 2 * LANES].T
    for c in range(3):
        cols = slice(c * LANES, (c + 1) * LANES)
        pj[c, 0:8, :] = jnp.zeros((8, LANES), F32)
        dm[c, length : length + 8, :] = jnp.zeros((8, LANES), F32)
        load_natural(member, [p[:, cols] for p in (p0, p1, p2, p3)], pj.at[c], size, 8)
    def products(first, head):
        keys = mixed_ref[first : first + KBLOCK, LANES : 2 * LANES]
        values = mixed_ref[first : first + KBLOCK, 2 * LANES : 3 * LANES]
        scores = dot_nt(keys, qh[head, first:, :])
        key_pos = lax.broadcasted_iota(jnp.int32, (KBLOCK, KBLOCK), 0)
        query_pos = lax.broadcasted_iota(jnp.int32, (KBLOCK, KBLOCK), 1)
        corner = jnp.where(key_pos <= query_pos, scores[:, :KBLOCK], NEGATIVE)
        if first + KBLOCK < length:
            corner = jnp.concatenate([corner, scores[:, KBLOCK:]], axis=1)
        return corner, dot_nt(values, doh[head, first:, :])

    jobs = [(first, head) for first in range(0, length, KBLOCK) for head in range(2)]
    ahead = 1
    ready = [products(*job) for job in jobs[:ahead]]
    for n, (first, head) in enumerate(jobs):
        if n + ahead < len(jobs):
            ready.append(products(*jobs[n + ahead]))
        scores, grad_probs = ready[n]
        probs = jnp.exp(scores - lse_ref[0, head : head + 1, first:])
        grad_scores = (probs * (grad_probs - dl[head : head + 1, first:])).astype(BF16)
        part_v = dot_nn(probs.astype(BF16), doh[head, first:, :])
        part_k = dot_nn(grad_scores, qh[head, first:, :])
        lanes = slice(head * HEAD_DIM, (head + 1) * HEAD_DIM)
        part_q = dot_nn(kt[lanes, first : first + KBLOCK], grad_scores)
        if first == 0:
            dqa[lanes, :] = part_q
        else:
            dqa[lanes, first:] += part_q
        if head == 0:
            sum_v, sum_k = part_v, part_k
        else:
            dm[1, first : first + KBLOCK, :] = sum_k + part_k
            dm[2, first : first + KBLOCK, :] = sum_v + part_v
    dm[0, 0:length, :] = dqa[...].T * HEAD_DIM ** (-0.5)
    for c in range(3):
        grad = dm[c, 0:length, :]
        for s in range(3):
            gconv_ref[3 * c + s : 3 * c + s + 1, :] = jnp.sum(
                grad * pj[c, 8 - s : 8 - s + length, :], axis=0, keepdims=True
            )
        total = taps_ref[0, 3 * c : 3 * c + 1, :] * grad
        total = total + taps_ref[0, 3 * c + 1 : 3 * c + 2, :] * dm[c, 1 : 1 + length, :]
        total = total + taps_ref[0, 3 * c + 2 : 3 * c + 3, :] * dm[c, 2 : 2 + length, :]
        gp[:, c * LANES : (c + 1) * LANES] = total.astype(BF16)
    total = None
    for slot in range(4):
        copies[slot].wait()
        start = pl.multiple_of(lax.bitwise_xor(member, slot) * size, size)
        dest = (gown_ref, gsend_ref)[slot % 2]
        block = gp[pl.ds(start, size), :]
        dest[slot // 2 * size : (slot // 2 + 1) * size, :] = block
        part = dot_nn(nv[slot], block)
        total = part if total is None else total + part
    rows = total.shape[0] // 8
    store_parts(
        m_ref[3],
        [
            [
                tile
                for b in (x, x + 4, x + 2, x + 6)
                for tile in lane_tiles(total[b * rows : (b + 1) * rows])
            ]
            for x in range(2)
        ],
        keep_ref,
        give_ref,
    )


def attend_back(pair, member, proj, mixed, lse, taps, own, send, grad_own, grad_recv, normed):
    size = proj[0].shape[0]
    length = 4 * size
    width = normed[0].shape[0]
    part = jax.ShapeDtypeStruct((2, 2, 3 * width // 8, LANES), BF16)
    half_spec = pl.BlockSpec((2 * size, LANES), lambda i: (0, pair))
    return pl.pallas_call(
        attend_back_kernel,
        grid=(1,),
        in_specs=[SMEM_SPEC]
        + [pl.BlockSpec((size, 3 * LANES), lambda i: (0, pair))] * 4
        + [
            pl.BlockSpec((length, 3 * LANES), lambda i: (0, pair)),
            pl.BlockSpec((1, 2, length), lambda i: (pair, 0, 0)),
            pl.BlockSpec((1, 16, LANES), lambda i: (pair, 0, 0)),
        ]
        + [half_spec] * 4
        + [pl.BlockSpec(memory_space=pltpu.HBM)] * 4,
        out_specs=[
            pl.BlockSpec((2 * size, 3 * LANES), lambda i: (0, 0)),
            pl.BlockSpec((2 * size, 3 * LANES), lambda i: (0, 0)),
            pl.BlockSpec((16, LANES), lambda i: (0, 0)),
            pl.BlockSpec(part.shape, lambda i: (0, 0, 0, 0)),
            pl.BlockSpec(part.shape, lambda i: (0, 0, 0, 0)),
        ],
        out_shape=[
            jax.ShapeDtypeStruct((2 * size, 3 * LANES), BF16),
            jax.ShapeDtypeStruct((2 * size, 3 * LANES), BF16),
            jax.ShapeDtypeStruct((16, LANES), F32),
            part,
            part,
        ],
        scratch_shapes=[
            pltpu.VMEM((3, 8 + length, LANES), F32),
            pltpu.VMEM((3, 8 + length, LANES), F32),
            pltpu.VMEM((2, length, LANES), BF16),
            pltpu.VMEM((2, length, LANES), BF16),
            pltpu.VMEM((LANES, length), BF16),
            pltpu.VMEM((8, length), F32),
            pltpu.VMEM((LANES, length), F32),
            pltpu.VMEM((2, length, LANES), BF16),
            pltpu.VMEM((length, 3 * LANES), BF16),
            pltpu.VMEM((4, width, size), BF16),
            pltpu.SemaphoreType.DMA((4,)),
        ],
        compiler_params=params(62),
        cost_estimate=CHEAP,
        name="attend_back",
    )(member, *proj, mixed, lse, taps, own, send, grad_own, grad_recv, *normed)


def canonical(flag, own_ref, recv_ref):
    own = own_ref[...]
    recv = recv_ref[...]
    return jnp.concatenate(
        [jnp.where(flag == 0, own, recv), jnp.where(flag == 0, recv, own)], axis=1
    )


def ffn_kernel(
    s_ref,
    hown_ref,
    hrecv_ref,
    wout_ref,
    tok0,
    tok1,
    cot0,
    cot1,
    vec_ref,
    up_ref,
    down_ref,
    out0,
    out1,
    down_keep,
    down_send,
    gres_ref,
    gown_ref,
    gsend_ref,
    sums_ref,
    up_keep,
    up_send,
    relus,
    res,
    nf,
    nft,
    gf,
    acc,
):
    step = pl.program_id(0)
    size = tok0.shape[0]
    core = s_ref[0]
    halves = ((0, s_ref[1] * size), (size, lax.bitwise_xor(s_ref[1], 2) * size))

    def valid(start):
        row = start + lax.broadcasted_iota(jnp.int32, tok0.shape, 0)
        return row < s_ref[2]

    def store(grad):
        rows = grad.shape[0] // 32
        store_parts(
            core,
            [
                [
                    tile
                    for place in range(16)
                    for chunk in [
                        bit
                        + (place >> 3 & 1) * 2
                        + (place >> 2 & 1) * 4
                        + (place >> 1 & 1) * 8
                        + (place & 1) * 16
                    ]
                    for tile in lane_tiles(grad[chunk * rows : (chunk + 1) * rows])
                ]
                for bit in range(2)
            ],
            up_keep,
            up_send,
        )

    @pl.when(step == 0)
    def _():
        attended = dot_nn(canonical(core, hown_ref, hrecv_ref), wout_ref[...])
        for tok, cot, (first, start) in zip((tok0, tok1), (cot0, cot1), halves):
            rows = slice(first, first + size)
            residual = tok[...].astype(F32) + attended[rows]
            res[rows, :] = residual
            scaled, _ = norm_stats(residual)
            nf[rows, :] = (scaled * vec_ref[2:3, :] + vec_ref[3:4, :]).astype(BF16)
            grad = cot[...].reshape(tok.shape)
            gf[rows, :] = jnp.where(valid(start), grad, jnp.zeros_like(grad))
        sums_ref[6:7, :] = jnp.sum(gf[...].astype(F32), axis=0, keepdims=True)
        sums_ref[7:8, :] = jnp.zeros_like(sums_ref[7:8, :])
        acc[...] = jnp.zeros_like(acc)

    @pl.when(step < 4)
    def _():
        relu = jnp.maximum(dot_nn(nf[...], up_ref[...]) + vec_ref[pl.ds(5 + step, 1), :], 0.0)
        relus[step] = relu
        act = (relu * relu).astype(BF16)
        acc[...] += dot_nn(act, down_ref[...])
        grad = dot_tn(act, gf[...])
        rows = grad.shape[0] // 8
        store_parts(
            core,
            [
                [
                    tile
                    for chunk in (bit, bit + 4, bit + 2, bit + 6)
                    for tile in lane_tiles(grad[chunk * rows : (chunk + 1) * rows])
                ]
                for bit in range(2)
            ],
            down_keep,
            down_send,
        )

    @pl.when(step == 3)
    def _():
        for out, (first, start) in zip((out0, out1), halves):
            rows = slice(first, first + size)
            total = res[rows, :] + (acc[rows, :] + vec_ref[4:5, :])
            out[...] = jnp.where(valid(start), total, 0.0).astype(BF16).reshape(out.shape)
        nft[...] = nf[...].T
        acc[...] = jnp.zeros_like(acc)

    @pl.when((step >= 4) & (step < 8))
    def _():
        grad_act = dot_nt(gf[...], down_ref[...])
        grad_pre = (2.0 * relus[step - 4] * grad_act).astype(BF16)
        sums_ref[pl.ds(step - 4, 1), :] = jnp.sum(grad_pre.astype(F32), axis=0, keepdims=True)
        acc[...] += dot_nt(grad_pre, up_ref[...])
        store(dot_nn(nft[...], grad_pre))

    @pl.when(step == 8)
    def _():
        scaled, inv_std = norm_stats(res[...])
        grad = acc[...]
        sums_ref[4:5, :] = jnp.sum(grad * scaled, axis=0, keepdims=True)
        sums_ref[5:6, :] = jnp.sum(grad, axis=0, keepdims=True)
        total = gf[...].astype(F32) + norm_backward(grad, vec_ref[2:3, :], scaled, inv_std)
        gres_ref[...] = total
        attended = total.astype(BF16)
        heads = dot_nt(attended, wout_ref[...]).astype(BF16)
        middle = heads.shape[1] // 2
        gown_ref[...] = jnp.where(core == 0, heads[:, :middle], heads[:, middle:])
        gsend_ref[...] = jnp.where(core == 0, heads[:, middle:], heads[:, :middle])
        store(dot_tn(canonical(core, hown_ref, hrecv_ref), attended))


def ffn(scalars, hown, hrecv, wout, toks, cots, vectors, up, down):
    rows = 2 * toks[0].shape[0]
    width, ff = up.shape
    tile = ff // 4
    assert tile == width
    down_part = jax.ShapeDtypeStruct((2, 2, 2, 2, tile // 8 * width // LANES, LANES), BF16)
    block = width // 32 * tile // LANES
    up_part = jax.ShapeDtypeStruct((2, 2, 2, 2, 5 * block, LANES), BF16)

    def forward(j):
        return jnp.minimum(j, 3)

    def backward(j):
        return jnp.maximum(j - 4, 0)

    def either(j):
        return jnp.where(j < 4, j, jnp.minimum(j - 4, 3))

    down_spec = pl.BlockSpec(
        (2, 2, 1, 1) + down_part.shape[4:],
        lambda j, _: (0, 0, lax.rem(forward(j), 2), lax.div(forward(j), 2), 0, 0),
    )
    up_spec = pl.BlockSpec((2, 2, 2, 2, block, LANES), lambda j, _: (0, 0, 0, 0, backward(j), 0))
    token_block = jax.ShapeDtypeStruct(toks[0].shape, BF16)
    half = jax.ShapeDtypeStruct(hown.shape, BF16)
    return pl.pallas_call(
        ffn_kernel,
        grid_spec=pltpu.PrefetchScalarGridSpec(
            num_scalar_prefetch=1,
            grid=(9,),
            in_specs=[still(a) for a in (hown, hrecv, wout, *toks)]
            + [
                once((1,) + cots[0].shape[1:], lambda j, s: (s[4], 0, 0)),
                still(cots[1]),
                still(vectors),
                pl.BlockSpec((width, tile), lambda j, _: (0, either(j))),
                pl.BlockSpec((tile, width), lambda j, _: (either(j), 0)),
            ],
            out_specs=[
                once((1,) + token_block.shape, lambda j, s: (s[4], 0, 0)),
                once(token_block.shape, lambda j, _: (0, 0)),
                down_spec,
                down_spec,
                once((rows, width), lambda j, _: (0, 0)),
                once(half.shape, lambda j, _: (0, 0)),
                once(half.shape, lambda j, _: (0, 0)),
                pl.BlockSpec((8, width), lambda j, _: (0, 0)),
                up_spec,
                up_spec,
            ],
            scratch_shapes=[
                pltpu.VMEM((4, rows, tile), F32),
                pltpu.VMEM((rows, width), F32),
                pltpu.VMEM((rows, width), BF16),
                pltpu.VMEM((width, rows), BF16),
                pltpu.VMEM((rows, width), BF16),
                pltpu.VMEM((rows, width), F32),
            ],
        ),
        out_shape=[
            jax.ShapeDtypeStruct((2,) + token_block.shape, BF16),
            token_block,
            down_part,
            down_part,
            jax.ShapeDtypeStruct((rows, width), F32),
            half,
            half,
            jax.ShapeDtypeStruct((8, width), F32),
            up_part,
            up_part,
        ],
        compiler_params=params(63),
        cost_estimate=CHEAP,
        name="ffn",
    )(scalars, hown, hrecv, wout, *toks, *cots, vectors, up, down)


def input_grad_kernel(
    s_ref, o0, o1, o2, r0, r1, r2, w_ref, xp_ref, xo_ref, gres_ref, vec_ref, early_ref, *refs
):
    convs, (pair_ref, own_ref, sums_ref, buf) = refs[:3], refs[3:]
    step = pl.program_id(0)
    for n, ref in enumerate((o0, o1, o2, r0, r1, r2)):
        side = s_ref[0] if n < 3 else 1 - s_ref[0]
        start = pl.multiple_of((side * 3 + n % 3) * LANES, LANES)
        for c, tile in enumerate(lane_tiles(ref[...])):
            buf[c, :, pl.ds(start, LANES)] = tile
    grad = dot_nt(buf[0], w_ref[0]) + dot_nt(buf[1], w_ref[1]) + dot_nt(buf[2], w_ref[2])
    x = jnp.where(step < 2, xp_ref[...], xo_ref[...])
    scaled, inv_std = norm_stats(x.astype(F32))

    @pl.when(step == 0)
    def _():
        sums_ref[...] = jnp.zeros_like(sums_ref)
        sums_ref[0:8, :] = early_ref[...]
        for n, conv in enumerate(convs):
            start = pl.multiple_of((s_ref[0] * 3 + n) * LANES, LANES)
            sums_ref[8:17, pl.ds(start, LANES)] = conv[0:9, :]

    sums_ref[17:18, :] += jnp.sum(grad * scaled, axis=0, keepdims=True)
    sums_ref[18:19, :] += jnp.sum(grad, axis=0, keepdims=True)
    total = gres_ref[...] + norm_backward(grad, vec_ref[0:1, :], scaled, inv_std)
    total = total.astype(BF16)

    @pl.when(step < 2)
    def _():
        pair_ref[...] = total

    @pl.when(step >= 2)
    def _():
        own_ref[0] = total


def input_grad(scalars, owns, recvs, weights, x_pair, x_own, grad_residual, vectors, early, convs):
    rows, width = x_own.shape
    tile = rows // 2
    flipped = lambda i, _: (jnp.where(i < 2, i + 2, i - 2), 0)
    first = lambda i: jnp.minimum(i, 1)
    second = lambda i: jnp.maximum(i - 2, 0)
    return pl.pallas_call(
        input_grad_kernel,
        grid_spec=pltpu.PrefetchScalarGridSpec(
            num_scalar_prefetch=1,
            grid=(4,),
            in_specs=[pl.BlockSpec((tile, 3 * LANES), flipped)] * 6
            + [
                still(weights),
                pl.BlockSpec((tile, width), lambda i, _: (first(i), 0)),
                pl.BlockSpec((tile, width), lambda i, _: (second(i), 0)),
                pl.BlockSpec((tile, width), flipped),
                still(vectors),
                still(early),
            ]
            + [still(a) for a in convs],
            out_specs=[
                pl.BlockSpec((tile, width), lambda i, _: (first(i), 0)),
                pl.BlockSpec((1, tile, width), lambda i, s: (s[4], second(i), 0)),
                pl.BlockSpec((24, width), lambda i, _: (0, 0)),
            ],
            scratch_shapes=[pltpu.VMEM((3, tile, width), BF16)],
        ),
        out_shape=[
            jax.ShapeDtypeStruct((rows, width), BF16),
            jax.ShapeDtypeStruct((2, rows, width), BF16),
            jax.ShapeDtypeStruct((24, width), F32),
        ],
        compiler_params=params(62),
        cost_estimate=CHEAP,
        name="input_grad",
    )(
        scalars,
        *owns,
        *recvs,
        weights,
        x_pair,
        x_own,
        grad_residual,
        vectors,
        early,
        *convs,
    )


FREE, ONE, MINE, OTHER = range(4)
BIT_AT = (4, 3, 5, 6)


class Segment:
    def __init__(self, arrays, first, rows):
        self.rows = rows
        self.parts = [(array, self.fresh(array), first) for array in arrays]

    @staticmethod
    def fresh(array):
        return [FREE if n == 2 else ONE for n in array.shape[:4]]

    def chosen(self, dim):
        found = []
        for array, marks, first in self.parts:
            marks = list(marks)
            if dim is not None and marks[dim] == FREE:
                marks[dim] = OTHER
            found.append((array, tuple(marks), first, self.rows))
        return found

    def settle(self, dim, arrived, first):
        parts = []
        for array, marks, own_first in self.parts:
            marks = list(marks)
            if marks[dim] == FREE:
                marks[dim] = MINE
            parts.append((array, marks, own_first))
        self.parts = parts + [(arrived, self.fresh(arrived), first)]


def settle(segments, dim, arrived):
    first = 0
    for segment in segments:
        segment.settle(dim, arrived, first)
        first += segment.rows


def sum_kernel(plan, finish, count, made, s_ref, *refs):
    pieces = [p for parts in plan for p in parts]
    arrays, outs, bufs = refs[:count], refs[count : count + made], refs[count + made : -1]
    sems = refs[-1]
    staged = bufs[len(pieces) :]
    results = []

    def send(n):
        if staged:
            copy = pltpu.make_async_copy(staged[n], outs[n], sems.at[len(pieces) + n])
            copy.start()
            results.append(copy)

    copies = []
    for n, (place, marks, first, rows) in enumerate(pieces):
        where = []
        for dim, mark in enumerate(marks):
            bit = s_ref[BIT_AT[dim]]
            start = {FREE: 0, ONE: 0, MINE: bit, OTHER: 1 - bit}[mark]
            where.append(pl.ds(start, 2 if mark == FREE else 1))
        source = arrays[place].at[tuple(where) + (pl.ds(first, rows), slice(None))]
        copies.append(pltpu.make_async_copy(source, bufs[n], sems.at[n]))
        copies[-1].start()
    n = 0
    totals = []
    for parts in plan:
        own = bufs[n : n + len(parts)]
        pending = copies[n : n + len(parts)]
        n += len(parts)

        def total(lead, rows, own=own, pending=pending):
            while pending:
                pending.pop(0).wait()
            value = None
            for buf in own:
                piece = buf[lead + (rows, slice(None))].astype(F32)
                value = piece if value is None else value + piece
            return value

        totals.append(total)
    finish(s_ref, totals, staged or outs, send)
    for copy in results:
        copy.wait()


def sum_call(scalars, segments, dims, finish, out_shape, name, cost=BUSY, stream=False):
    arrays, plan, scratch = [], [], []
    for segment, dim in zip(segments, dims):
        parts = []
        for array, marks, first, rows in segment.chosen(dim):
            place = next((n for n, a in enumerate(arrays) if a is array), None)
            if place is None:
                place = len(arrays)
                arrays.append(array)
            parts.append((place, marks, first, rows))
            sizes = tuple(2 if mark == FREE else 1 for mark in marks)
            scratch.append(pltpu.VMEM(sizes + (rows, LANES), BF16))
        plan.append(parts)
    whole = lambda shape: pl.BlockSpec(shape, lambda i: (0,) * len(shape))
    sems = len(scratch)
    if stream:
        whole = lambda _: pl.BlockSpec(memory_space=pltpu.HBM)
        scratch += [pltpu.VMEM(o.shape, o.dtype) for o in out_shape]
        sems += len(out_shape)
    return pl.pallas_call(
        functools.partial(sum_kernel, plan, finish, len(arrays), len(out_shape)),
        grid=(1,),
        in_specs=[SMEM_SPEC] + [pl.BlockSpec(memory_space=pltpu.HBM)] * len(arrays),
        out_specs=[whole(o.shape) for o in out_shape],
        out_shape=out_shape,
        scratch_shapes=scratch + [pltpu.SemaphoreType.DMA((sems,))],
        compiler_params=params(62),
        cost_estimate=cost,
        name=name,
    )(scalars, *arrays)


def outgoing(scalars, groups, dims, cost=CHEAP):
    shapes = []
    for group, dim in zip(groups, dims):
        marks = [group[0].chosen(dim)[0][1]]
        sizes = tuple(2 if mark == FREE else 1 for mark in marks[0])
        shapes.append(jax.ShapeDtypeStruct(sizes + (sum(g.rows for g in group), LANES), BF16))

    def finish(s_ref, totals, outs, send):
        n = 0
        for place, (group, out) in enumerate(zip(groups, outs)):
            first = 0
            for segment in group:
                for lead in itertools.product(*[range(size) for size in out.shape[:4]]):
                    for row in range(0, segment.rows, 144):
                        value = totals[n](lead, slice(row, row + 144))
                        out[lead + (slice(first + row, first + row + 144), slice(None))] = (
                            value.astype(BF16)
                        )
                first += segment.rows
                n += 1
            send(place)

    segments = [segment for group in groups for segment in group]
    each = [dim for group, dim in zip(groups, dims) for _ in group]
    return sum_call(scalars, segments, each, finish, shapes, "stage_sum", cost, True)


def hop(value, stage):
    return lax.ppermute(value, stage[0], stage[1])


def ffn_plain(heads, toks, cot, valid, wout, gain, bias, up, upb, down, downb):
    residual = toks.astype(F32) + jnp.dot(heads, wout, preferred_element_type=F32)
    scaled, inv_std = norm_stats(residual)
    normed = (scaled * gain + bias).astype(BF16)
    relu = jnp.maximum(jnp.dot(normed, up, preferred_element_type=F32) + upb, 0.0)
    act = jnp.square(relu).astype(BF16)
    out = jnp.dot(act, down, preferred_element_type=F32) + downb
    result = jnp.where(valid, residual + out, 0.0).astype(BF16)
    grad_ffn = jnp.where(valid, cot, jnp.zeros_like(cot))
    grad_y = grad_ffn.astype(F32)
    grad_act = jnp.einsum("td,fd->tf", grad_ffn, down, preferred_element_type=F32)
    grad_pre = (2.0 * relu * grad_act).astype(BF16)
    grad = jnp.einsum("tf,df->td", grad_pre, up, preferred_element_type=F32)
    sums = jnp.stack([jnp.sum(grad * scaled, axis=0), jnp.sum(grad, axis=0)])
    grad_residual = grad_y + norm_backward(grad, gain, scaled, inv_std)
    attended = grad_residual.astype(BF16)
    grad_heads = jnp.einsum("td,ed->te", attended, wout, preferred_element_type=F32)
    return (
        result,
        grad_residual,
        grad_heads.astype(BF16),
        sums,
        jnp.sum(grad_pre.astype(F32), axis=0),
        jnp.sum(grad_y, axis=0),
        jnp.einsum("td,tf->df", normed, grad_pre, preferred_element_type=F32),
        jnp.einsum("tf,td->fd", act, grad_ffn, preferred_element_type=F32),
        jnp.einsum("te,td->ed", heads, attended, preferred_element_type=F32),
    )


def on_device(
    tokens,
    cotangent,
    lengths,
    pre_attn_gain,
    pre_attn_bias,
    qkv_weight,
    conv_weight,
    out_weight,
    pre_ffn_gain,
    pre_ffn_bias,
    up_weight,
    up_bias,
    down_weight,
    down_bias,
):
    groups = lax.axis_size("mp")
    batch_groups = lax.axis_size("batch")
    devices = groups * batch_groups
    member = lax.axis_index("mp").astype(jnp.int32)
    batch = lax.axis_index("batch").astype(jnp.int32)
    seqs, rows, width = tokens.shape
    ff = up_weight.shape[1]
    middle = width // 2
    quarter = width // groups
    pairs = middle // LANES
    taps = conv_weight.shape[1]
    assert groups == 4 and seqs == 2 and pairs == 3 and taps == 3
    fast = batch_groups == 8 and (width // devices) % 8 == 0
    half = lax.shift_right_logical(member, 1)
    core = lax.bitwise_and(member, 1)
    x_bit = lax.bitwise_and(batch, 1)
    z0_bit = lax.bitwise_and(lax.shift_right_logical(batch, 1), 1)
    z1_bit = lax.shift_right_logical(batch, 2)
    vectors = (pre_attn_gain, pre_attn_bias, pre_ffn_gain, pre_ffn_bias, down_bias, up_bias)
    vectors = jnp.concatenate(vectors).astype(F32).reshape(5 + ff // width, width)

    def swap_core(value):
        return lax.ppermute(value, "mp", CORE)

    def swap_pair(value):
        return lax.ppermute(value, "mp", PAIR)

    def pick(value, index):
        starts = (index,) + (jnp.int32(0),) * (value.ndim - 1)
        return lax.dynamic_slice(value, starts, (1,) + value.shape[1:])[0]

    length = pick(lengths, half)
    scalars = jnp.stack([core, member, length, x_bit, half, z0_bit, z1_bit]).astype(jnp.int32)

    hops = [("mp", PAIR)] + [
        ("batch", [(i, i ^ flip) for i in range(batch_groups)]) for flip in (1, 2, 4)
    ]
    DY, DX, DZ0, DZ1 = range(4)
    tie = lax.optimization_barrier

    tok_pair = swap_pair(pick(tokens, 1 - half))
    tok_own = pick(tokens, half)
    tok_core = swap_core(tok_own)
    taps_own = lax.dynamic_slice_in_dim(conv_weight, core * middle, middle, 2).astype(F32)
    taps_own = taps_own.reshape(3 * taps, pairs, LANES).transpose(1, 0, 2)
    taps_own = jnp.pad(taps_own, ((0, 0), (0, 16 - 3 * taps), (0, 0)))

    def norm_project(block):
        return project(scalars, block, vectors, qkv_weight)

    first = norm_project(tok_own)
    tok_core, cot_send, taps_own = tie((tok_core, pick(cotangent, 1 - half), taps_own))
    second = norm_project(tok_core)
    tok_pair, first, second = tie((tok_pair, first, second))
    tok_cross = swap_core(tok_pair)
    third = norm_project(tok_pair)
    tok_cross, third = tie((tok_cross, third))
    fourth = norm_project(tok_cross)
    cot_send, fourth = tie((cot_send, fourth))
    cot_pair = swap_pair(cot_send)
    normed, proj = zip(first, second, third, fourth)
    mixed, heads_own, heads_send, lse = attend(scalars, proj, taps_own)
    heads_recv = swap_core(heads_send)

    if fast:
        (
            result_all,
            result_give,
            down_keep,
            down_send,
            grad_residual,
            grad_own,
            grad_send,
            early,
            up_keep,
            up_send,
        ) = ffn(
            scalars,
            heads_own,
            heads_recv,
            out_weight,
            (tok_own, tok_pair),
            (cotangent, cot_pair),
            vectors,
            up_weight,
            down_weight,
        )
    else:
        row = jnp.arange(rows, dtype=jnp.int32)
        row_pos = [member * rows + row, jnp.bitwise_xor(member, 2) * rows + row]
        heads_all = jnp.concatenate(
            [
                jnp.where(core == 0, heads_own, heads_recv),
                jnp.where(core == 0, heads_recv, heads_own),
            ],
            axis=1,
        )
        (
            result,
            grad_residual,
            grad_heads,
            sums_ffn,
            sums_up,
            sums_down,
            grad_up,
            grad_down,
            grad_out,
        ) = ffn_plain(
            heads_all,
            jnp.concatenate([tok_own, tok_pair], axis=0),
            jnp.concatenate([pick(cotangent, half), cot_pair], axis=0),
            (jnp.concatenate(row_pos) < length)[:, None],
            out_weight,
            vectors[2:3],
            vectors[3:4],
            up_weight,
            vectors[5:].reshape(1, ff),
            down_weight,
            vectors[4:5],
        )
        result_all, result_give = jnp.stack([result[:rows]] * 2), result[rows:]
        early = [sums_up.reshape(ff // width, width), sums_ffn, sums_down[None]]
        early = jnp.concatenate(early + [jnp.zeros((1, width), F32)], axis=0)
        grad_own = lax.dynamic_slice_in_dim(grad_heads, core * middle, middle, 1)
        grad_send = lax.dynamic_slice_in_dim(grad_heads, (1 - core) * middle, middle, 1)
    grad_recv = swap_core(grad_send)
    if fast:
        down_recv = swap_core(down_send)
        grad_recv, down_recv, up_send = tie((grad_recv, down_recv, up_send))
        up_recv = swap_core(up_send)
        down_rows = down_keep.shape[4]
        up_rows = up_keep.shape[4]
        each = (down_rows + up_rows) // 3
        down = (down_keep, down_recv)
        up = (up_keep, up_recv)
        rest = down_rows - each
        down_a, down_b = Segment(down, 0, each), Segment(down, each, rest)
        up_a, up_b = Segment(up, 0, each - rest), Segment(up, each - rest, each)
        group_1, group_2, group_3 = [down_a], [down_b, up_a], [up_b]

        def stage(dims, groups=(group_1, group_2, group_3)):
            return outgoing(scalars, groups, dims)

        def arrive(dims, sent, groups=(group_1, group_2, group_3)):
            for group, dim, value in zip(groups, dims, sent):
                settle(group, dim, value)

        dims = (DX, DZ0, DY)
        sent = stage(dims[:1], (group_1,))
        sent, grad_recv, up_recv = tie((sent, grad_recv, up_recv))
        up_a.parts[1] = (up_recv,) + up_a.parts[1][1:]
        up_b.parts[1] = (up_recv,) + up_b.parts[1][1:]
        sent = list(sent) + list(stage(dims[1:], (group_2, group_3)))
        grad_own, grad_recv, sent = tie((grad_own, grad_recv, sent))
        sent = [hop(v, hops[d]) for v, d in zip(sent, dims)]
        arrive(dims, sent)

    def backward(pair, grad_recv):
        own, send, conv, keep, give = attend_back(
            pair,
            scalars,
            proj,
            mixed,
            lse,
            taps_own,
            heads_own,
            heads_send,
            grad_own,
            grad_recv,
            normed,
        )
        keep = keep.reshape((1, 1) + keep.shape)
        give = give.reshape((1, 1) + give.shape)
        return own, send, conv, keep, give

    qkv_rows = 3 * width // 8
    own_0, send_0, conv_0, keep_0, give_0 = backward(0, grad_recv)
    if fast:
        dims = (DY, DZ1, DX)
        sent = stage(dims)
        grad_recv, own_0, send_0, give_0, sent = tie((grad_recv, own_0, send_0, give_0, sent))
        sent = [hop(v, hops[d]) for v, d in zip(sent, dims)]
        arrive(dims, sent)
        qkv_0 = Segment((keep_0, hop(give_0, hops[DX])), 0, qkv_rows)
        group_1.append(qkv_0)
    recv_0 = swap_core(send_0)
    own_1, send_1, conv_1, keep_1, give_1 = backward(1, grad_recv)
    if fast:
        dims = (DZ0, DX, DZ1)
        sent = stage(dims)
        grad_recv, own_1, send_1, give_1, recv_0, result_give, sent = tie(
            (grad_recv, own_1, send_1, give_1, recv_0, result_give, sent)
        )
        sent = [hop(v, hops[d]) for v, d in zip(sent, dims)]
    result_back = swap_pair(result_give)
    recv_1 = swap_core(send_1)
    own_2, send_2, conv_2, keep_2, give_2 = backward(2, grad_recv)
    if fast:
        own_2, send_2, give_1, give_2, recv_1, result_back, sent = tie(
            (own_2, send_2, give_1, give_2, recv_1, result_back, sent)
        )
        arrive(dims, sent)
        give_1 = hop(give_1, hops[DX])
        give_2 = hop(give_2, hops[DX])
    recv_2 = swap_core(send_2)
    if fast:
        dims = (DZ1, DY, DZ0)
        sent = stage(dims)
        recv_2, sent = tie((recv_2, sent))
        ffn_waiting = [hop(v, hops[d]) for v, d in zip(sent, dims)]
    g_own = (own_0, own_1, own_2)
    g_send = (send_0, send_1, send_2)
    g_recv = (recv_0, recv_1, recv_2)
    g_conv = (conv_0, conv_1, conv_2)
    grad_in_pair, tokens_grad, small = input_grad(
        scalars,
        g_own,
        g_recv,
        qkv_weight,
        tok_pair,
        tok_own,
        grad_residual,
        vectors,
        early,
        g_conv,
    )
    grad_in_back = swap_pair(grad_in_pair)

    def place(both, other):
        return lax.dynamic_update_slice(both, other[None], (1 - half, 0, 0))

    result_all = place(result_all, result_back)
    index = batch * groups + member
    share = width // devices
    part = width // batch_groups

    if not fast:
        axes = ("batch", "mp")
        grad_qkv = 0.0
        for n, (norm, slot) in enumerate(zip(normed, (0, 0, 1, 1))):
            source = (g_own, g_send)[n % 2]
            grads = jnp.concatenate([g[slot * rows : (slot + 1) * rows] for g in source], axis=1)
            grad_qkv = grad_qkv + jnp.einsum("dt,te->de", norm, grads, preferred_element_type=F32)
        grad_qkv = grad_qkv.reshape(width, pairs, 3, LANES).transpose(2, 0, 1, 3)
        qkv_full = lax.dynamic_update_slice_in_dim(
            jnp.zeros((3, width, width), F32), grad_qkv.reshape(3, width, middle), core * middle, 2
        )
        qkv_flat = qkv_full.reshape(3, batch_groups, part, groups, quarter)
        qkv_flat = qkv_flat.transpose(1, 3, 0, 2, 4).reshape(devices * 3 * part, quarter)

        def scatter(value):
            return lax.psum_scatter(value, axes, scatter_dimension=0, tiled=True)

        small = lax.psum(small, axes)
        qkv_out = scatter(qkv_flat).reshape(3, part, quarter)
        up_out, down_out, out_out = scatter(grad_up), scatter(grad_down), scatter(grad_out)
    else:
        give_1, give_2, small, ffn_waiting = tie((give_1, give_2, small, ffn_waiting))
        arrive((DZ1, DY, DZ0), ffn_waiting)
        qkv_1 = Segment((keep_1, give_1), 0, qkv_rows)
        qkv_2 = Segment((keep_2, give_2), 0, qkv_rows)
        (sent,) = outgoing(scalars, [[qkv_1, qkv_2]], [DZ0])
        small = small + hop(small, ("mp", CORE))
        small, sent = tie((small, sent))
        waiting = hop(sent, hops[DZ0])
        small = small + hop(small, hops[DX])
        def finish_ffn(s_ref, totals, outs, send):
            whole = [total((0,) * 4, slice(None)) for total in totals]
            downs = jnp.concatenate(whole[0:2], axis=0)
            ups = jnp.concatenate(whole[2:4], axis=0)
            down_out, up_out, out_out = outs
            for out, values in ((down_out, downs), (up_out, ups), (out_out, ups[down_rows:])):
                size, cols = out.shape
                for n in range(cols // LANES):
                    out[:, n * LANES : (n + 1) * LANES] = values[n * size : (n + 1) * size]

        down_out, up_out, out_out = sum_call(
            scalars,
            [down_a, down_b, up_a, up_b],
            [None] * 4,
            finish_ffn,
            [
                jax.ShapeDtypeStruct((ff // devices, width), F32),
                jax.ShapeDtypeStruct((share, ff), F32),
                jax.ShapeDtypeStruct((share, width), F32),
            ],
            "ffn_sum",
        )

        small, waiting, result_all, down_out, up_out, out_out = tie(
            (small, waiting, result_all, down_out, up_out, out_out)
        )
        settle([qkv_1, qkv_2], DZ0, waiting)
        (sent,) = outgoing(scalars, [[qkv_1, qkv_2]], [DZ1], BUSY)
        sent = hop(sent, hops[DZ1])
        small = small + hop(small, hops[DZ0])
        small = small + hop(small, hops[DZ1])
        small, sent, grad_in_back = tie((small, sent, grad_in_back))
        settle([qkv_1, qkv_2], DZ1, sent)
        small = small + hop(small, hops[DY])

        def finish_qkv(s_ref, totals, outs, send):
            first, middle, last = [total((0,) * 4, slice(None)) for total in totals]
            lower = jnp.concatenate([first, middle[:, :HEAD_DIM]], axis=1)
            upper = jnp.concatenate([middle[:, HEAD_DIM:], last], axis=1)
            outs[0][...] = jnp.where(s_ref[0] == 0, lower, upper)
            outs[1][...] = jnp.where(s_ref[4] == 0, upper, lower).astype(BF16)
            outs[2][...] = jnp.where(s_ref[4] == 0, lower, upper).astype(BF16)

        keep, straight, crossed = sum_call(
            scalars,
            [qkv_0, qkv_1, qkv_2],
            [None] * 3,
            finish_qkv,
            [jax.ShapeDtypeStruct((qkv_rows, quarter), t) for t in (F32, BF16, BF16)],
            "qkv_sum",
        )
        straight = lax.ppermute(straight, "mp", [(2, 0), (0, 1), (3, 2), (1, 3)])
        crossed = lax.ppermute(crossed, "mp", [(2, 1), (1, 2)])
        qkv_out = straight.astype(F32) + jnp.where(half == core, keep, crossed.astype(F32))
        qkv_out = qkv_out.reshape(3, part, quarter)

    tokens_grad = place(tokens_grad, grad_in_back)
    up_bias_out = pick(small[: ff // width].reshape(devices, ff // devices), index)
    mine = pick(small.reshape(24, devices, share).transpose(1, 0, 2), index)
    return (
        result_all,
        tokens_grad,
        mine[17],
        mine[18],
        qkv_out,
        mine[8:17].reshape(3, taps, share),
        out_out,
        mine[4],
        mine[5],
        up_out,
        up_bias_out,
        down_out,
        mine[6],
    )


def solution(mesh):
    in_specs = (
        P("batch", "mp", None),
        P("batch", "mp", None),
        P("batch"),
    ) + (P(),) * 11
    out_specs = (
        P("batch", "mp", None),
        P("batch", "mp", None),
        P(("batch", "mp")),
        P(("batch", "mp")),
        P(None, "batch", "mp"),
        P(None, None, ("batch", "mp")),
        P(("batch", "mp"), None),
        P(("batch", "mp")),
        P(("batch", "mp")),
        P(("batch", "mp"), None),
        P(("batch", "mp")),
        P(("batch", "mp"), None),
        P(("batch", "mp")),
    )
    return jax.shard_map(
        on_device, mesh=mesh, in_specs=in_specs, out_specs=out_specs, check_vma=False
    )
```
